32 devices in a mesh: rows: 16 (over z, y, x), tgt: 2 (over core).
Axes of the slice: x: 2, y: 2, z: 4, core: 2. Of those that a mesh axis runs over, the one named last changes fastest.
Arguments:
- counts: int32 [16], P('rows'), may hold values from 512 to 2048, as said below
- samples: float32 [32768, 256], P('rows'), may hold values from -6 to 6
- targets: float32 [32768, 256], P('rows', 'tgt'), may hold values from -6 to 6
- point_ids: int32 [2, 512], replicated, may hold values from 0 to 32767, as said below
- block_inverse: float32 [2, 512, 512], replicated, may hold values from -1.34869915e-06 to 1.6607488e-05
Outputs:
- residual: float32 [32768, 256], P('rows', 'tgt')
The draws below stay inside these ranges and needn't reach their ends.
Inputs may be any that keep to these rules, and one draw needn't show every extreme that they name: `counts`: some device has exactly 2048 live rows. `point_ids`: every id is d * 2048 + s with s < counts[d].
All inputs are finite; a program needn't handle non-finite values.
Results may differ from the reference program's by a relative error of at most 0.0003.
Values sent between devices are 32-bit elements; how exact they have to be, the bound alone decides.
No kernel may reach another device: no remote copies, remote signals or barrier semaphores. Data moves between devices by JAX's collectives and lax.ppermute only.
A program may use at most 64 MiB of HBM per device.

```python
import jax
import jax.numpy as jnp
from jax import lax

FEAT = 256
TARGETS = 256
BLOCK = 512
NBLK = 2
ROW_DEV = 2048
TOTAL = 32768


def shared_counts(key):
    groups = TOTAL // ROW_DEV
    drawn = jax.random.randint(jax.random.fold_in(key, 11), (groups,), ROW_DEV // 4, ROW_DEV + 1)
    fullest = jax.random.randint(jax.random.fold_in(key, 12), (), 0, groups)
    return drawn.at[fullest].set(ROW_DEV).astype(jnp.int32)


def draw_counts(key, part):
    return shared_counts(key)


def draw_point_ids(key, part):
    groups = TOTAL // ROW_DEV
    live = shared_counts(key)
    owner = jax.random.randint(jax.random.fold_in(key, 21), (NBLK, BLOCK), 0, groups)
    raw_slot = jax.random.randint(jax.random.fold_in(key, 22), (NBLK, BLOCK), 0, 1 << 20)
    slot = raw_slot % live[owner]
    return (owner * ROW_DEV + slot).astype(jnp.int32)


def draw_block_inverse(key, part):
    noise = jax.random.truncated_normal(key, -4.0, 4.0, (NBLK, BLOCK, BLOCK), jnp.float32)
    noise = noise * (1.0 / BLOCK ** 0.5)
    eye = jnp.eye(BLOCK, dtype=jnp.float32)[None]
    return ((2.0 * eye + noise) / (32.0 * (TOTAL * BLOCK) ** 0.5)).astype(jnp.float32)


def block_scale(stream_key, dims, split, least, top_value):
    loudness, own = 1.0, jax.random.fold_in(stream_key, 6)
    for dim, shards_of in split:
        steps = jnp.exp(jax.random.uniform(jax.random.fold_in(own, dim), (shards_of,), jnp.float32, least / len(split), top_value / len(split)))
        loudness = loudness * jnp.repeat(steps, dims[dim] // shards_of).reshape([-1 if axis == dim else 1 for axis in range(len(dims))])
    return loudness


def gaussian(rng, dims, width, limit, pieces=(), kind=jnp.bfloat16):
    array = jax.random.normal(rng, dims, jnp.float32) * width
    if len(pieces) > 0:
        array = block_scale(rng, dims, pieces, -0.22, 0.18) * array
    return jnp.clip(array, min=-limit, max=limit).astype(kind)


def setup_inputs(seed: int = 0) -> dict:
    keys = jax.random.split(jax.random.key(seed), 6)
    counts = draw_counts(jax.random.fold_in(keys[5], 71), 0)
    samples = gaussian(keys[1], (TOTAL, FEAT), 1.0, 6.0, ((0, 16),), jnp.float32)
    targets = gaussian(keys[2], (TOTAL, TARGETS), 1.0, 6.0, ((0, 16), (1, 2)), jnp.float32)
    point_ids = draw_point_ids(jax.random.fold_in(keys[5], 71), 0)
    block_inverse = draw_block_inverse(jax.random.fold_in(keys[5], 71), 0)
    return {"counts": counts, "samples": samples, "targets": targets, "point_ids": point_ids, "block_inverse": block_inverse}


def kernel_columns(rows_in, points):
    scaled = lax.dot_general(rows_in, points, (((1,), (1,)), ((), ())), precision=lax.Precision.HIGHEST, preferred_element_type=jnp.float32)
    scaled = scaled * (1.0 / FEAT ** 0.5)
    return (0.5 * scaled + 1.0) ** 3


def reference(counts, samples, targets, point_ids, block_inverse):
    groups = samples.shape[0] // ROW_DEV
    stacked = samples.reshape(groups, ROW_DEV, FEAT)
    alive = jnp.arange(ROW_DEV, dtype=jnp.int32)[None, :] < counts[:, None]
    residual = targets.reshape(groups, ROW_DEV, TARGETS)
    for block_index in range(NBLK):
        points = jnp.take(samples, point_ids[block_index].astype(jnp.int32), axis=0)

        def masked(rows_in, marks):
            return jnp.where(marks[:, None], kernel_columns(rows_in, points), 0.0)

        def add_sum(total, item):
            rows_in, marks, current = item
            columns = masked(rows_in, marks)
            return total + lax.dot_general(columns, current, (((0,), (0,)), ((), ())), precision=lax.Precision.HIGHEST, preferred_element_type=jnp.float32), None

        sums, unused = lax.scan(add_sum, jnp.zeros((BLOCK, TARGETS), jnp.float32), (stacked, alive, residual))
        coefs = jnp.dot(block_inverse[block_index], sums, precision=lax.Precision.HIGHEST, preferred_element_type=jnp.float32)

        def update(item):
            rows_in, marks, current = item
            return current - jnp.dot(masked(rows_in, marks), coefs, precision=lax.Precision.HIGHEST, preferred_element_type=jnp.float32)

        residual = lax.map(update, (stacked, alive, residual))
    return residual.reshape(groups * ROW_DEV, TARGETS)
```

```python
import functools

import jax
import jax.numpy as jnp
from jax import lax
from jax.experimental import pallas as pl
from jax.experimental.pallas import tpu as pltpu
from jax.sharding import PartitionSpec as P

F32 = jnp.float32
BF16 = jnp.bfloat16
ROWS_STEP = 512


def round_up(value, unit):
    return -(-value // unit) * unit


def split(x):
    high = x.astype(BF16)
    return high, (x - high.astype(F32)).astype(BF16)


def dot(a, b, dims):
    return lax.dot_general(a, b, (dims, ((), ())), preferred_element_type=F32)


def dot3(a, b, dims):
    return dot(a[0], b[0], dims) + dot(a[0], b[1], dims) + dot(a[1], b[0], dims)


def pick_kernel(groups, cores, cap, ids_ref, samples_ref, rows_ref, slots_ref, most_ref, index_v, index_s, sems):
    rows_here = samples_ref.shape[0]
    me, core = lax.axis_index("rows"), lax.axis_index("tgt")
    ids = jnp.concatenate([ids_ref[b : b + 1, :] for b in range(ids_ref.shape[0])], axis=1)
    count = ids.shape[1]
    owner = lax.div(ids, jnp.int32(rows_here))
    local = ids - owner * rows_here
    mine = lax.broadcasted_iota(jnp.int32, (groups, count), 0) == owner
    seen = mine.astype(jnp.int32)
    lane = lax.broadcasted_iota(jnp.int32, (groups, count), 1)
    step = 1
    while step < count:
        seen = seen + jnp.where(lane >= step, pltpu.roll(seen, step, 1), 0)
        step *= 2
    most = jnp.max(seen)
    rank = jnp.sum(jnp.where(mine, seen, 0), axis=0, keepdims=True) - 1
    half = lax.div(rank, jnp.int32(cap))
    packed = (half * groups + owner) * cap + (rank - half * cap)
    place = lax.broadcasted_iota(jnp.int32, (1, count), 1)
    slots_ref[...] = jnp.where(most > cap * cores, place, packed)
    most_ref[0] = most

    wanted = lax.broadcasted_iota(jnp.int32, (cap, count), 0) + core * cap
    chosen = jnp.where((wanted == rank) & (owner == me), local, 0)
    index_v[...] = jnp.broadcast_to(jnp.sum(chosen, axis=1, keepdims=True), index_v.shape)
    move = pltpu.make_async_copy(index_v, index_s, sems.at[0])
    move.start()
    move.wait()

    @pl.loop(0, cap)
    def _(k):
        pltpu.make_async_copy(samples_ref.at[pl.ds(index_s[k, 0], 1)], rows_ref.at[pl.ds(k, 1)], sems.at[1]).start()

    pltpu.make_async_copy(samples_ref.at[pl.ds(0, cap)], rows_ref, sems.at[1]).wait()


def pick(ids, samples, groups, cores, cap):
    count = ids.shape[0] * ids.shape[1]
    vmem = pl.BlockSpec(memory_space=pltpu.VMEM)
    return pl.pallas_call(
        functools.partial(pick_kernel, groups, cores, cap),
        out_shape=(
            jax.ShapeDtypeStruct((cap, samples.shape[1]), F32),
            jax.ShapeDtypeStruct((1, count), jnp.int32),
            jax.ShapeDtypeStruct((1,), jnp.int32),
        ),
        in_specs=[vmem, pl.BlockSpec(memory_space=pl.ANY)],
        out_specs=(vmem, vmem, pl.BlockSpec(memory_space=pltpu.SMEM)),
        scratch_shapes=[
            pltpu.VMEM((cap, 128), jnp.int32),
            pltpu.SMEM((cap, 128), jnp.int32),
            pltpu.SemaphoreType.DMA((2,)),
        ],
        name="pick",
    )(ids, samples)


def unpack(held, slots_ref, core, cores):
    depth = held[0].shape[0]
    total = None
    for shift, ref in enumerate(held):
        base = lax.rem(core + shift, cores) * depth
        slot = lax.broadcasted_iota(jnp.int32, (depth, slots_ref.shape[1]), 0) + base
        taken = jnp.where(slot == slots_ref[...], 1.0, 0.0).astype(BF16)
        parts = jnp.concatenate(split(ref[...]), axis=1)
        found = dot(parts, taken, ((0,), (0,)))
        total = found if total is None else total + found
    feat = held[0].shape[1]
    return total[:feat].astype(BF16), total[feat:].astype(BF16)


def block_kernel(cores, first, last, *refs):
    refs = list(refs)
    live_ref = refs.pop(0)
    step = pl.program_id(0)
    residual_ref = refs.pop(0)
    if not first:
        sums_ref, inverse_ref, old_high_ref, old_low_ref = refs[:4]
        refs = refs[4:]
    if not last:
        samples_ref, slots_ref = refs[:2]
        held = refs[2 : 2 + cores]
        refs = refs[2 + cores :]
    if not first:
        out_ref = refs.pop(0)
    if not last:
        high_ref, low_ref, total_ref = refs[:3]
        refs = refs[3:]
    if not first:
        coefs_ref = refs.pop(0)
    if not last:
        points_ref = refs.pop(0)

    @pl.when(step == 0)
    def _():
        if not first:
            coefs = dot3(split(sums_ref[...]), split(inverse_ref[0]), ((1,), (1,)))
            coefs_ref[0], coefs_ref[1] = split(coefs)
        if not last:
            points_ref[0], points_ref[1] = unpack(held, slots_ref, lax.axis_index("tgt"), cores)
            total_ref[...] = jnp.zeros_like(total_ref)

    residual = residual_ref[...]
    if not first:
        old = (old_high_ref[...], old_low_ref[...])
        residual = residual - dot3(old, (coefs_ref[0], coefs_ref[1]), ((1,), (1,)))
        out_ref[...] = residual
    if not last:
        scale = 0.5 / samples_ref.shape[1] ** 0.5
        base = dot3(split(samples_ref[...]), (points_ref[0], points_ref[1]), ((1,), (0,))) * scale + 1.0
        rows = residual.shape[0]
        slot = lax.broadcasted_iota(jnp.int32, (rows, 1), 0) + step * rows
        columns = split(jnp.where(slot < live_ref[0], base * base * base, 0.0))
        high_ref[...], low_ref[...] = columns
        total_ref[...] += dot3(split(residual), columns, ((0,), (0,)))


def block_pass(live, residual, previous, following, cores):
    rows, width = residual.shape
    first, last = previous is None, following is None
    step = min(ROWS_STEP, rows)
    by_step = lambda columns: pl.BlockSpec((step, columns), lambda i, live: (i, 0))
    whole = lambda a: pl.BlockSpec(a.shape, lambda i, live: (0,) * a.ndim)
    args, in_specs = [residual], [by_step(width)]
    out_shape, out_specs, scratch = [], [], []
    if not first:
        sums, inverse, index, high, low = previous
        size = high.shape[1]
        args += [sums, inverse, high, low]
        in_specs += [whole(sums), pl.BlockSpec((1, size, size), lambda i, live, b=index: (b, 0, 0)), by_step(size), by_step(size)]
        out_shape.append(jax.ShapeDtypeStruct((rows, width), F32))
        out_specs.append(by_step(width))
    if not last:
        samples, slots, index, held, blocks = following
        feat = samples.shape[1]
        size = slots.shape[1] // blocks
        args += [samples, slots, *held]
        in_specs += [by_step(feat), pl.BlockSpec((1, size), lambda i, live, b=index: (0, b)), *[whole(h) for h in held]]
        out_shape += [jax.ShapeDtypeStruct((rows, size), BF16)] * 2 + [jax.ShapeDtypeStruct((width, size), F32)]
        out_specs += [by_step(size), by_step(size), pl.BlockSpec((width, size), lambda i, live: (0, 0))]
    if not first:
        scratch.append(pltpu.VMEM((2, width, size), BF16))
    if not last:
        scratch.append(pltpu.VMEM((2, feat, size), BF16))
    return pl.pallas_call(
        functools.partial(block_kernel, cores, first, last),
        grid_spec=pltpu.PrefetchScalarGridSpec(
            num_scalar_prefetch=1, grid=(rows // step,), in_specs=in_specs, out_specs=out_specs, scratch_shapes=scratch
        ),
        out_shape=out_shape,
        name="block",
    )(live, *args)


def sum_over_rows(totals, groups):
    width, size = totals.shape
    piece = round_up(width, groups) // groups
    padded = jnp.pad(totals, ((0, piece * groups - width), (0, 0))) if piece * groups != width else totals
    got = lax.all_to_all(padded.reshape(groups, piece, size), "rows", 0, 0)
    own = jnp.sum(got, axis=0)
    back = lax.all_to_all(jnp.broadcast_to(own[None], (groups, piece, size)), "rows", 0, 0)
    return back.reshape(groups * piece, size)[:width]


def on_device(groups, cores, counts, samples, targets, point_ids, block_inverse):
    rows_here, feat = samples.shape
    blocks, size = point_ids.shape
    mean = blocks * size / groups
    cap = round_up(max(1, round((mean + 4 * mean**0.5) / cores)), 8)

    rows, slots, most = pick(point_ids, samples, groups, cores, cap)

    def general(rows):
        ids = jnp.pad(point_ids.reshape(-1), (0, cores * groups * cap - blocks * size), constant_values=-1)
        ids = lax.dynamic_slice_in_dim(ids, lax.axis_index("tgt") * groups * cap, groups * cap)
        local = ids - lax.axis_index("rows") * rows_here
        owned = (local >= 0) & (local < rows_here)
        taken = jnp.take(samples, jnp.clip(local, 0, rows_here - 1), axis=0)
        taken = jnp.where(owned[:, None], taken, 0.0)
        return jnp.sum(lax.all_to_all(taken.reshape(groups, cap, feat), "rows", 0, 0), axis=0)

    rows = lax.cond(most[0] > cap * cores, general, lambda rows: rows, rows)
    got = lax.all_to_all(jnp.broadcast_to(rows[None], (groups, cap, feat)), "rows", 0, 0).reshape(groups * cap, feat)
    held = [got]
    for shift in range(1, cores):
        held.append(lax.ppermute(got, "tgt", [((c + shift) % cores, c) for c in range(cores)]))

    residual, previous = targets, None
    for b in range(blocks):
        out = list(block_pass(counts, residual, previous, (samples, slots, b, held, blocks), cores))
        if b > 0:
            residual = out.pop(0)
        high, low, totals = out
        previous = (sum_over_rows(totals, groups), block_inverse, b, high, low)
    return block_pass(counts, residual, previous, None, cores)[0]


def solution(mesh):
    return jax.shard_map(
        functools.partial(on_device, mesh.shape["rows"], mesh.shape["tgt"]),
        mesh=mesh,
        in_specs=(P("rows"), P("rows", None), P("rows", "tgt"), P(), P()),
        out_specs=P("rows", "tgt"),
        check_vma=False,
    )
```

```python
import functools

import jax
import jax.numpy as jnp
from jax import lax
from jax.experimental import pallas as pl
from jax.experimental.pallas import tpu as pltpu
from jax.sharding import PartitionSpec as P

F32 = jnp.float32
BF16 = jnp.bfloat16
ROWS_STEP = 512


def round_up(value, unit):
    return -(-value // unit) * unit


def split(x):
    high = x.astype(BF16)
    return high, (x - high.astype(F32)).astype(BF16)


def dot(a, b, dims):
    return lax.dot_general(a, b, (dims, ((), ())), preferred_element_type=F32)


def dot3(a, b, dims):
    return dot(a[0], b[0], dims) + dot(a[0], b[1], dims) + dot(a[1], b[0], dims)


def pick_kernel(groups, cores, cap, ids_ref, samples_ref, rows_ref, slots_ref, most_ref, index_v, index_s, sems):
    rows_here = samples_ref.shape[0]
    me, core = lax.axis_index("rows"), lax.axis_index("tgt")
    ids = jnp.concatenate([ids_ref[b : b + 1, :] for b in range(ids_ref.shape[0])], axis=1)
    count = ids.shape[1]
    owner = lax.div(ids, jnp.int32(rows_here))
    local = ids - owner * rows_here
    mine = lax.broadcasted_iota(jnp.int32, (groups, count), 0) == owner
    seen = mine.astype(jnp.int32)
    lane = lax.broadcasted_iota(jnp.int32, (groups, count), 1)
    step = 1
    while step < count:
        seen = seen + jnp.where(lane >= step, pltpu.roll(seen, step, 1), 0)
        step *= 2
    most = jnp.max(seen)
    rank = jnp.sum(jnp.where(mine, seen, 0), axis=0, keepdims=True) - 1
    half = lax.div(rank, jnp.int32(cap))
    packed = (half * groups + owner) * cap + (rank - half * cap)
    place = lax.broadcasted_iota(jnp.int32, (1, count), 1)
    slots_ref[...] = jnp.where(most > cap * cores, place, packed)
    most_ref[0] = most

    wanted = lax.broadcasted_iota(jnp.int32, (cap, count), 0) + core * cap
    chosen = jnp.where((wanted == rank) & (owner == me), local, 0)
    index_v[...] = jnp.broadcast_to(jnp.sum(chosen, axis=1, keepdims=True), index_v.shape)
    move = pltpu.make_async_copy(index_v, index_s, sems.at[0])
    move.start()
    move.wait()

    @pl.loop(0, cap)
    def _(k):
        pltpu.make_async_copy(samples_ref.at[pl.ds(index_s[k, 0], 1)], rows_ref.at[pl.ds(k, 1)], sems.at[1]).start()

    pltpu.make_async_copy(samples_ref.at[pl.ds(0, cap)], rows_ref, sems.at[1]).wait()


def pick(ids, samples, groups, cores, cap):
    count = ids.shape[0] * ids.shape[1]
    vmem = pl.BlockSpec(memory_space=pltpu.VMEM)
    return pl.pallas_call(
        functools.partial(pick_kernel, groups, cores, cap),
        out_shape=(
            jax.ShapeDtypeStruct((cap, samples.shape[1]), F32),
            jax.ShapeDtypeStruct((1, count), jnp.int32),
            jax.ShapeDtypeStruct((1,), jnp.int32),
        ),
        in_specs=[vmem, pl.BlockSpec(memory_space=pl.ANY)],
        out_specs=(vmem, vmem, pl.BlockSpec(memory_space=pltpu.SMEM)),
        scratch_shapes=[
            pltpu.VMEM((cap, 128), jnp.int32),
            pltpu.SMEM((cap, 128), jnp.int32),
            pltpu.SemaphoreType.DMA((2,)),
        ],
        name="pick",
    )(ids, samples)


def pieces(rows):
    step = min(ROWS_STEP, rows)
    return [pl.ds(start, step) for start in range(0, rows, step)]


def rows_of(ref, at):
    return ref.at[at] if len(ref.shape) == 2 else ref.at[:, at]


def start_copies(source, target, sems):
    copies = [
        pltpu.make_async_copy(rows_of(source, at), rows_of(target, at), sems.at[index])
        for index, at in enumerate(pieces(source.shape[-2]))
    ]
    for copy in copies:
        copy.start()
    return copies


def update(residual, columns, coefs):
    width = residual.shape[1]
    both = dot(columns[0], coefs, ((1,), (0,)))
    return residual - (both[:, :width] + both[:, width:] + dot(columns[1], coefs[:, :width], ((1,), (0,))))


def unpack(held, slots_ref):
    depth, feat = held[0].shape
    cores = len(held)
    core = lax.axis_index("tgt")
    total = None
    for shift, ref in enumerate(held):
        base = lax.rem(core + shift, cores) * depth
        slot = lax.broadcasted_iota(jnp.int32, (depth, slots_ref.shape[1]), 0) + base
        taken = jnp.where(slot == slots_ref[...], 1.0, 0.0).astype(BF16)
        found = dot(jnp.concatenate(split(ref[...]), axis=1), taken, ((0,), (0,)))
        total = found if total is None else total + found
    return total[:feat].astype(BF16), total[feat:].astype(BF16)


def columns_kernel(live_ref, residual_ref, samples_ref, slots_ref, *refs):
    *held, columns_ref, total_ref, residual_v, samples_v, columns_v, sems = refs
    feat, width = samples_ref.shape[1], residual_ref.shape[1]
    samples_in = start_copies(samples_ref, samples_v, sems.at[0])
    residual_in = start_copies(residual_ref, residual_v, sems.at[1])
    points = unpack(held, slots_ref)
    scale = 0.5 / feat**0.5

    def add(index, at):
        residual_in[index].wait()
        high, low = split(residual_v[at, :])
        both = dot(jnp.concatenate([high, low], axis=1), columns_v[0, at, :], ((0,), (0,)))
        term = both[:width] + both[width:] + dot(high, columns_v[1, at, :], ((0,), (0,)))
        total_ref[...] = term if index == 0 else total_ref[...] + term

    parts, columns_out = pieces(samples_ref.shape[0]), []
    for index, at in enumerate(parts):
        samples_in[index].wait()
        base = dot3(split(samples_v[at, :]), points, ((1,), (0,))) * scale + 1.0
        slot = lax.broadcasted_iota(jnp.int32, (at.size, 1), 0) + at.start
        columns_v[0, at, :], columns_v[1, at, :] = split(jnp.where(slot < live_ref[0], base * base * base, 0.0))
        columns_out.append(pltpu.make_async_copy(columns_v.at[:, at], columns_ref.at[:, at], sems.at[2, index]))
        columns_out[-1].start()
        if index > 0:
            add(index - 1, parts[index - 1])
    add(len(parts) - 1, parts[-1])
    for copy in columns_out:
        copy.wait()


def cross_kernel(first_ref, second_ref, inverse_ref, out_ref, first_v, second_v, inverse_v, sems):
    first_in = start_copies(first_ref, first_v, sems.at[0])
    second_in = start_copies(second_ref, second_v, sems.at[1])
    inverse_in = pltpu.make_async_copy(inverse_ref, inverse_v, sems.at[2, 0])
    inverse_in.start()
    for copy in [*first_in, *second_in]:
        copy.wait()
    cross = dot3((first_v[0], first_v[1]), (second_v[0], second_v[1]), ((0,), (0,)))
    inverse_in.wait()
    out_ref[0], out_ref[1] = split(dot3(split(inverse_v[...]), split(cross), ((0,), (0,))))


def next_kernel(sums_ref, cross_ref, ahead_ref, next_ref):
    next_ref[...] = ahead_ref[...] - dot3(split(sums_ref[...]), (cross_ref[0], cross_ref[1]), ((1,), (0,)))


def side_by_side(transposed):
    return jnp.concatenate(split(transposed.T), axis=1)


def update_kernel(sums_ref, inverse_ref, residual_ref, columns_ref, out_ref, residual_v, columns_v, sems):
    columns_in = start_copies(columns_ref, columns_v, sems.at[0])
    residual_in = start_copies(residual_ref, residual_v, sems.at[1])
    coefs = side_by_side(dot3(split(sums_ref[...]), split(inverse_ref[...]), ((1,), (1,))))
    finish_update(coefs, columns_in, residual_in, columns_v, residual_v, out_ref, sems.at[2])


def finish_update(coefs, columns_in, residual_in, columns_v, residual_v, out_ref, sems):
    out = []
    for index, at in enumerate(pieces(out_ref.shape[0])):
        columns_in[index].wait()
        residual_in[index].wait()
        residual_v[at, :] = update(residual_v[at, :], (columns_v[0, at, :], columns_v[1, at, :]), coefs)
        out.append(pltpu.make_async_copy(residual_v.at[at], out_ref.at[at], sems.at[index]))
        out[-1].start()
    for copy in out:
        copy.wait()


def solved_kernel(columns_ref, inverse_ref, out_ref, columns_v, sems):
    columns_in = start_copies(columns_ref, columns_v, sems.at[0])
    inverse = split(inverse_ref[...])
    out = []
    for index, at in enumerate(pieces(columns_ref.shape[1])):
        columns_in[index].wait()
        columns_v[0, at, :], columns_v[1, at, :] = split(dot3((columns_v[0, at, :], columns_v[1, at, :]), inverse, ((1,), (0,))))
        out.append(pltpu.make_async_copy(columns_v.at[:, at], out_ref.at[:, at], sems.at[1, index]))
        out[-1].start()
    for copy in out:
        copy.wait()


def last_kernel(sums_ref, residual_ref, columns_ref, out_ref, residual_v, columns_v, sems):
    columns_in = start_copies(columns_ref, columns_v, sems.at[0])
    residual_in = start_copies(residual_ref, residual_v, sems.at[1])
    finish_update(side_by_side(sums_ref[...]), columns_in, residual_in, columns_v, residual_v, out_ref, sems.at[2])


VMEM = pl.BlockSpec(memory_space=pltpu.VMEM)
HBM = pl.BlockSpec(memory_space=pltpu.HBM)
SMEM = pl.BlockSpec(memory_space=pltpu.SMEM)


def local(kernel, out_shape, args, flops, in_specs, out_specs, scratch_shapes=(), limit=61):
    moved = sum(a.size * a.dtype.itemsize for a in [*args, *(out_shape if isinstance(out_shape, list) else [out_shape])])
    return pl.pallas_call(
        kernel,
        out_shape=out_shape,
        in_specs=in_specs,
        out_specs=out_specs,
        scratch_shapes=scratch_shapes,
        cost_estimate=pl.CostEstimate(flops=flops, bytes_accessed=moved, transcendentals=0),
        compiler_params=pltpu.CompilerParams(vmem_limit_bytes=limit * 2**20),
        name=kernel.__name__,
    )(*args)


def shape_of(*shape, dtype=F32):
    return jax.ShapeDtypeStruct(shape, dtype)


def columns_and_sums(live, residual, samples, slots, held):
    (rows, width), feat, size = residual.shape, samples.shape[1], slots.shape[1]
    return local(
        columns_kernel,
        [shape_of(2, rows, size, dtype=BF16), shape_of(width, size)],
        (live, residual, samples, slots, *held),
        6 * rows * size * (feat + width),
        [SMEM, HBM, HBM, VMEM] + [VMEM] * len(held),
        [HBM, VMEM],
        [
            pltpu.VMEM((rows, width), F32),
            pltpu.VMEM((rows, feat), F32),
            pltpu.VMEM((2, rows, size), BF16),
            pltpu.SemaphoreType.DMA((3, len(pieces(rows)))),
        ],
    )


def sum_over_rows(totals, groups, during_first, during_second):
    width, size = totals.shape
    piece = round_up(width, groups) // groups
    padded = jnp.pad(totals, ((0, piece * groups - width), (0, 0))) if piece * groups != width else totals
    got = lax.all_to_all(padded.reshape(groups, piece, size), "rows", 0, 0)
    got, made = lax.optimization_barrier((got, during_first()))
    own = jnp.sum(got, axis=0)
    back = lax.all_to_all(jnp.broadcast_to(own[None], (groups, piece, size)), "rows", 0, 0)
    back, more = lax.optimization_barrier((back, during_second(made)))
    return back.reshape(groups * piece, size)[:width], made, more


def on_device(groups, cores, counts, samples, targets, point_ids, block_inverse):
    rows_here, feat = samples.shape
    blocks, size = point_ids.shape
    mean = blocks * size / groups
    cap = round_up(max(1, round((mean + 4 * mean**0.5) / cores)), 8)

    rows, slots, most = pick(point_ids, samples, groups, cores, cap)

    def general(rows):
        ids = jnp.pad(point_ids.reshape(-1), (0, cores * groups * cap - blocks * size), constant_values=-1)
        ids = lax.dynamic_slice_in_dim(ids, lax.axis_index("tgt") * groups * cap, groups * cap)
        local = ids - lax.axis_index("rows") * rows_here
        owned = (local >= 0) & (local < rows_here)
        taken = jnp.take(samples, jnp.clip(local, 0, rows_here - 1), axis=0)
        taken = jnp.where(owned[:, None], taken, 0.0)
        return jnp.sum(lax.all_to_all(taken.reshape(groups, cap, feat), "rows", 0, 0), axis=0)

    rows = lax.cond(most[0] > cap * cores, general, lambda rows: rows, rows)
    got = lax.all_to_all(jnp.broadcast_to(rows[None], (groups, cap, feat)), "rows", 0, 0).reshape(groups * cap, feat)
    held = [got]
    for shift in range(1, cores):
        held.append(lax.ppermute(got, "tgt", [((c + shift) % cores, c) for c in range(cores)]))

    slots = [slots[:, b * size : (b + 1) * size] for b in range(blocks)]
    width = targets.shape[1]
    parts = len(pieces(rows_here))
    columns_v = pltpu.VMEM((2, rows_here, size), BF16)
    residual_v = pltpu.VMEM((rows_here, width), F32)
    def cross_of(columns, following, b):
        return local(
            cross_kernel,
            shape_of(2, size, size, dtype=BF16),
            (columns, following, block_inverse[b]),
            6 * rows_here * size * size,
            [HBM, HBM, HBM],
            VMEM,
            [columns_v, columns_v, pltpu.VMEM((size, size), F32), pltpu.SemaphoreType.DMA((3, parts))],
        )

    def updated(sums, residual, columns, b):
        return local(
            update_kernel,
            shape_of(rows_here, width),
            (sums, block_inverse[b], residual, columns),
            6 * rows_here * size * width,
            [VMEM, VMEM, HBM, HBM],
            HBM,
            [residual_v, columns_v, pltpu.SemaphoreType.DMA((3, parts))],
        )

    def solved_of(columns):
        return local(
            solved_kernel,
            shape_of(2, rows_here, size, dtype=BF16),
            (columns, block_inverse[blocks - 1]),
            6 * rows_here * size * size,
            [HBM, VMEM],
            HBM,
            [columns_v, pltpu.SemaphoreType.DMA((2, parts))],
        )

    residual = targets
    columns, totals = columns_and_sums(counts, residual, samples, slots[0], held)
    sums = before = None
    for b in range(blocks):
        def first(b=b, sums=sums, residual=residual, before=before, columns=columns):
            now = residual if b == 0 else updated(sums, residual, before, b - 1)
            return (now, *columns_and_sums(counts, now, samples, slots[b + 1], held)) if b + 1 < blocks else (now,)

        def second(made, b=b, columns=columns):
            return cross_of(columns, made[1], b) if b + 1 < blocks else solved_of(columns)

        sums, made, more = sum_over_rows(totals, groups, first, second)
        residual, before = made[0], columns
        if b + 1 < blocks:
            _, columns, ahead = made
            totals = local(next_kernel, shape_of(width, size), (sums, more, ahead), 6 * width * size * size, [VMEM] * 3, VMEM)
    return local(
        last_kernel,
        shape_of(rows_here, width),
        (sums, residual, more),
        6 * rows_here * size * width,
        [VMEM, HBM, HBM],
        HBM,
        [residual_v, columns_v, pltpu.SemaphoreType.DMA((3, parts))],
    )


def solution(mesh):
    return jax.shard_map(
        functools.partial(on_device, mesh.shape["rows"], mesh.shape["tgt"]),
        mesh=mesh,
        in_specs=(P("rows"), P("rows", None), P("rows", "tgt"), P(), P()),
        out_specs=P("rows", "tgt"),
        check_vma=False,
    )
```

```python
import functools

import jax
import jax.numpy as jnp
from jax import lax
from jax.experimental import pallas as pl
from jax.experimental.pallas import tpu as pltpu
from jax.sharding import PartitionSpec as P

F32 = jnp.float32
BF16 = jnp.bfloat16
ROWS_STEP = 512
HALF_STEP = 1024
LIMIT = 24 * 2**20


def round_up(value, unit):
    return -(-value // unit) * unit


def split(x):
    high = x.astype(BF16)
    return high, (x - high.astype(F32)).astype(BF16)


def dot(a, b, dims):
    return lax.dot_general(a, b, (dims, ((), ())), preferred_element_type=F32)


def dot3(a, b, dims):
    return dot(a[0], b[0], dims) + dot(a[0], b[1], dims) + dot(a[1], b[0], dims)


def pick_kernel(groups, cores, cap, ids_ref, samples_ref, rows_ref, slots_ref, most_ref, index_v, index_s, sems):
    rows_here = samples_ref.shape[0]
    me, core = lax.axis_index("rows"), lax.axis_index("tgt")
    ids = jnp.concatenate([ids_ref[b : b + 1, :] for b in range(ids_ref.shape[0])], axis=1)
    count = ids.shape[1]
    owner = lax.div(ids, jnp.int32(rows_here))
    local = ids - owner * rows_here
    mine = lax.broadcasted_iota(jnp.int32, (groups, count), 0) == owner
    seen = mine.astype(jnp.int32)
    lane = lax.broadcasted_iota(jnp.int32, (groups, count), 1)
    step = 1
    while step < count:
        seen = seen + jnp.where(lane >= step, pltpu.roll(seen, step, 1), 0)
        step *= 2
    most = jnp.max(seen)
    rank = jnp.sum(jnp.where(mine, seen, 0), axis=0, keepdims=True) - 1
    half = lax.div(rank, jnp.int32(cap))
    packed = (half * groups + owner) * cap + (rank - half * cap)
    place = lax.broadcasted_iota(jnp.int32, (1, count), 1)
    slots_ref[...] = jnp.where(most > cap * cores, place, packed)
    most_ref[0] = most

    wanted = lax.broadcasted_iota(jnp.int32, (cap, count), 0) + core * cap
    chosen = jnp.where((wanted == rank) & (owner == me), local, 0)
    index_v[...] = jnp.broadcast_to(jnp.sum(chosen, axis=1, keepdims=True), index_v.shape)
    move = pltpu.make_async_copy(index_v, index_s, sems.at[0])
    move.start()
    move.wait()

    @pl.loop(0, cap)
    def _(k):
        pltpu.make_async_copy(samples_ref.at[pl.ds(index_s[k, 0], 1)], rows_ref.at[pl.ds(k, 1)], sems.at[1]).start()

    pltpu.make_async_copy(samples_ref.at[pl.ds(0, cap)], rows_ref, sems.at[1]).wait()


def pick(ids, samples, groups, cores, cap):
    count = ids.shape[0] * ids.shape[1]
    vmem = pl.BlockSpec(memory_space=pltpu.VMEM)
    return pl.pallas_call(
        functools.partial(pick_kernel, groups, cores, cap),
        out_shape=(
            jax.ShapeDtypeStruct((cap, samples.shape[1]), F32),
            jax.ShapeDtypeStruct((1, count), jnp.int32),
            jax.ShapeDtypeStruct((1,), jnp.int32),
        ),
        in_specs=[vmem, pl.BlockSpec(memory_space=pl.ANY)],
        out_specs=(vmem, vmem, pl.BlockSpec(memory_space=pltpu.SMEM)),
        scratch_shapes=[
            pltpu.VMEM((cap, 128), jnp.int32),
            pltpu.SMEM((cap, 128), jnp.int32),
            pltpu.SemaphoreType.DMA((2,)),
        ],
        name="pick",
    )(ids, samples)


def pieces(rows, step=ROWS_STEP):
    step = min(step, rows)
    return [pl.ds(start, step) for start in range(0, rows, step)]


def copy_of(source, target, sem):
    copy = pltpu.make_async_copy(source, target, sem)
    copy.start()
    return copy


def copies_of(source, target, sems, parts):
    rows_of = lambda ref, at: ref.at[at] if len(ref.shape) == 2 else ref.at[:, at]
    return [copy_of(rows_of(source, at), rows_of(target, at), sems.at[i]) for i, at in enumerate(parts)]


def wait_all(*copies):
    for copy in copies:
        copy.wait()


def unpack(held, slots_ref):
    depth, feat = held[0].shape
    cores = len(held)
    core = lax.axis_index("tgt")
    total = None
    for shift, ref in enumerate(held):
        base = lax.rem(core + shift, cores) * depth
        slot = lax.broadcasted_iota(jnp.int32, (depth, slots_ref.shape[1]), 0) + base
        taken = jnp.where(slot == slots_ref[...], 1.0, 0.0).astype(BF16)
        found = dot(jnp.concatenate(split(ref[...]), axis=1), taken, ((0,), (0,)))
        total = found if total is None else total + found
    return total[:feat].astype(BF16), total[feat:].astype(BF16)


def columns_kernel(live_ref, residual_ref, samples_ref, slots_ref, *refs):
    *held, columns_ref, total_ref, residual_v, samples_v, columns_v, sems = refs
    rows, feat = samples_ref.shape
    width = residual_ref.shape[1]
    samples_in = copy_of(samples_ref, samples_v, sems.at[0])
    residual_in = copy_of(residual_ref, residual_v, sems.at[1])
    points = unpack(held, slots_ref)
    scale = 0.5 / feat**0.5
    wait_all(samples_in, residual_in)
    for at in pieces(rows):
        base = dot3(split(samples_v[at, :]), points, ((1,), (0,))) * scale + 1.0
        slot = lax.broadcasted_iota(jnp.int32, (at.size, 1), 0) + at.start
        columns_v[0, at, :], columns_v[1, at, :] = split(jnp.where(slot < live_ref[0], base * base * base, 0.0))
    columns_out = copy_of(columns_v, columns_ref, sems.at[2])
    for index, at in enumerate(pieces(rows)):
        high, low = split(residual_v[at, :])
        both = dot(jnp.concatenate([high, low], axis=1), columns_v[0, at, :], ((0,), (0,)))
        term = both[:width] + both[width:] + dot(high, columns_v[1, at, :], ((0,), (0,)))
        total_ref[...] = term if index == 0 else total_ref[...] + term
    columns_out.wait()


def cross_kernel(block, first_ref, second_ref, inverse_ref, out_ref, first_v, second_v, inverse_v, sems):
    size = first_ref.shape[2]
    parts = pieces(first_ref.shape[1], HALF_STEP)
    first_in = copies_of(first_ref, first_v, sems.at[0], parts)
    second_in = copies_of(second_ref, second_v, sems.at[1], parts)
    inverse_in = copy_of(inverse_ref.at[block], inverse_v, sems.at[2, 0])
    cross = None
    for index, at in enumerate(parts):
        wait_all(first_in[index], second_in[index])
        both = dot(jnp.concatenate([first_v[0, at, :], first_v[1, at, :]], axis=1), second_v[0, at, :], ((0,), (0,)))
        term = both[:size] + both[size:] + dot(first_v[0, at, :], second_v[1, at, :], ((0,), (0,)))
        cross = term if cross is None else cross + term
    inverse_in.wait()
    out_ref[0], out_ref[1] = split(dot3(split(inverse_v[...]), split(cross), ((0,), (0,))))


def next_kernel(sums_ref, cross_ref, ahead_ref, next_ref):
    next_ref[...] = ahead_ref[...] - dot3(split(sums_ref[...]), (cross_ref[0], cross_ref[1]), ((1,), (0,)))


def side_by_side(transposed):
    return jnp.concatenate(split(transposed.T), axis=1)


def finish_update(coefs, parts, columns_in, residual_in, columns_v, residual_v, out_ref, sems):
    width = out_ref.shape[1]
    out = []
    for index, at in enumerate(parts):
        wait_all(columns_in[index], residual_in[index])
        both = dot(columns_v[0, at, :], coefs, ((1,), (0,)))
        both = both[:, :width] + both[:, width:] + dot(columns_v[1, at, :], coefs[:, :width], ((1,), (0,)))
        residual_v[at, :] = residual_v[at, :] - both
        out.append(copy_of(residual_v.at[at], out_ref.at[at], sems.at[index]))
    wait_all(*out)


def update_kernel(block, sums_ref, inverse_ref, residual_ref, columns_ref, out_ref, residual_v, columns_v, inverse_v, sems):
    parts = pieces(residual_ref.shape[0])
    inverse_in = copy_of(inverse_ref.at[block], inverse_v, sems.at[3, 0])
    columns_in = copies_of(columns_ref, columns_v, sems.at[0], parts)
    residual_in = copies_of(residual_ref, residual_v, sems.at[1], parts)
    inverse_in.wait()
    coefs = side_by_side(dot3(split(sums_ref[...]), split(inverse_v[...]), ((1,), (1,))))
    finish_update(coefs, parts, columns_in, residual_in, columns_v, residual_v, out_ref, sems.at[2])


def solved_kernel(block, columns_ref, inverse_ref, out_ref, columns_v, inverse_v, sems):
    parts = pieces(columns_ref.shape[1], HALF_STEP)
    inverse_in = copy_of(inverse_ref.at[block], inverse_v, sems.at[2, 0])
    columns_in = copies_of(columns_ref, columns_v, sems.at[0], parts)
    inverse_in.wait()
    inverse = split(inverse_v[...])
    out = []
    for index, at in enumerate(parts):
        columns_in[index].wait()
        columns_v[0, at, :], columns_v[1, at, :] = split(dot3((columns_v[0, at, :], columns_v[1, at, :]), inverse, ((1,), (0,))))
        out.append(copy_of(columns_v.at[:, at], out_ref.at[:, at], sems.at[1, index]))
    wait_all(*out)


def last_kernel(sums_ref, residual_ref, columns_ref, out_ref, residual_v, columns_v, sems):
    parts = pieces(residual_ref.shape[0])
    columns_in = copies_of(columns_ref, columns_v, sems.at[0], parts)
    residual_in = copies_of(residual_ref, residual_v, sems.at[1], parts)
    finish_update(side_by_side(sums_ref[...]), parts, columns_in, residual_in, columns_v, residual_v, out_ref, sems.at[2])


SPACES = {"V": pltpu.VMEM, "H": pltpu.HBM, "S": pltpu.SMEM}


def local(kernel, args, places, outs, scratch_shapes, flops, name):
    args = [pltpu.with_memory_space_constraint(a, SPACES[p]) if p != "S" else a for a, p in zip(args, places)]
    moved = sum(a.size * a.dtype.itemsize for a in args)
    made = pl.pallas_call(
        kernel,
        out_shape=[SPACES[p](shape, dtype) for p, shape, dtype in outs],
        in_specs=[pl.BlockSpec(memory_space=SPACES[p]) for p in places],
        out_specs=[pl.BlockSpec(memory_space=SPACES[p]) for p, _, _ in outs],
        scratch_shapes=scratch_shapes,
        cost_estimate=pl.CostEstimate(flops=flops, bytes_accessed=moved, transcendentals=0),
        compiler_params=pltpu.CompilerParams(vmem_limit_bytes=LIMIT),
        name=name,
    )(*args)
    return made if len(outs) > 1 else made[0]


def columns_and_sums(live, residual, samples, slots, held):
    (rows, width), feat, size = residual.shape, samples.shape[1], slots.shape[1]
    return local(
        columns_kernel,
        (live, residual, samples, slots, *held),
        "SHHV" + "V" * len(held),
        [("H", (2, rows, size), BF16), ("V", (width, size), F32)],
        [
            pltpu.VMEM((rows, width), F32),
            pltpu.VMEM((rows, feat), F32),
            pltpu.VMEM((2, rows, size), BF16),
            pltpu.SemaphoreType.DMA((3,)),
        ],
        6 * rows * size * (feat + width),
        "columns",
    )


def sum_over_rows(totals, groups, during_first, during_second):
    width, size = totals.shape
    piece = round_up(width, groups) // groups
    padded = jnp.pad(totals, ((0, piece * groups - width), (0, 0))) if piece * groups != width else totals
    got = lax.all_to_all(padded.reshape(groups, piece, size), "rows", 0, 0)
    got, made = lax.optimization_barrier((got, during_first()))
    own = jnp.sum(got, axis=0)
    back = lax.all_to_all(jnp.broadcast_to(own[None], (groups, piece, size)), "rows", 0, 0)
    back, more = lax.optimization_barrier((back, during_second(made)))
    return back.reshape(groups * piece, size)[:width], made, more


def on_device(groups, cores, counts, samples, targets, point_ids, block_inverse):
    rows_here, feat = samples.shape
    blocks, size = point_ids.shape
    mean = blocks * size / groups
    cap = round_up(max(1, round((mean + 4 * mean**0.5) / cores)), 8)

    rows, slots, most = pick(point_ids, samples, groups, cores, cap)

    def general(rows):
        ids = jnp.pad(point_ids.reshape(-1), (0, cores * groups * cap - blocks * size), constant_values=-1)
        ids = lax.dynamic_slice_in_dim(ids, lax.axis_index("tgt") * groups * cap, groups * cap)
        local = ids - lax.axis_index("rows") * rows_here
        owned = (local >= 0) & (local < rows_here)
        taken = jnp.take(samples, jnp.clip(local, 0, rows_here - 1), axis=0)
        taken = jnp.where(owned[:, None], taken, 0.0)
        return jnp.sum(lax.all_to_all(taken.reshape(groups, cap, feat), "rows", 0, 0), axis=0)

    rows = lax.cond(most[0] > cap * cores, general, lambda rows: rows, rows)
    got = lax.all_to_all(jnp.broadcast_to(rows[None], (groups, cap, feat)), "rows", 0, 0).reshape(groups * cap, feat)
    held = [got]
    for shift in range(1, cores):
        held.append(lax.ppermute(got, "tgt", [((c + shift) % cores, c) for c in range(cores)]))

    slots = [slots[:, b * size : (b + 1) * size] for b in range(blocks)]
    width = targets.shape[1]
    parts = len(pieces(rows_here))
    columns_v = pltpu.VMEM((2, rows_here, size), BF16)
    residual_v = pltpu.VMEM((rows_here, width), F32)
    inverse_v = pltpu.VMEM((size, size), F32)
    sems = pltpu.SemaphoreType.DMA((4, parts))

    def cross_of(columns, following, b):
        return local(
            functools.partial(cross_kernel, b),
            (columns, following, block_inverse),
            "HHH",
            [("V", (2, size, size), BF16)],
            [columns_v, columns_v, inverse_v, sems],
            6 * rows_here * size * size,
            "cross",
        )

    def updated(sums, residual, columns, b):
        return local(
            functools.partial(update_kernel, b),
            (sums, block_inverse, residual, columns),
            "VHHH",
            [("H", (rows_here, width), F32)],
            [residual_v, columns_v, inverse_v, sems],
            6 * rows_here * size * width,
            "update",
        )

    def solved_of(columns):
        return local(
            functools.partial(solved_kernel, blocks - 1),
            (columns, block_inverse),
            "HH",
            [("H", (2, rows_here, size), BF16)],
            [columns_v, inverse_v, sems],
            6 * rows_here * size * size,
            "solved",
        )

    residual = targets
    columns, totals = columns_and_sums(counts, residual, samples, slots[0], held)
    sums = before = None
    for b in range(blocks):
        def first(b=b, sums=sums, residual=residual, before=before, columns=columns):
            now = residual if b == 0 else updated(sums, residual, before, b - 1)
            return (now, *columns_and_sums(counts, now, samples, slots[b + 1], held)) if b + 1 < blocks else (now,)

        def second(made, b=b, columns=columns):
            return cross_of(columns, made[1], b) if b + 1 < blocks else solved_of(columns)

        sums, made, more = sum_over_rows(totals, groups, first, second)
        residual, before = made[0], columns
        if b + 1 < blocks:
            _, columns, ahead = made
            out = [("V", (width, size), F32)]
            totals = local(next_kernel, (sums, more, ahead), "VVV", out, [], 6 * width * size * size, "next")
    return local(
        last_kernel,
        (sums, residual, more),
        "VHH",
        [("H", (rows_here, width), F32)],
        [residual_v, columns_v, sems],
        6 * rows_here * size * width,
        "last",
    )


def solution(mesh):
    return jax.shard_map(
        functools.partial(on_device, mesh.shape["rows"], mesh.shape["tgt"]),
        mesh=mesh,
        in_specs=(P("rows"), P("rows", None), P("rows", "tgt"), P(), P()),
        out_specs=P("rows", "tgt"),
        check_vma=False,
    )
```

```python
import functools
import random

import jax
import jax.numpy as jnp
from jax import lax
from jax.experimental import pallas as pl
from jax.experimental.pallas import tpu as pltpu
from jax.sharding import PartitionSpec as P

F32 = jnp.float32
BF16 = jnp.bfloat16
ROWS_STEP = 512
HALF_STEP = 1024
LIMIT = 24 * 2**20
POINTS_SEED = 14
SUMS_SEED = 152


def order_of(groups, seed):
    order = list(range(groups))
    random.Random(seed).shuffle(order)
    return order


def exchange(x, order):
    return lax.all_to_all(x, "rows", 0, 0, axis_index_groups=[order])


def round_up(value, unit):
    return -(-value // unit) * unit


def split(x):
    high = x.astype(BF16)
    return high, (x - high.astype(F32)).astype(BF16)


def dot(a, b, dims):
    return lax.dot_general(a, b, (dims, ((), ())), preferred_element_type=F32)


def dot3(a, b, dims):
    return dot(a[0], b[0], dims) + dot(a[0], b[1], dims) + dot(a[1], b[0], dims)


def pick_kernel(order, cores, cap, ids_ref, samples_ref, rows_ref, slots_ref, most_ref, index_v, index_s, sems):
    rows_here, groups = samples_ref.shape[0], len(order)
    me, core = lax.axis_index("rows"), lax.axis_index("tgt")
    ids = jnp.concatenate([ids_ref[b : b + 1, :] for b in range(ids_ref.shape[0])], axis=1)
    count = ids.shape[1]
    owner = lax.div(ids, jnp.int32(rows_here))
    local = ids - owner * rows_here
    mine = lax.broadcasted_iota(jnp.int32, (groups, count), 0) == owner
    seen = mine.astype(jnp.int32)
    lane = lax.broadcasted_iota(jnp.int32, (groups, count), 1)
    step = 1
    while step < count:
        seen = seen + jnp.where(lane >= step, pltpu.roll(seen, step, 1), 0)
        step *= 2
    most = jnp.max(seen)
    rank = jnp.sum(jnp.where(mine, seen, 0), axis=0, keepdims=True) - 1
    half = lax.div(rank, jnp.int32(cap))
    turn = jnp.zeros_like(owner)
    for index, device in enumerate(order):
        turn = jnp.where(owner == device, index, turn)
    packed = (half * groups + turn) * cap + (rank - half * cap)
    place = lax.broadcasted_iota(jnp.int32, (1, count), 1)
    slots_ref[...] = jnp.where(most > cap * cores, place, packed)
    most_ref[0] = most

    wanted = lax.broadcasted_iota(jnp.int32, (cap, count), 0) + core * cap
    chosen = jnp.where((wanted == rank) & (owner == me), local, 0)
    index_v[...] = jnp.broadcast_to(jnp.sum(chosen, axis=1, keepdims=True), index_v.shape)
    move = pltpu.make_async_copy(index_v, index_s, sems.at[0])
    move.start()
    move.wait()

    @pl.loop(0, cap)
    def _(k):
        pltpu.make_async_copy(samples_ref.at[pl.ds(index_s[k, 0], 1)], rows_ref.at[pl.ds(k, 1)], sems.at[1]).start()

    pltpu.make_async_copy(samples_ref.at[pl.ds(0, cap)], rows_ref, sems.at[1]).wait()


def pick(ids, samples, order, cores, cap):
    count = ids.shape[0] * ids.shape[1]
    vmem = pl.BlockSpec(memory_space=pltpu.VMEM)
    return pl.pallas_call(
        functools.partial(pick_kernel, order, cores, cap),
        out_shape=(
            jax.ShapeDtypeStruct((cap, samples.shape[1]), F32),
            jax.ShapeDtypeStruct((1, count), jnp.int32),
            jax.ShapeDtypeStruct((1,), jnp.int32),
        ),
        in_specs=[vmem, pl.BlockSpec(memory_space=pl.ANY)],
        out_specs=(vmem, vmem, pl.BlockSpec(memory_space=pltpu.SMEM)),
        scratch_shapes=[
            pltpu.VMEM((cap, 128), jnp.int32),
            pltpu.SMEM((cap, 128), jnp.int32),
            pltpu.SemaphoreType.DMA((2,)),
        ],
        name="pick",
    )(ids, samples)


def pieces(rows, step=ROWS_STEP):
    step = min(step, rows)
    return [pl.ds(start, step) for start in range(0, rows, step)]


def copy_of(source, target, sem):
    copy = pltpu.make_async_copy(source, target, sem)
    copy.start()
    return copy


def copies_of(source, target, sems, parts):
    rows_of = lambda ref, at: ref.at[at] if len(ref.shape) == 2 else ref.at[:, at]
    return [copy_of(rows_of(source, at), rows_of(target, at), sems.at[i]) for i, at in enumerate(parts)]


def wait_all(*copies):
    for copy in copies:
        copy.wait()


def unpack(held, slots_ref):
    depth, feat = held[0].shape
    cores = len(held)
    core = lax.axis_index("tgt")
    total = None
    for shift, ref in enumerate(held):
        base = lax.rem(core + shift, cores) * depth
        slot = lax.broadcasted_iota(jnp.int32, (depth, slots_ref.shape[1]), 0) + base
        taken = jnp.where(slot == slots_ref[...], 1.0, 0.0).astype(BF16)
        found = dot(jnp.concatenate(split(ref[...]), axis=1), taken, ((0,), (0,)))
        total = found if total is None else total + found
    return total[:feat].astype(BF16), total[feat:].astype(BF16)


def columns_kernel(resident, live_ref, residual_ref, samples_ref, slots_ref, *refs):
    if resident:
        *held, high_ref, low_ref, total_ref, columns_v, sems = refs
    else:
        *held, high_ref, low_ref, total_ref, columns_v, sems, residual_v, samples_v = refs
        samples_in = copy_of(samples_ref, samples_v, sems.at[2, 0])
        residual_in = copy_of(residual_ref, residual_v, sems.at[3, 0])
    rows, feat = samples_ref.shape
    width = residual_ref.shape[1]
    points = unpack(held, slots_ref)
    scale = 0.5 / feat**0.5
    if not resident:
        wait_all(samples_in, residual_in)
        samples_ref, residual_ref = samples_v, residual_v
    columns_out = []
    for index, half in enumerate(pieces(rows, HALF_STEP)):
        for at in [pl.ds(half.start + part.start, part.size) for part in pieces(half.size)]:
            base = dot3(split(samples_ref[at, :]), points, ((1,), (0,))) * scale + 1.0
            slot = lax.broadcasted_iota(jnp.int32, (at.size, 1), 0) + at.start
            columns_v[0, at, :], columns_v[1, at, :] = split(jnp.where(slot < live_ref[0], base * base * base, 0.0))
        for kind, ref in enumerate((high_ref, low_ref)):
            columns_out.append(copy_of(columns_v.at[kind, half], ref.at[half], sems.at[kind, index]))
    for index, at in enumerate(pieces(rows)):
        high, low = split(residual_ref[at, :])
        both = dot(jnp.concatenate([high, low], axis=1), columns_v[0, at, :], ((0,), (0,)))
        term = both[:width] + both[width:] + dot(high, columns_v[1, at, :], ((0,), (0,)))
        total_ref[...] = term if index == 0 else total_ref[...] + term
    wait_all(*columns_out)


def cross_kernel(block, first_high, first_low, second_high, second_low, inverse_ref, out_ref, first_v, second_v, inverse_v, sems):
    rows, size = first_high.shape
    parts = pieces(rows)
    into = lambda ref, scratch, kind, i, at: copy_of(ref.at[at], scratch.at[kind, at], sems.at[2 * kind + (scratch is second_v), i])
    copies = [
        [into(ref, scratch, kind, i, at) for ref, scratch, kind in zip((first_high, first_low, second_high, second_low), (first_v, first_v, second_v, second_v), (0, 1, 0, 1))]
        for i, at in enumerate(parts)
    ]
    inverse_in = copy_of(inverse_ref.at[block], inverse_v, sems.at[4, 0])
    cross = None
    for index, at in enumerate(parts):
        wait_all(*copies[index])
        both = dot(jnp.concatenate([first_v[0, at, :], first_v[1, at, :]], axis=1), second_v[0, at, :], ((0,), (0,)))
        term = both[:size] + both[size:] + dot(first_v[0, at, :], second_v[1, at, :], ((0,), (0,)))
        cross = term if cross is None else cross + term
    inverse_in.wait()
    out_ref[0], out_ref[1] = split(dot3(split(inverse_v[...]), split(cross), ((0,), (0,))))


def next_kernel(sums_ref, cross_ref, ahead_ref, next_ref):
    next_ref[...] = ahead_ref[...] - dot3(split(sums_ref[...]), (cross_ref[0], cross_ref[1]), ((1,), (0,)))


def coefs_of(sums_ref, inverse):
    return jnp.concatenate(split(dot3(split(sums_ref[...]), split(inverse), ((1,), (1,))).T), axis=1)


def update_kernel(block, sums_ref, inverse_ref, residual_ref, high_ref, low_ref, out_ref, residual_v, columns_v, inverse_v, sems):
    width = residual_ref.shape[1]
    parts = pieces(residual_ref.shape[0], HALF_STEP)
    inverse_in = copy_of(inverse_ref.at[block], inverse_v, sems.at[4, 0])
    copies = [
        [
            copy_of(high_ref.at[at], columns_v.at[0, at], sems.at[0, i]),
            copy_of(low_ref.at[at], columns_v.at[1, at], sems.at[1, i]),
            copy_of(residual_ref.at[at], residual_v.at[at], sems.at[2, i]),
        ]
        for i, at in enumerate(parts)
    ]
    inverse_in.wait()
    coefs = coefs_of(sums_ref, inverse_v[...])
    out = []
    for index, at in enumerate(parts):
        wait_all(*copies[index])
        both = dot(columns_v[0, at, :], coefs, ((1,), (0,)))
        residual_v[at, :] -= both[:, :width] + both[:, width:] + dot(columns_v[1, at, :], coefs[:, :width], ((1,), (0,)))
        out.append(copy_of(residual_v.at[at], out_ref.at[at], sems.at[3, index]))
    wait_all(*out)


def last_kernel(sums_ref, inverse_ref, high_ref, residual_ref, low_ref, out_ref, residual_v, low_v, sems):
    width = residual_ref.shape[1]
    residual_in = copy_of(residual_ref, residual_v, sems.at[0, 0])
    low_in = copy_of(low_ref, low_v, sems.at[1, 0])
    coefs = coefs_of(sums_ref, inverse_ref[0])
    residual_in.wait()
    for at in pieces(residual_ref.shape[0]):
        both = dot(high_ref[at, :], coefs, ((1,), (0,)))
        residual_v[at, :] -= both[:, :width] + both[:, width:]
    low_in.wait()
    out = []
    for index, at in enumerate(pieces(residual_ref.shape[0], HALF_STEP)):
        residual_v[at, :] -= dot(low_v[at, :], coefs[:, :width], ((1,), (0,)))
        out.append(copy_of(residual_v.at[at], out_ref.at[at], sems.at[3, index]))
    wait_all(*out)


SPACES = {"V": pltpu.VMEM, "H": pltpu.HBM, "S": pltpu.SMEM}


def local(kernel, args, places, outs, scratch_shapes, flops, name):
    args = [pltpu.with_memory_space_constraint(a, SPACES[p]) if p != "S" else a for a, p in zip(args, places)]
    moved = sum(a.size * a.dtype.itemsize for a in args)
    made = pl.pallas_call(
        kernel,
        out_shape=[SPACES[p](shape, dtype) for p, shape, dtype in outs],
        in_specs=[pl.BlockSpec(memory_space=SPACES[p]) for p in places],
        out_specs=[pl.BlockSpec(memory_space=SPACES[p]) for p, _, _ in outs],
        scratch_shapes=scratch_shapes,
        cost_estimate=pl.CostEstimate(flops=flops, bytes_accessed=moved, transcendentals=0),
        compiler_params=pltpu.CompilerParams(vmem_limit_bytes=LIMIT),
        name=name,
    )(*args)
    return made if len(outs) > 1 else made[0]


def columns_and_sums(live, residual, samples, slots, held, resident):
    (rows, width), feat, size = residual.shape, samples.shape[1], slots.shape[1]
    scratch = [pltpu.VMEM((2, rows, size), BF16), pltpu.SemaphoreType.DMA((4, len(pieces(rows))))]
    return local(
        functools.partial(columns_kernel, resident),
        (live, residual, samples, slots, *held),
        ("SVVV" if resident else "SHHV") + "V" * len(held),
        [("H", (rows, size), BF16), ("H", (rows, size), BF16), ("V", (width, size), F32)],
        scratch if resident else [*scratch, pltpu.VMEM((rows, width), F32), pltpu.VMEM((rows, feat), F32)],
        6 * rows * size * (feat + width),
        "columns",
    )


def sum_over_rows(totals, groups, during_first, during_second=None):
    order = order_of(groups, SUMS_SEED)
    width, size = totals.shape
    piece = round_up(width, groups) // groups
    padded = jnp.pad(totals, ((0, piece * groups - width), (0, 0))) if piece * groups != width else totals
    got = exchange(padded.reshape(groups, piece, size), order)
    got, made = lax.optimization_barrier((got, during_first()))
    own = jnp.sum(got, axis=0)
    back = exchange(jnp.broadcast_to(own[None], (groups, piece, size)), order)
    more = None
    if during_second is not None:
        back, more = lax.optimization_barrier((back, during_second(made)))
    return back.reshape(groups * piece, size)[:width], made, more


def on_device(groups, cores, counts, samples, targets, point_ids, block_inverse):
    rows_here, feat = samples.shape
    blocks, size = point_ids.shape
    mean = blocks * size / groups
    cap = round_up(max(1, round((mean + 4 * mean**0.5) / cores)), 8)

    order = order_of(groups, POINTS_SEED)
    rows, slots, most = pick(point_ids, samples, order, cores, cap)

    def general(rows):
        ids = jnp.pad(point_ids.reshape(-1), (0, cores * groups * cap - blocks * size), constant_values=-1)
        ids = lax.dynamic_slice_in_dim(ids, lax.axis_index("tgt") * groups * cap, groups * cap)
        local = ids - lax.axis_index("rows") * rows_here
        owned = (local >= 0) & (local < rows_here)
        taken = jnp.take(samples, jnp.clip(local, 0, rows_here - 1), axis=0)
        taken = jnp.where(owned[:, None], taken, 0.0)
        return jnp.sum(exchange(taken.reshape(groups, cap, feat), order), axis=0)

    rows = lax.cond(most[0] > cap * cores, general, lambda rows: rows, rows)
    got = exchange(jnp.broadcast_to(rows[None], (groups, cap, feat)), order).reshape(groups * cap, feat)
    held = [got]
    for shift in range(1, cores):
        held.append(lax.ppermute(got, "tgt", [((c + shift) % cores, c) for c in range(cores)]))

    slots = [slots[:, b * size : (b + 1) * size] for b in range(blocks)]
    width = targets.shape[1]
    parts = len(pieces(rows_here))
    columns_v = pltpu.VMEM((2, rows_here, size), BF16)
    residual_v = pltpu.VMEM((rows_here, width), F32)
    inverse_v = pltpu.VMEM((size, size), F32)
    sems = pltpu.SemaphoreType.DMA((5, parts))

    def cross_of(columns, following, b):
        return local(
            functools.partial(cross_kernel, b),
            (*columns, *following, block_inverse),
            "HHHHH",
            [("V", (2, size, size), BF16)],
            [columns_v, columns_v, inverse_v, sems],
            6 * rows_here * size * size,
            "cross",
        )

    def updated(sums, residual, columns, b):
        return local(
            functools.partial(update_kernel, b),
            (sums, block_inverse, residual, *columns),
            "VHHHH",
            [("H", (rows_here, width), F32)],
            [residual_v, columns_v, inverse_v, sems],
            6 * rows_here * size * width,
            "update",
        )

    residual = targets
    *columns, totals = columns_and_sums(counts, residual, samples, slots[0], held, True)
    sums = before = None
    for b in range(blocks):
        def first(b=b, sums=sums, residual=residual, before=before):
            now = residual if b == 0 else updated(sums, residual, before, b - 1)
            if b + 1 == blocks:
                return now, block_inverse[b : b + 1]
            return (now, *columns_and_sums(counts, now, samples, slots[b + 1], held, False))

        def second(made, b=b, columns=columns):
            return cross_of(columns, made[1:3], b)

        sums, made, cross = sum_over_rows(totals, groups, first, second if b + 1 < blocks else None)
        residual, before = made[0], columns
        if b + 1 < blocks:
            _, *columns, ahead = made
            out = [("V", (width, size), F32)]
            totals = local(next_kernel, (sums, cross, ahead), "VVV", out, [], 6 * width * size * size, "next")
    return local(
        last_kernel,
        (sums, made[1], columns[0], residual, columns[1]),
        "VVVHH",
        [("H", (rows_here, width), F32)],
        [residual_v, pltpu.VMEM((rows_here, size), BF16), sems],
        6 * rows_here * size * width,
        "last",
    )


def solution(mesh):
    return jax.shard_map(
        functools.partial(on_device, mesh.shape["rows"], mesh.shape["tgt"]),
        mesh=mesh,
        in_specs=(P("rows"), P("rows", None), P("rows", "tgt"), P(), P()),
        out_specs=P("rows", "tgt"),
        check_vma=False,
    )
```

```python
import functools
import random

import jax
import jax.numpy as jnp
from jax import lax
from jax.experimental import pallas as pl
from jax.experimental.pallas import tpu as pltpu
from jax.sharding import PartitionSpec as P

F32 = jnp.float32
BF16 = jnp.bfloat16
ROWS_STEP = 512
HALF_STEP = 1024
LIMIT = 24 * 2**20
POINTS_SEED = 14
SUMS_SEED = 152


def order_of(groups, seed):
    order = list(range(groups))
    random.Random(seed).shuffle(order)
    return order


def exchange(x, order):
    return lax.all_to_all(x, "rows", 0, 0, axis_index_groups=[order])


def round_up(value, unit):
    return -(-value // unit) * unit


def split(x):
    high = x.astype(BF16)
    return high, (x - high.astype(F32)).astype(BF16)


def dot(a, b, dims):
    return lax.dot_general(a, b, (dims, ((), ())), preferred_element_type=F32)


def dot3(a, b, dims):
    return dot(a[0], b[0], dims) + dot(a[0], b[1], dims) + dot(a[1], b[0], dims)


def pick_kernel(order, cores, cap, ids_ref, samples_ref, rows_ref, slots_ref, most_ref, index_v, index_s, sems):
    rows_here, groups = samples_ref.shape[0], len(order)
    me, core = lax.axis_index("rows"), lax.axis_index("tgt")
    ids = jnp.concatenate([ids_ref[b : b + 1, :] for b in range(ids_ref.shape[0])], axis=1)
    count = ids.shape[1]
    owner = lax.div(ids, jnp.int32(rows_here))
    local = ids - owner * rows_here
    mine = lax.broadcasted_iota(jnp.int32, (groups, count), 0) == owner
    seen = mine.astype(jnp.int32)
    lane = lax.broadcasted_iota(jnp.int32, (groups, count), 1)
    step = 1
    while step < count:
        seen = seen + jnp.where(lane >= step, pltpu.roll(seen, step, 1), 0)
        step *= 2
    most = jnp.max(seen)
    rank = jnp.sum(jnp.where(mine, seen, 0), axis=0, keepdims=True) - 1
    half = lax.div(rank, jnp.int32(cap))
    turn = jnp.zeros_like(owner)
    for index, device in enumerate(order):
        turn = jnp.where(owner == device, index, turn)
    packed = (half * groups + turn) * cap + (rank - half * cap)
    place = lax.broadcasted_iota(jnp.int32, (1, count), 1)
    slots_ref[...] = jnp.where(most > cap * cores, place, packed)
    most_ref[0] = most

    wanted = lax.broadcasted_iota(jnp.int32, (cap, count), 0) + core * cap
    chosen = jnp.where((wanted == rank) & (owner == me), local, 0)
    index_v[...] = jnp.broadcast_to(jnp.sum(chosen, axis=1, keepdims=True), index_v.shape)
    move = pltpu.make_async_copy(index_v, index_s, sems.at[0])
    move.start()
    move.wait()

    @pl.loop(0, cap)
    def _(k):
        pltpu.make_async_copy(samples_ref.at[pl.ds(index_s[k, 0], 1)], rows_ref.at[pl.ds(k, 1)], sems.at[1]).start()

    pltpu.make_async_copy(samples_ref.at[pl.ds(0, cap)], rows_ref, sems.at[1]).wait()


def pick(ids, samples, order, cores, cap):
    count = ids.shape[0] * ids.shape[1]
    vmem = pl.BlockSpec(memory_space=pltpu.VMEM)
    return pl.pallas_call(
        functools.partial(pick_kernel, order, cores, cap),
        out_shape=(
            jax.ShapeDtypeStruct((cap, samples.shape[1]), F32),
            jax.ShapeDtypeStruct((1, count), jnp.int32),
            jax.ShapeDtypeStruct((1,), jnp.int32),
        ),
        in_specs=[vmem, pl.BlockSpec(memory_space=pl.ANY)],
        out_specs=(vmem, vmem, pl.BlockSpec(memory_space=pltpu.SMEM)),
        scratch_shapes=[
            pltpu.VMEM((cap, 128), jnp.int32),
            pltpu.SMEM((cap, 128), jnp.int32),
            pltpu.SemaphoreType.DMA((2,)),
        ],
        name="pick",
    )(ids, samples)


def pieces(rows, step=ROWS_STEP):
    step = min(step, rows)
    return [pl.ds(start, step) for start in range(0, rows, step)]


def copy_of(source, target, sem):
    copy = pltpu.make_async_copy(source, target, sem)
    copy.start()
    return copy


def copies_of(source, target, sems, parts):
    rows_of = lambda ref, at: ref.at[at] if len(ref.shape) == 2 else ref.at[:, at]
    return [copy_of(rows_of(source, at), rows_of(target, at), sems.at[i]) for i, at in enumerate(parts)]


def wait_all(*copies):
    for copy in copies:
        copy.wait()


def unpack(held, slots):
    depth, feat = held[0].shape
    cores = len(held)
    core = lax.axis_index("tgt")
    total = None
    for shift, ref in enumerate(held):
        base = lax.rem(core + shift, cores) * depth
        slot = lax.broadcasted_iota(jnp.int32, (depth, slots.shape[1]), 0) + base
        taken = jnp.where(slot == slots, 1.0, 0.0).astype(BF16)
        found = dot(jnp.concatenate(split(ref[...]), axis=1), taken, ((0,), (0,)))
        total = found if total is None else total + found
    return total[:feat].astype(BF16), total[feat:].astype(BF16)


def make_columns(live_ref, samples_ref, points, columns_v, high_ref, low_ref, sems):
    rows, feat = samples_ref.shape
    scale = 0.5 / feat**0.5
    copies = []
    for index, half in enumerate(pieces(rows, HALF_STEP)):
        for at in [pl.ds(half.start + part.start, part.size) for part in pieces(half.size)]:
            base = dot3(split(samples_ref[at, :]), points, ((1,), (0,))) * scale + 1.0
            slot = lax.broadcasted_iota(jnp.int32, (at.size, 1), 0) + at.start
            columns_v[0, at, :], columns_v[1, at, :] = split(jnp.where(slot < live_ref[0], base * base * base, 0.0))
        for kind, ref in enumerate((high_ref, low_ref)):
            copies.append(copy_of(columns_v.at[kind, half], ref.at[half], sems.at[kind, index]))
    return copies


def sum_high(residual, high):
    width = residual[0].shape[1]
    both = dot(jnp.concatenate(residual, axis=1), high, ((0,), (0,)))
    return both[:width] + both[width:]


def first_kernel(live_ref, residual_ref, samples_ref, slots_ref, *refs):
    *held, high_ref, low_ref, total_ref, points_ref, points_v, columns_v, sems = refs
    others, _, _, size = points_ref.shape
    points = unpack(held, slots_ref[:, :size])
    for b in range(others):
        points_v[b, 0], points_v[b, 1] = unpack(held, slots_ref[:, (b + 1) * size : (b + 2) * size])
    points_out = copy_of(points_v, points_ref, sems.at[3, 0])
    copies = make_columns(live_ref, samples_ref, points, columns_v, high_ref, low_ref, sems)
    for index, at in enumerate(pieces(samples_ref.shape[0])):
        residual = split(residual_ref[at, :])
        term = sum_high(residual, columns_v[0, at, :]) + dot(residual[0], columns_v[1, at, :], ((0,), (0,)))
        total_ref[...] = term if index == 0 else total_ref[...] + term
    wait_all(points_out, *copies)


def beside_kernel(block, live_ref, samples_ref, points_ref, inverse_ref, high_ref, low_ref, inverse_v, points_v, columns_v, sems):
    points_in = copy_of(points_ref.at[block], points_v, sems.at[3, 0])
    inverse_in = copy_of(inverse_ref.at[block], inverse_v, sems.at[2, 0])
    points_in.wait()
    points = (points_v[0], points_v[1])
    wait_all(inverse_in, *make_columns(live_ref, samples_ref, points, columns_v, high_ref, low_ref, sems))


def coefs_of(sums_ref, inverse_ref):
    return jnp.concatenate(split(dot3(split(sums_ref[...]), split(inverse_ref[...]), ((1,), (1,))).T), axis=1)


def halves(source, target, sems):
    return [copy_of(source.at[at], target.at[at], sems.at[i]) for i, at in enumerate(pieces(source.shape[0], HALF_STEP))]


def update(coefs, residual_in, high_in, low_in, residual_v, columns_v, out_ref, sems):
    width = residual_v.shape[1]
    parts = pieces(residual_v.shape[0], HALF_STEP)
    for index, half in enumerate(parts):
        wait_all(residual_in[index], high_in[index])
        both = dot(columns_v[0, half, :], coefs, ((1,), (0,)))
        residual_v[half, :] -= both[:, :width] + both[:, width:]
    out = []
    for index, half in enumerate(parts):
        low_in[index].wait()
        residual_v[half, :] -= dot(columns_v[1, half, :], coefs[:, :width], ((1,), (0,)))
        out.append(copy_of(residual_v.at[half], out_ref.at[half], sems.at[index]))
    return out


def middle_kernel(block, sums_ref, inverse_ref, residual_ref, high_ref, low_ref, next_high, next_low, inverses, *refs):
    out_ref, total_ref, inverse_v, residual_v, columns_v, next_v, sems = refs
    residual_in = halves(residual_ref, residual_v, sems.at[0])
    high_in = halves(high_ref, columns_v.at[0], sems.at[1])
    low_in = halves(low_ref, columns_v.at[1], sems.at[2])
    next_in = [copy_of(ref, next_v.at[kind], sems.at[3, kind]) for kind, ref in enumerate((next_high, next_low))]
    inverse_in = copy_of(inverses.at[block + 1], inverse_v, sems.at[4, 0])
    coefs = coefs_of(sums_ref, inverse_ref)
    out = update(coefs, residual_in, high_in, low_in, residual_v, columns_v, out_ref, sems.at[5])
    next_in[0].wait()
    parts = pieces(residual_v.shape[0])
    for index, at in enumerate(parts):
        term = sum_high(split(residual_v[at, :]), next_v[0, at, :])
        total_ref[...] = term if index == 0 else total_ref[...] + term
    next_in[1].wait()
    for at in parts:
        total_ref[...] += dot(residual_v[at, :].astype(BF16), next_v[1, at, :], ((0,), (0,)))
    wait_all(inverse_in, *out)


def last_kernel(sums_ref, inverse_ref, residual_ref, high_ref, low_ref, out_ref, residual_v, columns_v, sems):
    residual_in = halves(residual_ref, residual_v, sems.at[0])
    high_in = halves(high_ref, columns_v.at[0], sems.at[1])
    low_in = halves(low_ref, columns_v.at[1], sems.at[2])
    coefs = coefs_of(sums_ref, inverse_ref)
    wait_all(*update(coefs, residual_in, high_in, low_in, residual_v, columns_v, out_ref, sems.at[3]))


SPACES = {"V": pltpu.VMEM, "H": pltpu.HBM, "S": pltpu.SMEM}


def local(kernel, args, places, outs, scratch_shapes, flops, name):
    args = [pltpu.with_memory_space_constraint(a, SPACES[p]) if p != "S" else a for a, p in zip(args, places)]
    moved = sum(a.size * a.dtype.itemsize for a in args)
    made = pl.pallas_call(
        kernel,
        out_shape=[SPACES[p](shape, dtype) for p, shape, dtype in outs],
        in_specs=[pl.BlockSpec(memory_space=SPACES[p]) for p in places],
        out_specs=[pl.BlockSpec(memory_space=SPACES[p]) for p, _, _ in outs],
        scratch_shapes=scratch_shapes,
        cost_estimate=pl.CostEstimate(flops=flops, bytes_accessed=moved, transcendentals=0),
        compiler_params=pltpu.CompilerParams(vmem_limit_bytes=LIMIT),
        name=name,
    )(*args)
    return made if len(outs) > 1 else made[0]


def sum_over_rows(totals, groups, beside):
    order = order_of(groups, SUMS_SEED)
    width, size = totals.shape
    piece = round_up(width, groups) // groups
    padded = jnp.pad(totals, ((0, piece * groups - width), (0, 0))) if piece * groups != width else totals
    got = exchange(padded.reshape(groups, piece, size), order)
    made = None
    if beside is not None:
        got, made = lax.optimization_barrier((got, beside()))
    own = jnp.sum(got, axis=0)
    back = exchange(jnp.broadcast_to(own[None], (groups, piece, size)), order)
    return back.reshape(groups * piece, size)[:width], made


def on_device(groups, cores, counts, samples, targets, point_ids, block_inverse):
    rows_here, feat = samples.shape
    blocks, size = point_ids.shape
    mean = blocks * size / groups
    cap = round_up(max(1, round((mean + 4 * mean**0.5) / cores)), 8)

    order = order_of(groups, POINTS_SEED)
    rows, slots, most = pick(point_ids, samples, order, cores, cap)

    def general(rows):
        ids = jnp.pad(point_ids.reshape(-1), (0, cores * groups * cap - blocks * size), constant_values=-1)
        ids = lax.dynamic_slice_in_dim(ids, lax.axis_index("tgt") * groups * cap, groups * cap)
        local = ids - lax.axis_index("rows") * rows_here
        owned = (local >= 0) & (local < rows_here)
        taken = jnp.take(samples, jnp.clip(local, 0, rows_here - 1), axis=0)
        taken = jnp.where(owned[:, None], taken, 0.0)
        return jnp.sum(exchange(taken.reshape(groups, cap, feat), order), axis=0)

    rows = lax.cond(most[0] > cap * cores, general, lambda rows: rows, rows)
    got = exchange(jnp.broadcast_to(rows[None], (groups, cap, feat)), order).reshape(groups * cap, feat)
    held = [got]
    for shift in range(1, cores):
        held.append(lax.ppermute(got, "tgt", [((c + shift) % cores, c) for c in range(cores)]))

    width = targets.shape[1]
    columns_v = pltpu.VMEM((2, rows_here, size), BF16)
    residual_v = pltpu.VMEM((rows_here, width), F32)
    sems = pltpu.SemaphoreType.DMA((6, len(pieces(rows_here, HALF_STEP))))
    columns_out = [("H", (rows_here, size), BF16)] * 2
    inverse_out = ("V", (size, size), F32)
    totals_out = ("V", (width, size), F32)
    work = 6 * rows_here * size

    residual = targets
    *columns, totals, points = local(
        first_kernel,
        (counts, residual, samples, slots, *held),
        "SVVV" + "V" * cores,
        [*columns_out, totals_out, ("H", (blocks - 1, 2, feat, size), BF16)],
        [pltpu.VMEM((blocks - 1, 2, feat, size), BF16), columns_v, sems],
        work * (feat + width),
        "first",
    )
    for b in range(blocks - 1):

        def beside(b=b, points=points):
            args = (counts, samples, points, block_inverse)
            outs = [*columns_out, inverse_out]
            scratch = [pltpu.VMEM((2, feat, size), BF16), columns_v, sems]
            return local(functools.partial(beside_kernel, b), args, "SVHH", outs, scratch, work * feat, "beside")

        sums, (*following, inverse) = sum_over_rows(totals, groups, beside)
        residual, totals, inverse = local(
            functools.partial(middle_kernel, b),
            (sums, inverse, residual, *columns, *following, block_inverse),
            "VVHHHHHH",
            [("H", (rows_here, width), F32), totals_out, inverse_out],
            [residual_v, columns_v, columns_v, sems],
            2 * work * width,
            "middle",
        )
        columns = following
    sums, _ = sum_over_rows(totals, groups, None)
    return local(
        last_kernel,
        (sums, inverse, residual, *columns),
        "VVHHH",
        [("H", (rows_here, width), F32)],
        [residual_v, columns_v, sems],
        work * width,
        "last",
    )


def solution(mesh):
    return jax.shard_map(
        functools.partial(on_device, mesh.shape["rows"], mesh.shape["tgt"]),
        mesh=mesh,
        in_specs=(P("rows"), P("rows", None), P("rows", "tgt"), P(), P()),
        out_specs=P("rows", "tgt"),
        check_vma=False,
    )
```

```python
import functools
import random

import jax
import jax.numpy as jnp
from jax import lax
from jax.experimental import pallas as pl
from jax.experimental.pallas import tpu as pltpu
from jax.sharding import PartitionSpec as P

F32 = jnp.float32
BF16 = jnp.bfloat16
ROWS_STEP = 512
HALF_STEP = 1024
LIMIT = 24 * 2**20
POINTS_SEED = 14
SUMS_SEED = 152


def order_of(groups, seed):
    order = list(range(groups))
    random.Random(seed).shuffle(order)
    return order


def exchange(x, order):
    return lax.all_to_all(x, "rows", 0, 0, axis_index_groups=[order])


def round_up(value, unit):
    return -(-value // unit) * unit


def split(x):
    high = x.astype(BF16)
    return high, (x - high.astype(F32)).astype(BF16)


def dot(a, b, dims):
    return lax.dot_general(a, b, (dims, ((), ())), preferred_element_type=F32)


def dot3(a, b, dims):
    return dot(a[0], b[0], dims) + dot(a[0], b[1], dims) + dot(a[1], b[0], dims)


def pick_kernel(order, cores, cap, ids_ref, samples_ref, rows_ref, slots_ref, most_ref, index_v, index_s, sems):
    rows_here, groups = samples_ref.shape[0], len(order)
    me, core = lax.axis_index("rows"), lax.axis_index("tgt")
    ids = jnp.concatenate([ids_ref[b : b + 1, :] for b in range(ids_ref.shape[0])], axis=1)
    count = ids.shape[1]
    owner = lax.div(ids, jnp.int32(rows_here))
    local = ids - owner * rows_here
    mine = lax.broadcasted_iota(jnp.int32, (groups, count), 0) == owner
    seen = mine.astype(jnp.int32)
    lane = lax.broadcasted_iota(jnp.int32, (groups, count), 1)
    step = 1
    while step < count:
        seen = seen + jnp.where(lane >= step, pltpu.roll(seen, step, 1), 0)
        step *= 2
    most = jnp.max(seen)
    rank = jnp.sum(jnp.where(mine, seen, 0), axis=0, keepdims=True) - 1
    half = lax.div(rank, jnp.int32(cap))
    turn = jnp.zeros_like(owner)
    for index, device in enumerate(order):
        turn = jnp.where(owner == device, index, turn)
    packed = (half * groups + turn) * cap + (rank - half * cap)
    place = lax.broadcasted_iota(jnp.int32, (1, count), 1)
    slots_ref[...] = jnp.where(most > cap * cores, place, packed)
    most_ref[0] = most

    wanted = lax.broadcasted_iota(jnp.int32, (cap, count), 0) + core * cap
    chosen = jnp.where((wanted == rank) & (owner == me), local, 0)
    index_v[...] = jnp.broadcast_to(jnp.sum(chosen, axis=1, keepdims=True), index_v.shape)
    move = pltpu.make_async_copy(index_v, index_s, sems.at[0])
    move.start()
    move.wait()

    @pl.loop(0, cap)
    def _(k):
        pltpu.make_async_copy(samples_ref.at[pl.ds(index_s[k, 0], 1)], rows_ref.at[pl.ds(k, 1)], sems.at[1]).start()

    pltpu.make_async_copy(samples_ref.at[pl.ds(0, cap)], rows_ref, sems.at[1]).wait()


def pieces(rows, step=ROWS_STEP):
    step = min(step, rows)
    return [pl.ds(start, step) for start in range(0, rows, step)]


def copy_of(source, target, sem):
    copy = pltpu.make_async_copy(source, target, sem)
    copy.start()
    return copy


def halves(source, target, sems):
    return [copy_of(source.at[at], target.at[at], sems.at[i]) for i, at in enumerate(pieces(source.shape[0], HALF_STEP))]


def wait_all(*copies):
    for copy in copies:
        copy.wait()


def found_in(ref, slots, shift, cores):
    depth = ref.shape[0]
    base = lax.rem(lax.axis_index("tgt") + shift, cores) * depth
    slot = lax.broadcasted_iota(jnp.int32, (depth, slots.shape[1]), 0) + base
    taken = jnp.where(slot == slots, 1.0, 0.0).astype(BF16)
    return dot(jnp.concatenate(split(ref[...]), axis=1), taken, ((0,), (0,)))


def own_kernel(cores, slots_ref, held_ref, found_ref):
    blocks, _, size = found_ref.shape
    for b in range(blocks):
        found_ref[b] = found_in(held_ref, slots_ref[:, b * size : (b + 1) * size], 0, cores).astype(BF16)


def make_columns(live_ref, samples_ref, points, high_v, low_v, high_ref, low_ref, sems):
    rows, feat = samples_ref.shape
    scale = 0.5 / feat**0.5
    copies = []
    for index, half in enumerate(pieces(rows, HALF_STEP)):
        for at in [pl.ds(half.start + part.start, part.size) for part in pieces(half.size)]:
            base = dot3(split(samples_ref[at, :]), points, ((1,), (0,))) * scale + 1.0
            slot = lax.broadcasted_iota(jnp.int32, (at.size, 1), 0) + at.start
            high_v[at, :], low_v[at, :] = split(jnp.where(slot < live_ref[0], base * base * base, 0.0))
        copies.append(copy_of(high_v.at[half], high_ref.at[half], sems.at[0, index]))
        copies.append(copy_of(low_v.at[half], low_ref.at[half], sems.at[1, index]))
    return copies


def sum_high(residual, high):
    width = residual[0].shape[1]
    both = dot(jnp.concatenate(residual, axis=1), high, ((0,), (0,)))
    return both[:width] + both[width:]


def first_kernel(live_ref, residual_ref, samples_ref, slots_ref, found_ref, *refs):
    *held, high_ref, low_ref, total_ref, points_ref, points_v, columns_v, sems = refs
    blocks, _, size = found_ref.shape
    feat = samples_ref.shape[1]
    for b in range(blocks):
        found = found_ref[b].astype(F32)
        for shift, ref in enumerate(held):
            found = found + found_in(ref, slots_ref[:, b * size : (b + 1) * size], shift + 1, len(held) + 1)
        points_v[b, 0], points_v[b, 1] = found[:feat].astype(BF16), found[feat:].astype(BF16)
    points_out = copy_of(points_v, points_ref, sems.at[3, 0])
    points = (points_v[0, 0], points_v[0, 1])
    copies = make_columns(live_ref, samples_ref, points, columns_v.at[0], columns_v.at[1], high_ref, low_ref, sems)
    for index, at in enumerate(pieces(samples_ref.shape[0])):
        residual = split(residual_ref[at, :])
        term = sum_high(residual, columns_v[0, at, :]) + dot(residual[0], columns_v[1, at, :], ((0,), (0,)))
        total_ref[...] = term if index == 0 else total_ref[...] + term
    wait_all(points_out, *copies)


def beside_kernel(block, live_ref, samples_ref, points_ref, inverse_ref, high_ref, low_ref, inverse_v, points_v, columns_v, sems):
    points_in = copy_of(points_ref.at[block + 1], points_v, sems.at[3, 0])
    inverse_in = copy_of(inverse_ref.at[block], inverse_v, sems.at[2, 0])
    points_in.wait()
    points = (points_v[0], points_v[1])
    wait_all(inverse_in, *make_columns(live_ref, samples_ref, points, columns_v.at[0], columns_v.at[1], high_ref, low_ref, sems))


def coefs_of(sums_ref, inverse_ref):
    return jnp.concatenate(split(dot3(split(sums_ref[...]), split(inverse_ref[...]), ((1,), (1,))).T), axis=1)


def update_high(coefs, residual_ref, columns_v, out_ref, waits):
    width = residual_ref.shape[1]
    for half, ready in zip(pieces(residual_ref.shape[0], HALF_STEP), waits):
        wait_all(*ready)
        both = dot(columns_v[0, half, :], coefs, ((1,), (0,)))
        out_ref[half, :] = residual_ref[half, :] - (both[:, :width] + both[:, width:])


def middle_kernel(block, sums_ref, inverse_ref, residual_ref, high_ref, low_ref, next_high, next_low, inverses, *refs):
    out_ref, total_ref, inverse_v, residual_v, columns_v, next_v, sems = refs
    residual_in = halves(residual_ref, residual_v, sems.at[0])
    high_in = halves(high_ref, columns_v.at[0], sems.at[1])
    low_in = halves(low_ref, columns_v.at[1], sems.at[2])
    next_in = [copy_of(ref, next_v.at[kind], sems.at[3, kind]) for kind, ref in enumerate((next_high, next_low))]
    inverse_in = copy_of(inverses.at[block + 1], inverse_v, sems.at[4, 0])
    coefs = coefs_of(sums_ref, inverse_ref)
    width = out_ref.shape[1]
    update_high(coefs, residual_v, columns_v, out_ref, zip(residual_in, high_in))
    wait_all(*low_in, next_in[0])
    parts = pieces(out_ref.shape[0])
    for index, at in enumerate(parts):
        residual = out_ref[at, :] - dot(columns_v[1, at, :], coefs[:, :width], ((1,), (0,)))
        out_ref[at, :] = residual
        term = sum_high(split(residual), next_v[0, at, :])
        total_ref[...] = term if index == 0 else total_ref[...] + term
    next_in[1].wait()
    for at in parts:
        total_ref[...] += dot(out_ref[at, :].astype(BF16), next_v[1, at, :], ((0,), (0,)))
    inverse_in.wait()


def last_kernel(sums_ref, inverse_ref, residual_ref, high_ref, low_ref, out_ref, residual_v, columns_v, sems):
    high_in = halves(high_ref, columns_v.at[0], sems.at[1])
    low_in = halves(low_ref, columns_v.at[1], sems.at[2])
    coefs = coefs_of(sums_ref, inverse_ref)
    width = residual_ref.shape[1]
    update_high(coefs, residual_ref, columns_v, residual_v, zip(high_in))
    out = []
    for index, half in enumerate(pieces(out_ref.shape[0], HALF_STEP)):
        low_in[index].wait()
        residual_v[half, :] -= dot(columns_v[1, half, :], coefs[:, :width], ((1,), (0,)))
        out.append(copy_of(residual_v.at[half], out_ref.at[half], sems.at[3, index]))
    wait_all(*out)


SPACES = {"V": pltpu.VMEM, "H": pltpu.HBM, "S": pltpu.SMEM}


def local(kernel, args, places, outs, scratch_shapes, flops, name):
    args = [pltpu.with_memory_space_constraint(a, SPACES[p]) if p != "S" else a for a, p in zip(args, places)]
    moved = sum(a.size * a.dtype.itemsize for a in args)
    made = pl.pallas_call(
        kernel,
        out_shape=[SPACES[p](shape, dtype) for p, shape, dtype in outs],
        in_specs=[pl.BlockSpec(memory_space=SPACES[p]) for p in places],
        out_specs=[pl.BlockSpec(memory_space=SPACES[p]) for p, _, _ in outs],
        scratch_shapes=scratch_shapes,
        cost_estimate=pl.CostEstimate(flops=flops, bytes_accessed=moved, transcendentals=0),
        compiler_params=pltpu.CompilerParams(vmem_limit_bytes=LIMIT),
        name=name,
    )(*args)
    return made if len(outs) > 1 else made[0]


def sum_over_rows(totals, groups, beside):
    order = order_of(groups, SUMS_SEED)
    width, size = totals.shape
    piece = round_up(width, groups) // groups
    padded = jnp.pad(totals, ((0, piece * groups - width), (0, 0))) if piece * groups != width else totals
    got = exchange(padded.reshape(groups, piece, size), order)
    made = None
    if beside is not None:
        got, made = lax.optimization_barrier((got, beside()))
    own = jnp.sum(got, axis=0)
    back = exchange(jnp.broadcast_to(own[None], (groups, piece, size)), order)
    return back.reshape(groups * piece, size)[:width], made


def on_device(groups, cores, counts, samples, targets, point_ids, block_inverse):
    rows_here, feat = samples.shape
    blocks, size = point_ids.shape
    mean = blocks * size / groups
    cap = round_up(max(1, round((mean + 4 * mean**0.5) / cores)), 8)

    order = order_of(groups, POINTS_SEED)
    rows, slots, most = local(
        functools.partial(pick_kernel, order, cores, cap),
        (point_ids, samples),
        "VH",
        [("V", (cap, feat), F32), ("V", (1, blocks * size), jnp.int32), ("S", (1,), jnp.int32)],
        [pltpu.VMEM((cap, 128), jnp.int32), pltpu.SMEM((cap, 128), jnp.int32), pltpu.SemaphoreType.DMA((2,))],
        0,
        "pick",
    )

    def general(rows):
        ids = jnp.pad(point_ids.reshape(-1), (0, cores * groups * cap - blocks * size), constant_values=-1)
        ids = lax.dynamic_slice_in_dim(ids, lax.axis_index("tgt") * groups * cap, groups * cap)
        local = ids - lax.axis_index("rows") * rows_here
        owned = (local >= 0) & (local < rows_here)
        taken = jnp.take(samples, jnp.clip(local, 0, rows_here - 1), axis=0)
        taken = jnp.where(owned[:, None], taken, 0.0)
        return jnp.sum(exchange(taken.reshape(groups, cap, feat), order), axis=0)

    rows = lax.cond(most[0] > cap * cores, general, lambda rows: rows, rows)
    got = exchange(jnp.broadcast_to(rows[None], (groups, cap, feat)), order).reshape(groups * cap, feat)
    held = [lax.ppermute(got, "tgt", [((c + shift) % cores, c) for c in range(cores)]) for shift in range(1, cores)]
    found = local(
        functools.partial(own_kernel, cores),
        (slots, got),
        "VV",
        [("V", (blocks, 2 * feat, size), BF16)],
        [],
        4 * groups * cap * feat * blocks * size,
        "own",
    )
    held, found = lax.optimization_barrier((held, found))

    width = targets.shape[1]
    columns_v = pltpu.VMEM((2, rows_here, size), BF16)
    residual_v = pltpu.VMEM((rows_here, width), F32)
    sems = pltpu.SemaphoreType.DMA((6, len(pieces(rows_here, HALF_STEP))))
    columns_out = [("H", (rows_here, size), BF16)] * 2
    inverse_out = ("V", (size, size), F32)
    totals_out = ("V", (width, size), F32)
    work = 6 * rows_here * size

    residual = targets
    *columns, totals, points = local(
        first_kernel,
        (counts, residual, samples, slots, found, *held),
        "SVVVV" + "V" * len(held),
        [*columns_out, totals_out, ("H", (blocks, 2, feat, size), BF16)],
        [pltpu.VMEM((blocks, 2, feat, size), BF16), columns_v, sems],
        work * (feat + width),
        "first",
    )
    for b in range(blocks - 1):

        def beside(b=b, points=points):
            args = (counts, samples, points, block_inverse)
            outs = [*columns_out, inverse_out]
            scratch = [pltpu.VMEM((2, feat, size), BF16), columns_v, sems]
            return local(functools.partial(beside_kernel, b), args, "SVHH", outs, scratch, work * feat, "beside")

        sums, (*following, inverse) = sum_over_rows(totals, groups, beside)
        residual, totals, inverse = local(
            functools.partial(middle_kernel, b),
            (sums, inverse, residual, *columns, *following, block_inverse),
            "VVHHHHHH",
            [("V", (rows_here, width), F32), totals_out, inverse_out],
            [residual_v, columns_v, columns_v, sems],
            2 * work * width,
            "middle",
        )
        columns = following
    sums, _ = sum_over_rows(totals, groups, None)
    return local(
        last_kernel,
        (sums, inverse, residual, *columns),
        "VVVHH",
        [("H", (rows_here, width), F32)],
        [residual_v, columns_v, sems],
        work * width,
        "last",
    )


def solution(mesh):
    return jax.shard_map(
        functools.partial(on_device, mesh.shape["rows"], mesh.shape["tgt"]),
        mesh=mesh,
        in_specs=(P("rows"), P("rows", None), P("rows", "tgt"), P(), P()),
        out_specs=P("rows", "tgt"),
        check_vma=False,
    )
```

```python
import functools
import random

import jax
import jax.numpy as jnp
from jax import lax
from jax.experimental import pallas as pl
from jax.experimental.pallas import tpu as pltpu
from jax.sharding import PartitionSpec as P

F32 = jnp.float32
BF16 = jnp.bfloat16
ROWS_STEP = 512
HALF_STEP = 1024
LIMIT = 24 * 2**20
POINTS_SEED = 14
SUMS_SEED = 152


def order_of(groups, seed):
    order = list(range(groups))
    random.Random(seed).shuffle(order)
    return order


def exchange(x, order):
    return lax.all_to_all(x, "rows", 0, 0, axis_index_groups=[order])


def round_up(value, unit):
    return -(-value // unit) * unit


def split(x):
    high = x.astype(BF16)
    return high, (x - high.astype(F32)).astype(BF16)


def dot(a, b, dims):
    return lax.dot_general(a, b, (dims, ((), ())), preferred_element_type=F32)


def dot3(a, b, dims):
    return dot(a[0], b[0], dims) + dot(a[0], b[1], dims) + dot(a[1], b[0], dims)


def pick_kernel(order, cores, cap, ids_ref, samples_ref, rows_ref, slots_ref, most_ref, index_v, index_s, sems):
    rows_here, groups = samples_ref.shape[0], len(order)
    me, core = lax.axis_index("rows"), lax.axis_index("tgt")
    ids = jnp.concatenate([ids_ref[b : b + 1, :] for b in range(ids_ref.shape[0])], axis=1)
    count = ids.shape[1]
    owner = lax.div(ids, jnp.int32(rows_here))
    local = ids - owner * rows_here
    mine = lax.broadcasted_iota(jnp.int32, (groups, count), 0) == owner
    seen = mine.astype(jnp.int32)
    lane = lax.broadcasted_iota(jnp.int32, (groups, count), 1)
    step = 1
    while step < count:
        seen = seen + jnp.where(lane >= step, pltpu.roll(seen, step, 1), 0)
        step *= 2
    most = jnp.max(seen)
    rank = jnp.sum(jnp.where(mine, seen, 0), axis=0, keepdims=True) - 1
    half = lax.div(rank, jnp.int32(cap))
    turn = jnp.zeros_like(owner)
    for index, device in enumerate(order):
        turn = jnp.where(owner == device, index, turn)
    packed = (half * groups + turn) * cap + (rank - half * cap)
    place = lax.broadcasted_iota(jnp.int32, (1, count), 1)
    slots_ref[...] = jnp.where(most > cap * cores, place, packed)
    most_ref[0] = most

    wanted = lax.broadcasted_iota(jnp.int32, (cap, count), 0) + core * cap
    chosen = jnp.where((wanted == rank) & (owner == me), local, 0)
    index_v[...] = jnp.broadcast_to(jnp.sum(chosen, axis=1, keepdims=True), index_v.shape)
    move = pltpu.make_async_copy(index_v, index_s, sems.at[0])
    move.start()
    move.wait()

    @pl.loop(0, cap)
    def _(k):
        pltpu.make_async_copy(samples_ref.at[pl.ds(index_s[k, 0], 1)], rows_ref.at[pl.ds(k, 1)], sems.at[1]).start()

    pltpu.make_async_copy(samples_ref.at[pl.ds(0, cap)], rows_ref, sems.at[1]).wait()


def pieces(rows, step=ROWS_STEP):
    step = min(step, rows)
    return [pl.ds(start, step) for start in range(0, rows, step)]


def copy_of(source, target, sem):
    copy = pltpu.make_async_copy(source, target, sem)
    copy.start()
    return copy


def stage(live_ref):
    return pl.when(live_ref[0] >= 0)


def wait_all(*copies):
    for copy in copies:
        copy.wait()


def found_in(ref, slots, shift, cores):
    depth = ref.shape[0]
    base = lax.rem(lax.axis_index("tgt") + shift, cores) * depth
    slot = lax.broadcasted_iota(jnp.int32, (depth, slots.shape[1]), 0) + base
    taken = jnp.where(slot == slots, 1.0, 0.0).astype(BF16)
    return dot(jnp.concatenate(split(ref[...]), axis=1), taken, ((0,), (0,)))


def own_kernel(cores, slots_ref, held_ref, found_ref):
    blocks, _, size = found_ref.shape
    for b in range(blocks):
        found_ref[b] = found_in(held_ref, slots_ref[:, b * size : (b + 1) * size], 0, cores).astype(BF16)


def make_columns(live_ref, samples_ref, points_of, columns_v, high_ref, low_ref, sems):
    rows, feat = samples_ref.shape
    scale = 0.5 / feat**0.5
    copies = []
    for index, half in enumerate(pieces(rows, HALF_STEP)):

        @stage(live_ref)
        def _():
            points = points_of()
            for at in [pl.ds(half.start + part.start, part.size) for part in pieces(half.size)]:
                base = dot3(split(samples_ref[at, :]), points, ((1,), (0,))) * scale + 1.0
                slot = lax.broadcasted_iota(jnp.int32, (at.size, 1), 0) + at.start
                columns_v[0, at, :], columns_v[1, at, :] = split(jnp.where(slot < live_ref[0], base * base * base, 0.0))

        for kind, ref in enumerate((high_ref, low_ref)):
            copies.append(copy_of(columns_v.at[kind, half], ref.at[half], sems.at[kind, index]))
    return copies


def sum_of(residual, high, low):
    width = residual.shape[1]
    residual = split(residual)
    both = dot(jnp.concatenate(residual, axis=1), high, ((0,), (0,)))
    return both[:width] + both[width:] + dot(residual[0], low, ((0,), (0,)))


def first_kernel(live_ref, residual_ref, samples_ref, slots_ref, found_ref, *refs):
    *held, high_ref, low_ref, total_ref, points_ref, points_v, columns_v, sems = refs
    blocks, _, size = found_ref.shape
    feat = samples_ref.shape[1]
    for b in range(blocks):
        found = found_ref[b].astype(F32)
        for shift, ref in enumerate(held):
            found = found + found_in(ref, slots_ref[:, b * size : (b + 1) * size], shift + 1, len(held) + 1)
        points_v[b, 0], points_v[b, 1] = found[:feat].astype(BF16), found[feat:].astype(BF16)
    copies = make_columns(live_ref, samples_ref, lambda: (points_v[0, 0], points_v[0, 1]), columns_v, high_ref, low_ref, sems)
    copies.append(copy_of(points_v, points_ref, sems.at[3, 0]))

    @stage(live_ref)
    def _():
        for index, at in enumerate(pieces(samples_ref.shape[0])):
            term = sum_of(residual_ref[at, :], columns_v[0, at, :], columns_v[1, at, :])
            total_ref[...] = term if index == 0 else total_ref[...] + term

    wait_all(*copies)


def beside_kernel(block, live_ref, samples_ref, points_ref, inverse_ref, high_ref, low_ref, inverse_v, points_v, columns_v, sems):
    points_in = copy_of(points_ref.at[block + 1], points_v, sems.at[3, 0])
    inverse_in = copy_of(inverse_ref.at[block], inverse_v, sems.at[2, 0])
    points_in.wait()
    copies = make_columns(live_ref, samples_ref, lambda: (points_v[0], points_v[1]), columns_v, high_ref, low_ref, sems)
    wait_all(inverse_in, *copies)


def coefs_of(sums_ref, inverse_ref):
    return jnp.concatenate(split(dot3(split(sums_ref[...]), split(inverse_ref[...]), ((1,), (1,))).T), axis=1)


def updated(residual, high, low, coefs):
    width = residual.shape[1]
    both = dot(high, coefs, ((1,), (0,)))
    return residual - (both[:, :width] + both[:, width:] + dot(low, coefs[:, :width], ((1,), (0,))))


def middle_kernel(block, live_ref, sums_ref, inverse_ref, residual_ref, high_ref, low_ref, next_high, next_low, inverses, *refs):
    out_ref, total_ref, inverse_v, coefs_v, residual_v, columns_v, next_v, sems = refs
    parts = pieces(out_ref.shape[0])
    first_in = [
        [
            copy_of(residual_ref.at[at], residual_v.at[at], sems.at[0, i]),
            copy_of(high_ref.at[at], columns_v.at[0, at], sems.at[1, i]),
            copy_of(low_ref.at[at], columns_v.at[1, at], sems.at[2, i]),
        ]
        for i, at in enumerate(parts)
    ]
    next_in = [
        [copy_of(ref.at[at], next_v.at[kind, at], sems.at[3 + kind, i]) for kind, ref in enumerate((next_high, next_low))]
        for i, at in enumerate(parts)
    ]
    inverse_in = copy_of(inverses.at[block + 1], inverse_v, sems.at[5, 0])

    @stage(live_ref)
    def _():
        coefs_v[...] = coefs_of(sums_ref, inverse_ref)

    for copies, at in zip(first_in, parts):
        wait_all(*copies)

        @stage(live_ref)
        def _():
            out_ref[at, :] = updated(residual_v[at, :], columns_v[0, at, :], columns_v[1, at, :], coefs_v[...])

    for copies, at in zip(next_in, parts):
        wait_all(*copies)

        @stage(live_ref)
        def _():
            term = sum_of(out_ref[at, :], next_v[0, at, :], next_v[1, at, :])
            total_ref[...] = term if at.start == 0 else total_ref[...] + term

    inverse_in.wait()


def last_kernel(live_ref, sums_ref, inverse_ref, residual_ref, high_ref, low_ref, out_ref, coefs_v, residual_v, columns_v, sems):
    parts = pieces(out_ref.shape[0])
    columns_in = [
        [copy_of(ref.at[at], columns_v.at[kind, at], sems.at[kind, i]) for kind, ref in enumerate((high_ref, low_ref))]
        for i, at in enumerate(parts)
    ]

    @stage(live_ref)
    def _():
        coefs_v[...] = coefs_of(sums_ref, inverse_ref)

    out = []
    for copies, at in zip(columns_in, parts):
        wait_all(*copies)

        @stage(live_ref)
        def _():
            residual_v[at, :] = updated(residual_ref[at, :], columns_v[0, at, :], columns_v[1, at, :], coefs_v[...])

        out.append(copy_of(residual_v.at[at], out_ref.at[at], sems.at[2, len(out)]))
    wait_all(*out)


SPACES = {"V": pltpu.VMEM, "H": pltpu.HBM, "S": pltpu.SMEM}


def local(kernel, args, places, outs, scratch_shapes, flops, name):
    args = [pltpu.with_memory_space_constraint(a, SPACES[p]) if p != "S" else a for a, p in zip(args, places)]
    moved = sum(a.size * a.dtype.itemsize for a in args)
    made = pl.pallas_call(
        kernel,
        out_shape=[SPACES[p](shape, dtype) for p, shape, dtype in outs],
        in_specs=[pl.BlockSpec(memory_space=SPACES[p]) for p in places],
        out_specs=[pl.BlockSpec(memory_space=SPACES[p]) for p, _, _ in outs],
        scratch_shapes=scratch_shapes,
        cost_estimate=pl.CostEstimate(flops=flops, bytes_accessed=moved, transcendentals=0),
        compiler_params=pltpu.CompilerParams(vmem_limit_bytes=LIMIT),
        name=name,
    )(*args)
    return made if len(outs) > 1 else made[0]


def sum_over_rows(totals, groups, beside):
    order = order_of(groups, SUMS_SEED)
    width, size = totals.shape
    piece = round_up(width, groups) // groups
    padded = jnp.pad(totals, ((0, piece * groups - width), (0, 0))) if piece * groups != width else totals
    got = exchange(padded.reshape(groups, piece, size), order)
    made = None
    if beside is not None:
        got, made = lax.optimization_barrier((got, beside()))
    own = jnp.sum(got, axis=0)
    back = exchange(jnp.broadcast_to(own[None], (groups, piece, size)), order)
    return back.reshape(groups * piece, size)[:width], made


def on_device(groups, cores, counts, samples, targets, point_ids, block_inverse):
    rows_here, feat = samples.shape
    blocks, size = point_ids.shape
    mean = blocks * size / groups
    cap = round_up(max(1, round((mean + 4 * mean**0.5) / cores)), 8)

    order = order_of(groups, POINTS_SEED)
    rows, slots, most = local(
        functools.partial(pick_kernel, order, cores, cap),
        (point_ids, samples),
        "VH",
        [("V", (cap, feat), F32), ("V", (1, blocks * size), jnp.int32), ("S", (1,), jnp.int32)],
        [pltpu.VMEM((cap, 128), jnp.int32), pltpu.SMEM((cap, 128), jnp.int32), pltpu.SemaphoreType.DMA((2,))],
        0,
        "pick",
    )

    def general(rows):
        ids = jnp.pad(point_ids.reshape(-1), (0, cores * groups * cap - blocks * size), constant_values=-1)
        ids = lax.dynamic_slice_in_dim(ids, lax.axis_index("tgt") * groups * cap, groups * cap)
        local = ids - lax.axis_index("rows") * rows_here
        owned = (local >= 0) & (local < rows_here)
        taken = jnp.take(samples, jnp.clip(local, 0, rows_here - 1), axis=0)
        taken = jnp.where(owned[:, None], taken, 0.0)
        return jnp.sum(exchange(taken.reshape(groups, cap, feat), order), axis=0)

    rows = lax.cond(most[0] > cap * cores, general, lambda rows: rows, rows)
    got = exchange(jnp.broadcast_to(rows[None], (groups, cap, feat)), order).reshape(groups * cap, feat)
    held = [lax.ppermute(got, "tgt", [((c + shift) % cores, c) for c in range(cores)]) for shift in range(1, cores)]
    found = local(
        functools.partial(own_kernel, cores),
        (slots, got),
        "VV",
        [("V", (blocks, 2 * feat, size), BF16)],
        [],
        4 * groups * cap * feat * blocks * size,
        "own",
    )
    held, found = lax.optimization_barrier((held, found))

    width = targets.shape[1]
    columns_v = pltpu.VMEM((2, rows_here, size), BF16)
    residual_v = pltpu.VMEM((rows_here, width), F32)
    coefs_v = pltpu.VMEM((size, 2 * width), BF16)
    sems = pltpu.SemaphoreType.DMA((6, len(pieces(rows_here))))
    columns_out = [("H", (rows_here, size), BF16)] * 2
    inverse_out = ("V", (size, size), F32)
    totals_out = ("V", (width, size), F32)
    work = 6 * rows_here * size

    residual = targets
    *columns, totals, points = local(
        first_kernel,
        (counts, residual, samples, slots, found, *held),
        "SVVVV" + "V" * len(held),
        [*columns_out, totals_out, ("H", (blocks, 2, feat, size), BF16)],
        [pltpu.VMEM((blocks, 2, feat, size), BF16), columns_v, sems],
        work * (feat + width),
        "first",
    )
    for b in range(blocks - 1):

        def beside(b=b, points=points):
            args = (counts, samples, points, block_inverse)
            outs = [*columns_out, inverse_out]
            scratch = [pltpu.VMEM((2, feat, size), BF16), columns_v, sems]
            return local(functools.partial(beside_kernel, b), args, "SVHH", outs, scratch, work * feat, "beside")

        sums, (*following, inverse) = sum_over_rows(totals, groups, beside)
        residual, totals, inverse = local(
            functools.partial(middle_kernel, b),
            (counts, sums, inverse, residual, *columns, *following, block_inverse),
            "SVVHHHHHH",
            [("V", (rows_here, width), F32), totals_out, inverse_out],
            [coefs_v, residual_v, columns_v, columns_v, sems],
            2 * work * width,
            "middle",
        )
        columns = following
    sums, _ = sum_over_rows(totals, groups, None)
    return local(
        last_kernel,
        (counts, sums, inverse, residual, *columns),
        "SVVVHH",
        [("H", (rows_here, width), F32)],
        [coefs_v, residual_v, columns_v, sems],
        work * width,
        "last",
    )


def solution(mesh):
    return jax.shard_map(
        functools.partial(on_device, mesh.shape["rows"], mesh.shape["tgt"]),
        mesh=mesh,
        in_specs=(P("rows"), P("rows", None), P("rows", "tgt"), P(), P()),
        out_specs=P("rows", "tgt"),
        check_vma=False,
    )
```

```python
import functools
import random

import jax
import jax.numpy as jnp
from jax import lax
from jax.experimental import pallas as pl
from jax.experimental.pallas import tpu as pltpu
from jax.sharding import PartitionSpec as P

F32 = jnp.float32
BF16 = jnp.bfloat16
ROWS_STEP = 512
HALF_STEP = 1024
LIMIT = 24 * 2**20
SLOW_SEED = 12
FAST_SEED = 16
SUMS_SEED = 152


def order_of(groups, seed):
    order = list(range(groups))
    random.Random(seed).shuffle(order)
    return order


def exchange(x, *orders):
    return lax.all_to_all(x, "rows", 0, 0, axis_index_groups=list(orders))


def gather(x, *orders):
    count = len(orders[0])
    return exchange(jnp.broadcast_to(x[None], (count, *x.shape)), *orders).reshape(count * x.shape[0], *x.shape[1:])


def round_up(value, unit):
    return -(-value // unit) * unit


def split(x):
    high = x.astype(BF16)
    return high, (x - high.astype(F32)).astype(BF16)


def dot(a, b, dims):
    return lax.dot_general(a, b, (dims, ((), ())), preferred_element_type=F32)


def dot3(a, b, dims):
    return dot(a[0], b[0], dims) + dot(a[0], b[1], dims) + dot(a[1], b[0], dims)


def pick_kernel(order, cores, cap, ids_ref, samples_ref, rows_ref, slots_ref, most_ref, index_v, index_s, sems):
    rows_here, groups = samples_ref.shape[0], len(order)
    me, core = lax.axis_index("rows"), lax.axis_index("tgt")
    ids = jnp.concatenate([ids_ref[b : b + 1, :] for b in range(ids_ref.shape[0])], axis=1)
    count = ids.shape[1]
    owner = lax.div(ids, jnp.int32(rows_here))
    local = ids - owner * rows_here
    mine = lax.broadcasted_iota(jnp.int32, (groups, count), 0) == owner
    seen = mine.astype(jnp.int32)
    lane = lax.broadcasted_iota(jnp.int32, (groups, count), 1)
    step = 1
    while step < count:
        seen = seen + jnp.where(lane >= step, pltpu.roll(seen, step, 1), 0)
        step *= 2
    most = jnp.max(seen)
    rank = jnp.sum(jnp.where(mine, seen, 0), axis=0, keepdims=True) - 1
    half = lax.div(rank, jnp.int32(cap))
    turn = jnp.zeros_like(owner)
    for index, device in enumerate(order):
        turn = jnp.where(owner == device, index, turn)
    packed = (half * groups + turn) * cap + (rank - half * cap)
    place = lax.broadcasted_iota(jnp.int32, (1, count), 1)
    slots_ref[...] = jnp.where(most > cap * cores, place, packed)
    most_ref[0] = most

    wanted = lax.broadcasted_iota(jnp.int32, (cap, count), 0) + core * cap
    chosen = jnp.where((wanted == rank) & (owner == me), local, 0)
    index_v[...] = jnp.broadcast_to(jnp.sum(chosen, axis=1, keepdims=True), index_v.shape)
    move = pltpu.make_async_copy(index_v, index_s, sems.at[0])
    move.start()
    move.wait()

    @pl.loop(0, cap)
    def _(k):
        pltpu.make_async_copy(samples_ref.at[pl.ds(index_s[k, 0], 1)], rows_ref.at[pl.ds(k, 1)], sems.at[1]).start()

    pltpu.make_async_copy(samples_ref.at[pl.ds(0, cap)], rows_ref, sems.at[1]).wait()


def pieces(rows, step=ROWS_STEP):
    step = min(step, rows)
    return [pl.ds(start, step) for start in range(0, rows, step)]


def copy_of(source, target, sem):
    copy = pltpu.make_async_copy(source, target, sem)
    copy.start()
    return copy


def stage(live_ref):
    return pl.when(live_ref[0] >= 0)


def wait_all(*copies):
    for copy in copies:
        copy.wait()


def found_in(ref, slots, shift, cores):
    depth = ref.shape[0]
    base = lax.rem(lax.axis_index("tgt") + shift, cores) * depth
    slot = lax.broadcasted_iota(jnp.int32, (depth, slots.shape[1]), 0) + base
    taken = jnp.where(slot == slots, 1.0, 0.0).astype(BF16)
    return dot(jnp.concatenate(split(ref[...]), axis=1), taken, ((0,), (0,)))


def own_kernel(cores, slots_ref, held_ref, found_ref):
    blocks, _, size = found_ref.shape
    for b in range(blocks):
        found_ref[b] = found_in(held_ref, slots_ref[:, b * size : (b + 1) * size], 0, cores).astype(BF16)


def make_columns(live_ref, samples_ref, points, columns_v, high_ref, low_ref, sems):
    rows, feat = samples_ref.shape
    scale = 0.5 / feat**0.5
    copies = []
    for index, half in enumerate(pieces(rows, HALF_STEP)):
        for at in [pl.ds(half.start + part.start, part.size) for part in pieces(half.size)]:
            base = dot3(split(samples_ref[at, :]), points, ((1,), (0,))) * scale + 1.0
            slot = lax.broadcasted_iota(jnp.int32, (at.size, 1), 0) + at.start
            columns_v[0, at, :], columns_v[1, at, :] = split(jnp.where(slot < live_ref[0], base * base * base, 0.0))
        for kind, ref in enumerate((high_ref, low_ref)):
            copies.append(copy_of(columns_v.at[kind, half], ref.at[half], sems.at[kind, index]))
    return copies


def sum_of(residual, high, low):
    width = residual.shape[1]
    residual = split(residual)
    both = dot(jnp.concatenate(residual, axis=1), high, ((0,), (0,)))
    return both[:width] + both[width:] + dot(residual[0], low, ((0,), (0,)))


def first_kernel(live_ref, residual_ref, samples_ref, slots_ref, found_ref, *refs):
    *held, high_ref, low_ref, total_ref, points_ref, points_v, columns_v, sems = refs
    blocks, _, size = found_ref.shape
    feat = samples_ref.shape[1]
    for b in range(blocks):
        found = found_ref[b].astype(F32)
        for shift, ref in enumerate(held):
            found = found + found_in(ref, slots_ref[:, b * size : (b + 1) * size], shift + 1, len(held) + 1)
        points_v[b, 0], points_v[b, 1] = found[:feat].astype(BF16), found[feat:].astype(BF16)
    copies = make_columns(live_ref, samples_ref, (points_v[0, 0], points_v[0, 1]), columns_v, high_ref, low_ref, sems)
    copies.append(copy_of(points_v, points_ref, sems.at[3, 0]))

    @stage(live_ref)
    def _():
        for index, at in enumerate(pieces(samples_ref.shape[0])):
            term = sum_of(residual_ref[at, :], columns_v[0, at, :], columns_v[1, at, :])
            total_ref[...] = term if index == 0 else total_ref[...] + term

    wait_all(*copies)


def beside_kernel(block, live_ref, samples_ref, points_ref, inverse_ref, high_ref, low_ref, inverse_v, points_v, columns_v, sems):
    points_in = copy_of(points_ref.at[block + 1], points_v, sems.at[3, 0])
    inverse_in = copy_of(inverse_ref.at[block], inverse_v, sems.at[2, 0])
    points_in.wait()
    copies = make_columns(live_ref, samples_ref, (points_v[0], points_v[1]), columns_v, high_ref, low_ref, sems)
    wait_all(inverse_in, *copies)


def coefs_of(sums_ref, inverse_ref):
    return jnp.concatenate(split(dot3(split(sums_ref[...]), split(inverse_ref[...]), ((1,), (1,))).T), axis=1)


def updated(residual, high, low, coefs):
    width = residual.shape[1]
    both = dot(high, coefs, ((1,), (0,)))
    return residual - (both[:, :width] + both[:, width:] + dot(low, coefs[:, :width], ((1,), (0,))))


def middle_kernel(block, live_ref, sums_ref, inverse_ref, residual_ref, high_ref, low_ref, next_high, next_low, inverses, *refs):
    out_ref, total_ref, inverse_v, coefs_v, residual_v, columns_v, next_v, sems = refs
    parts = pieces(out_ref.shape[0])
    first_in = [
        [
            copy_of(residual_ref.at[at], residual_v.at[at], sems.at[0, i]),
            copy_of(high_ref.at[at], columns_v.at[0, at], sems.at[1, i]),
            copy_of(low_ref.at[at], columns_v.at[1, at], sems.at[2, i]),
        ]
        for i, at in enumerate(parts)
    ]
    next_in = [
        [copy_of(ref.at[at], next_v.at[kind, at], sems.at[3 + kind, i]) for kind, ref in enumerate((next_high, next_low))]
        for i, at in enumerate(parts)
    ]
    inverse_in = copy_of(inverses.at[block + 1], inverse_v, sems.at[5, 0])

    @stage(live_ref)
    def _():
        coefs_v[...] = coefs_of(sums_ref, inverse_ref)

    for copies, at in zip(first_in, parts):
        wait_all(*copies)

        @stage(live_ref)
        def _():
            out_ref[at, :] = updated(residual_v[at, :], columns_v[0, at, :], columns_v[1, at, :], coefs_v[...])

    for copies, at in zip(next_in, parts):
        wait_all(*copies)

        @stage(live_ref)
        def _():
            term = sum_of(out_ref[at, :], next_v[0, at, :], next_v[1, at, :])
            total_ref[...] = term if at.start == 0 else total_ref[...] + term

    inverse_in.wait()


def last_kernel(live_ref, sums_ref, inverse_ref, residual_ref, high_ref, low_ref, out_ref, coefs_v, residual_v, columns_v, sems):
    parts = pieces(out_ref.shape[0])
    columns_in = [
        [copy_of(ref.at[at], columns_v.at[kind, at], sems.at[kind, i]) for kind, ref in enumerate((high_ref, low_ref))]
        for i, at in enumerate(parts)
    ]

    @stage(live_ref)
    def _():
        coefs_v[...] = coefs_of(sums_ref, inverse_ref)

    out = []
    for copies, at in zip(columns_in, parts):
        wait_all(*copies)

        @stage(live_ref)
        def _():
            residual_v[at, :] = updated(residual_ref[at, :], columns_v[0, at, :], columns_v[1, at, :], coefs_v[...])

        out.append(copy_of(residual_v.at[at], out_ref.at[at], sems.at[2, len(out)]))
    wait_all(*out)


SPACES = {"V": pltpu.VMEM, "H": pltpu.HBM, "S": pltpu.SMEM}


def local(kernel, args, places, outs, scratch_shapes, flops, name):
    args = [pltpu.with_memory_space_constraint(a, SPACES[p]) if p != "S" else a for a, p in zip(args, places)]
    moved = sum(a.size * a.dtype.itemsize for a in args)
    made = pl.pallas_call(
        kernel,
        out_shape=[SPACES[p](shape, dtype) for p, shape, dtype in outs],
        in_specs=[pl.BlockSpec(memory_space=SPACES[p]) for p in places],
        out_specs=[pl.BlockSpec(memory_space=SPACES[p]) for p, _, _ in outs],
        scratch_shapes=scratch_shapes,
        cost_estimate=pl.CostEstimate(flops=flops, bytes_accessed=moved, transcendentals=0),
        compiler_params=pltpu.CompilerParams(vmem_limit_bytes=LIMIT),
        name=name,
    )(*args)
    return made if len(outs) > 1 else made[0]


def sum_over_rows(totals, groups, beside):
    order = order_of(groups, SUMS_SEED)
    width, size = totals.shape
    piece = round_up(width, groups) // groups
    padded = jnp.pad(totals, ((0, piece * groups - width), (0, 0))) if piece * groups != width else totals
    got = exchange(padded.reshape(groups, piece, size), order)
    made = None
    if beside is not None:
        got, made = lax.optimization_barrier((got, beside()))
    own = jnp.sum(got, axis=0)
    return gather(own, order)[:width], made


def on_device(groups, cores, counts, samples, targets, point_ids, block_inverse):
    rows_here, feat = samples.shape
    blocks, size = point_ids.shape
    mean = blocks * size / groups
    cap = round_up(max(1, round((mean + 4 * mean**0.5) / cores)), 8)

    fast = max(d for d in range(1, groups + 1) if groups % d == 0 and d * d <= groups)
    slow = groups // fast
    slow_order, fast_order = order_of(slow, SLOW_SEED), order_of(fast, FAST_SEED)
    order = [s * fast + f for f in fast_order for s in slow_order]
    rows, slots, most = local(
        functools.partial(pick_kernel, order, cores, cap),
        (point_ids, samples),
        "VH",
        [("V", (cap, feat), F32), ("V", (1, blocks * size), jnp.int32), ("S", (1,), jnp.int32)],
        [pltpu.VMEM((cap, 128), jnp.int32), pltpu.SMEM((cap, 128), jnp.int32), pltpu.SemaphoreType.DMA((2,))],
        0,
        "pick",
    )

    def general(rows):
        ids = jnp.pad(point_ids.reshape(-1), (0, cores * groups * cap - blocks * size), constant_values=-1)
        ids = lax.dynamic_slice_in_dim(ids, lax.axis_index("tgt") * groups * cap, groups * cap)
        local = ids - lax.axis_index("rows") * rows_here
        owned = (local >= 0) & (local < rows_here)
        taken = jnp.take(samples, jnp.clip(local, 0, rows_here - 1), axis=0)
        taken = jnp.where(owned[:, None], taken, 0.0)
        return jnp.sum(exchange(taken.reshape(groups, cap, feat), order), axis=0)

    rows = lax.cond(most[0] > cap * cores, general, lambda rows: rows, rows)
    got = gather(rows, *[[s * fast + f for s in slow_order] for f in range(fast)])
    got = gather(got, *[[s * fast + f for f in fast_order] for s in range(slow)])
    held = [lax.ppermute(got, "tgt", [((c + shift) % cores, c) for c in range(cores)]) for shift in range(1, cores)]
    found = local(
        functools.partial(own_kernel, cores),
        (slots, got),
        "VV",
        [("V", (blocks, 2 * feat, size), BF16)],
        [],
        4 * groups * cap * feat * blocks * size,
        "own",
    )
    held, found = lax.optimization_barrier((held, found))

    width = targets.shape[1]
    columns_v = pltpu.VMEM((2, rows_here, size), BF16)
    residual_v = pltpu.VMEM((rows_here, width), F32)
    coefs_v = pltpu.VMEM((size, 2 * width), BF16)
    sems = pltpu.SemaphoreType.DMA((6, len(pieces(rows_here))))
    columns_out = [("H", (rows_here, size), BF16)] * 2
    inverse_out = ("V", (size, size), F32)
    totals_out = ("V", (width, size), F32)
    work = 6 * rows_here * size

    residual = targets
    *columns, totals, points = local(
        first_kernel,
        (counts, residual, samples, slots, found, *held),
        "SVVVV" + "V" * len(held),
        [*columns_out, totals_out, ("H", (blocks, 2, feat, size), BF16)],
        [pltpu.VMEM((blocks, 2, feat, size), BF16), columns_v, sems],
        work * (feat + width),
        "first",
    )
    for b in range(blocks - 1):

        def beside(b=b, points=points):
            args = (counts, samples, points, block_inverse)
            outs = [*columns_out, inverse_out]
            scratch = [pltpu.VMEM((2, feat, size), BF16), columns_v, sems]
            return local(functools.partial(beside_kernel, b), args, "SVHH", outs, scratch, work * feat, "beside")

        sums, (*following, inverse) = sum_over_rows(totals, groups, beside)
        residual, totals, inverse = local(
            functools.partial(middle_kernel, b),
            (counts, sums, inverse, residual, *columns, *following, block_inverse),
            "SVVHHHHHH",
            [("V", (rows_here, width), F32), totals_out, inverse_out],
            [coefs_v, residual_v, columns_v, columns_v, sems],
            2 * work * width,
            "middle",
        )
        columns = following
    sums, _ = sum_over_rows(totals, groups, None)
    return local(
        last_kernel,
        (counts, sums, inverse, residual, *columns),
        "SVVVHH",
        [("H", (rows_here, width), F32)],
        [coefs_v, residual_v, columns_v, sems],
        work * width,
        "last",
    )


def solution(mesh):
    return jax.shard_map(
        functools.partial(on_device, mesh.shape["rows"], mesh.shape["tgt"]),
        mesh=mesh,
        in_specs=(P("rows"), P("rows", None), P("rows", "tgt"), P(), P()),
        out_specs=P("rows", "tgt"),
        check_vma=False,
    )
```

```python
import functools
import random

import jax
import jax.numpy as jnp
from jax import lax
from jax.experimental import pallas as pl
from jax.experimental.pallas import tpu as pltpu
from jax.sharding import PartitionSpec as P

F32 = jnp.float32
BF16 = jnp.bfloat16
ROWS_STEP = 512
HALF_STEP = 1024
LIMIT = 24 * 2**20
POINTS_SEED = 14
SUMS_SEED = 152


def order_of(groups, seed):
    order = list(range(groups))
    random.Random(seed).shuffle(order)
    return order


def exchange(x, order):
    return lax.all_to_all(x, "rows", 0, 0, axis_index_groups=[order])


def round_up(value, unit):
    return -(-value // unit) * unit


def split(x):
    high = x.astype(BF16)
    return high, (x - high.astype(F32)).astype(BF16)


def dot(a, b, dims):
    return lax.dot_general(a, b, (dims, ((), ())), preferred_element_type=F32)


def dot3(a, b, dims):
    return dot(a[0], b[0], dims) + dot(a[0], b[1], dims) + dot(a[1], b[0], dims)


def pick_kernel(order, cores, cap, ids_ref, samples_ref, rows_ref, slots_ref, most_ref, index_v, index_s, sems):
    rows_here, groups = samples_ref.shape[0], len(order)
    me, core = lax.axis_index("rows"), lax.axis_index("tgt")
    ids = jnp.concatenate([ids_ref[b : b + 1, :] for b in range(ids_ref.shape[0])], axis=1)
    count = ids.shape[1]
    owner = lax.div(ids, jnp.int32(rows_here))
    local = ids - owner * rows_here
    mine = lax.broadcasted_iota(jnp.int32, (groups, count), 0) == owner
    seen = mine.astype(jnp.int32)
    lane = lax.broadcasted_iota(jnp.int32, (groups, count), 1)
    step = 1
    while step < count:
        seen = seen + jnp.where(lane >= step, pltpu.roll(seen, step, 1), 0)
        step *= 2
    most = jnp.max(seen)
    rank = jnp.sum(jnp.where(mine, seen, 0), axis=0, keepdims=True) - 1
    half = lax.div(rank, jnp.int32(cap))
    turn = jnp.zeros_like(owner)
    for index, device in enumerate(order):
        turn = jnp.where(owner == device, index, turn)
    packed = (half * groups + turn) * cap + (rank - half * cap)
    place = lax.broadcasted_iota(jnp.int32, (1, count), 1)
    slots_ref[...] = jnp.where(most > cap * cores, place, packed)
    most_ref[0] = most

    wanted = lax.broadcasted_iota(jnp.int32, (cap, count), 0) + core * cap
    chosen = jnp.where((wanted == rank) & (owner == me), local, 0)
    index_v[...] = jnp.broadcast_to(jnp.sum(chosen, axis=1, keepdims=True), index_v.shape)
    move = pltpu.make_async_copy(index_v, index_s, sems.at[0])
    move.start()
    move.wait()

    @pl.loop(0, cap)
    def _(k):
        pltpu.make_async_copy(samples_ref.at[pl.ds(index_s[k, 0], 1)], rows_ref.at[pl.ds(k, 1)], sems.at[1]).start()

    pltpu.make_async_copy(samples_ref.at[pl.ds(0, cap)], rows_ref, sems.at[1]).wait()


def pieces(rows, step=ROWS_STEP):
    step = min(step, rows)
    return [pl.ds(start, step) for start in range(0, rows, step)]


def copy_of(source, target, sem):
    copy = pltpu.make_async_copy(source, target, sem)
    copy.start()
    return copy


def stage(live_ref):
    return pl.when(live_ref[0] >= 0)


def wait_all(*copies):
    for copy in copies:
        copy.wait()


def found_in(ref, slots, shift, cores):
    depth = ref.shape[0]
    base = lax.rem(lax.axis_index("tgt") + shift, cores) * depth
    slot = lax.broadcasted_iota(jnp.int32, (depth, slots.shape[1]), 0) + base
    taken = jnp.where(slot == slots, 1.0, 0.0).astype(BF16)
    return dot(jnp.concatenate(split(ref[...]), axis=1), taken, ((0,), (0,)))


def own_kernel(cores, slots_ref, held_ref, found_ref):
    blocks, _, size = found_ref.shape
    for b in range(blocks):
        found_ref[b] = found_in(held_ref, slots_ref[:, b * size : (b + 1) * size], 0, cores).astype(BF16)


def make_columns(live_ref, samples_ref, points, columns_v, high_ref, low_ref, sems):
    rows, feat = samples_ref.shape
    scale = 0.5 / feat**0.5
    copies = []
    for index, half in enumerate(pieces(rows, HALF_STEP)):
        for at in [pl.ds(half.start + part.start, part.size) for part in pieces(half.size)]:
            base = dot3(split(samples_ref[at, :]), points, ((1,), (0,))) * scale + 1.0
            slot = lax.broadcasted_iota(jnp.int32, (at.size, 1), 0) + at.start
            columns_v[0, at, :], columns_v[1, at, :] = split(jnp.where(slot < live_ref[0], base * base * base, 0.0))
        for kind, ref in enumerate((high_ref, low_ref)):
            copies.append(copy_of(columns_v.at[kind, half], ref.at[half], sems.at[kind, index]))
    return copies


def sum_of(residual, high, low):
    width = residual.shape[1]
    residual = split(residual)
    both = dot(jnp.concatenate(residual, axis=1), high, ((0,), (0,)))
    return both[:width] + both[width:] + dot(residual[0], low, ((0,), (0,)))


def first_kernel(live_ref, residual_ref, samples_ref, slots_ref, found_ref, *refs):
    *held, high_ref, low_ref, total_ref, points_ref, points_v, columns_v, sems = refs
    blocks, _, size = found_ref.shape
    feat = samples_ref.shape[1]
    for b in range(blocks):
        found = found_ref[b].astype(F32)
        for shift, ref in enumerate(held):
            found = found + found_in(ref, slots_ref[:, b * size : (b + 1) * size], shift + 1, len(held) + 1)
        points_v[b, 0], points_v[b, 1] = found[:feat].astype(BF16), found[feat:].astype(BF16)
    points_out = copy_of(points_v, points_ref, sems.at[3, 0])
    copies = make_columns(live_ref, samples_ref, (points_v[0, 0], points_v[0, 1]), columns_v, high_ref, low_ref, sems)
    for index, at in enumerate(pieces(samples_ref.shape[0])):
        term = sum_of(residual_ref[at, :], columns_v[0, at, :], columns_v[1, at, :])
        total_ref[...] = term if index == 0 else total_ref[...] + term
    wait_all(points_out, *copies)


def beside_kernel(block, live_ref, samples_ref, points_ref, inverse_ref, high_ref, low_ref, inverse_v, points_v, columns_v, sems):
    points_in = copy_of(points_ref.at[block + 1], points_v, sems.at[3, 0])
    inverse_in = copy_of(inverse_ref.at[block], inverse_v, sems.at[2, 0])
    points_in.wait()
    copies = make_columns(live_ref, samples_ref, (points_v[0], points_v[1]), columns_v, high_ref, low_ref, sems)
    wait_all(inverse_in, *copies)


def coefs_of(sums_ref, inverse_ref):
    return jnp.concatenate(split(dot3(split(sums_ref[...]), split(inverse_ref[...]), ((1,), (1,))).T), axis=1)


def updated(residual, high, low, coefs):
    width = residual.shape[1]
    both = dot(high, coefs, ((1,), (0,)))
    return residual - (both[:, :width] + both[:, width:] + dot(low, coefs[:, :width], ((1,), (0,))))


def middle_kernel(block, live_ref, sums_ref, inverse_ref, residual_ref, high_ref, low_ref, next_high, next_low, inverses, *refs):
    out_ref, total_ref, inverse_v, coefs_v, residual_v, columns_v, next_v, sems = refs
    parts = pieces(out_ref.shape[0])
    first_in = [
        [
            copy_of(residual_ref.at[at], residual_v.at[at], sems.at[0, i]),
            copy_of(high_ref.at[at], columns_v.at[0, at], sems.at[1, i]),
            copy_of(low_ref.at[at], columns_v.at[1, at], sems.at[2, i]),
        ]
        for i, at in enumerate(parts)
    ]
    next_in = [
        [copy_of(ref.at[at], next_v.at[kind, at], sems.at[3 + kind, i]) for kind, ref in enumerate((next_high, next_low))]
        for i, at in enumerate(parts)
    ]
    inverse_in = copy_of(inverses.at[block + 1], inverse_v, sems.at[5, 0])

    @stage(live_ref)
    def _():
        coefs_v[...] = coefs_of(sums_ref, inverse_ref)

    for copies, at in zip(first_in, parts):
        wait_all(*copies)

        @stage(live_ref)
        def _():
            out_ref[at, :] = updated(residual_v[at, :], columns_v[0, at, :], columns_v[1, at, :], coefs_v[...])

    for copies, at in zip(next_in, parts):
        wait_all(*copies)

        @stage(live_ref)
        def _():
            term = sum_of(out_ref[at, :], next_v[0, at, :], next_v[1, at, :])
            total_ref[...] = term if at.start == 0 else total_ref[...] + term

    inverse_in.wait()


def last_kernel(live_ref, sums_ref, inverse_ref, residual_ref, high_ref, low_ref, out_ref, coefs_v, residual_v, columns_v, sems):
    parts = pieces(out_ref.shape[0])
    columns_in = [
        [copy_of(ref.at[at], columns_v.at[kind, at], sems.at[kind, i]) for kind, ref in enumerate((high_ref, low_ref))]
        for i, at in enumerate(parts)
    ]

    @stage(live_ref)
    def _():
        coefs_v[...] = coefs_of(sums_ref, inverse_ref)

    out = []
    for copies, at in zip(columns_in, parts):
        wait_all(*copies)

        @stage(live_ref)
        def _():
            residual_v[at, :] = updated(residual_ref[at, :], columns_v[0, at, :], columns_v[1, at, :], coefs_v[...])

        out.append(copy_of(residual_v.at[at], out_ref.at[at], sems.at[2, len(out)]))
    wait_all(*out)


SPACES = {"V": pltpu.VMEM, "H": pltpu.HBM, "S": pltpu.SMEM}


def local(kernel, args, places, outs, scratch_shapes, flops, name):
    args = [pltpu.with_memory_space_constraint(a, SPACES[p]) if p != "S" else a for a, p in zip(args, places)]
    moved = sum(a.size * a.dtype.itemsize for a in args)
    made = pl.pallas_call(
        kernel,
        out_shape=[SPACES[p](shape, dtype) for p, shape, dtype in outs],
        in_specs=[pl.BlockSpec(memory_space=SPACES[p]) for p in places],
        out_specs=[pl.BlockSpec(memory_space=SPACES[p]) for p, _, _ in outs],
        scratch_shapes=scratch_shapes,
        cost_estimate=pl.CostEstimate(flops=flops, bytes_accessed=moved, transcendentals=0),
        compiler_params=pltpu.CompilerParams(vmem_limit_bytes=LIMIT),
        name=name,
    )(*args)
    return made if len(outs) > 1 else made[0]


def sum_over_rows(totals, groups, beside):
    order = order_of(groups, SUMS_SEED)
    width, size = totals.shape
    piece = round_up(width, groups) // groups
    padded = jnp.pad(totals, ((0, piece * groups - width), (0, 0))) if piece * groups != width else totals
    got = exchange(padded.reshape(groups, piece, size), order)
    made = None
    if beside is not None:
        got, made = lax.optimization_barrier((got, beside()))
    own = jnp.sum(got, axis=0)
    back = exchange(jnp.broadcast_to(own[None], (groups, piece, size)), order)
    return back.reshape(groups * piece, size)[:width], made


def on_device(groups, cores, counts, samples, targets, point_ids, block_inverse):
    rows_here, feat = samples.shape
    blocks, size = point_ids.shape
    mean = blocks * size / groups
    cap = round_up(max(1, round((mean + 4 * mean**0.5) / cores)), 8)

    order = order_of(groups, POINTS_SEED)
    rows, slots, most = local(
        functools.partial(pick_kernel, order, cores, cap),
        (point_ids, samples),
        "VH",
        [("V", (cap, feat), F32), ("V", (1, blocks * size), jnp.int32), ("S", (1,), jnp.int32)],
        [pltpu.VMEM((cap, 128), jnp.int32), pltpu.SMEM((cap, 128), jnp.int32), pltpu.SemaphoreType.DMA((2,))],
        0,
        "pick",
    )

    def general(rows):
        ids = jnp.pad(point_ids.reshape(-1), (0, cores * groups * cap - blocks * size), constant_values=-1)
        ids = lax.dynamic_slice_in_dim(ids, lax.axis_index("tgt") * groups * cap, groups * cap)
        local = ids - lax.axis_index("rows") * rows_here
        owned = (local >= 0) & (local < rows_here)
        taken = jnp.take(samples, jnp.clip(local, 0, rows_here - 1), axis=0)
        taken = jnp.where(owned[:, None], taken, 0.0)
        return jnp.sum(exchange(taken.reshape(groups, cap, feat), order), axis=0)

    rows = lax.cond(most[0] > cap * cores, general, lambda rows: rows, rows)
    got = exchange(jnp.broadcast_to(rows[None], (groups, cap, feat)), order).reshape(groups * cap, feat)
    held = [lax.ppermute(got, "tgt", [((c + shift) % cores, c) for c in range(cores)]) for shift in range(1, cores)]
    found = local(
        functools.partial(own_kernel, cores),
        (slots, got),
        "VV",
        [("V", (blocks, 2 * feat, size), BF16)],
        [],
        4 * groups * cap * feat * blocks * size,
        "own",
    )
    held, found = lax.optimization_barrier((held, found))

    width = targets.shape[1]
    columns_v = pltpu.VMEM((2, rows_here, size), BF16)
    residual_v = pltpu.VMEM((rows_here, width), F32)
    coefs_v = pltpu.VMEM((size, 2 * width), BF16)
    sems = pltpu.SemaphoreType.DMA((6, len(pieces(rows_here))))
    columns_out = [("H", (rows_here, size), BF16)] * 2
    inverse_out = ("V", (size, size), F32)
    totals_out = ("V", (width, size), F32)
    work = 6 * rows_here * size

    residual = targets
    *columns, totals, points = local(
        first_kernel,
        (counts, residual, samples, slots, found, *held),
        "SVVVV" + "V" * len(held),
        [*columns_out, totals_out, ("H", (blocks, 2, feat, size), BF16)],
        [pltpu.VMEM((blocks, 2, feat, size), BF16), columns_v, sems],
        work * (feat + width),
        "first",
    )
    for b in range(blocks - 1):

        def beside(b=b, points=points):
            args = (counts, samples, points, block_inverse)
            outs = [*columns_out, inverse_out]
            scratch = [pltpu.VMEM((2, feat, size), BF16), columns_v, sems]
            return local(functools.partial(beside_kernel, b), args, "SVHH", outs, scratch, work * feat, "beside")

        sums, (*following, inverse) = sum_over_rows(totals, groups, beside)
        residual, totals, inverse = local(
            functools.partial(middle_kernel, b),
            (counts, sums, inverse, residual, *columns, *following, block_inverse),
            "SVVHHHHHH",
            [("V", (rows_here, width), F32), totals_out, inverse_out],
            [coefs_v, residual_v, columns_v, columns_v, sems],
            2 * work * width,
            "middle",
        )
        columns = following
    sums, _ = sum_over_rows(totals, groups, None)
    return local(
        last_kernel,
        (counts, sums, inverse, residual, *columns),
        "SVVVHH",
        [("H", (rows_here, width), F32)],
        [coefs_v, residual_v, columns_v, sems],
        work * width,
        "last",
    )


def solution(mesh):
    return jax.shard_map(
        functools.partial(on_device, mesh.shape["rows"], mesh.shape["tgt"]),
        mesh=mesh,
        in_specs=(P("rows"), P("rows", None), P("rows", "tgt"), P(), P()),
        out_specs=P("rows", "tgt"),
        check_vma=False,
    )
```

```python
import functools
import random

import jax
import jax.numpy as jnp
from jax import lax
from jax.experimental import pallas as pl
from jax.experimental.pallas import tpu as pltpu
from jax.sharding import PartitionSpec as P

F32 = jnp.float32
BF16 = jnp.bfloat16
ROWS_STEP = 512
HALF_STEP = 1024
LIMIT = 24 * 2**20
POINTS_SEED = 14
SUMS_SEED = 152


def order_of(groups, seed):
    order = list(range(groups))
    random.Random(seed).shuffle(order)
    return order


def exchange(x, order):
    return lax.all_to_all(x, "rows", 0, 0, axis_index_groups=[order])


def round_up(value, unit):
    return -(-value // unit) * unit


def split(x):
    high = x.astype(BF16)
    return high, (x - high.astype(F32)).astype(BF16)


def dot(a, b, dims):
    return lax.dot_general(a, b, (dims, ((), ())), preferred_element_type=F32)


def dot3(a, b, dims):
    return dot(a[0], b[0], dims) + dot(a[0], b[1], dims) + dot(a[1], b[0], dims)


def pieces(rows, step=ROWS_STEP):
    step = min(step, rows)
    return [pl.ds(start, step) for start in range(0, rows, step)]


def copy_of(source, target, sem):
    copy = pltpu.make_async_copy(source, target, sem)
    copy.start()
    return copy


def stage(live_ref):
    return pl.when(live_ref[0] >= 0)


def wait_all(*copies):
    for copy in copies:
        copy.wait()


def pick_kernel(order, cores, cap, live_ref, ids_ref, samples_ref, rows_ref, slots_ref, most_ref, parts_ref, samples_v, chosen_v, sems):
    (rows_here, feat), groups = samples_ref.shape, len(order)
    parts = pieces(rows_here, HALF_STEP)
    copies = [copy_of(samples_ref.at[at], samples_v.at[at], sems.at[i]) for i, at in enumerate(parts)]
    me, core = lax.axis_index("rows"), lax.axis_index("tgt")

    @stage(live_ref)
    def _():
        ids = jnp.concatenate([ids_ref[b : b + 1, :] for b in range(ids_ref.shape[0])], axis=1)
        count = ids.shape[1]
        owner = lax.div(ids, jnp.int32(rows_here))
        local = ids - owner * rows_here
        mine = lax.broadcasted_iota(jnp.int32, (groups, count), 0) == owner
        seen = mine.astype(jnp.int32)
        lane = lax.broadcasted_iota(jnp.int32, (groups, count), 1)
        step = 1
        while step < count:
            seen = seen + jnp.where(lane >= step, pltpu.roll(seen, step, 1), 0)
            step *= 2
        most = jnp.max(seen)
        rank = jnp.sum(jnp.where(mine, seen, 0), axis=0, keepdims=True) - 1
        half = lax.div(rank, jnp.int32(cap))
        turn = jnp.zeros_like(owner)
        for index, device in enumerate(order):
            turn = jnp.where(owner == device, index, turn)
        packed = (half * groups + turn) * cap + (rank - half * cap)
        place = lax.broadcasted_iota(jnp.int32, (1, count), 1)
        slots_ref[...] = jnp.where(most > cap * cores, place, packed)
        most_ref[0] = most

        wanted = lax.broadcasted_iota(jnp.int32, (cap, count), 0) + core * cap
        sent = jnp.sum(jnp.where((wanted == rank) & (owner == me), local, 0), axis=1, keepdims=True)
        chosen_v[...] = jnp.where(lax.broadcasted_iota(jnp.int32, (cap, rows_here), 1) == sent, 1.0, 0.0).astype(BF16)

    for copy, at in zip(copies, parts):
        copy.wait()

        @stage(live_ref)
        def _():
            parts_ref[at, :] = jnp.concatenate(split(samples_v[at, :]), axis=1)
            both = dot(chosen_v[:, at], parts_ref[at, :], ((1,), (0,)))
            found = both[:, :feat] + both[:, feat:]
            rows_ref[...] = found if at.start == 0 else rows_ref[...] + found


def found_in(ref, slots, shift, cores):
    depth = ref.shape[0]
    base = lax.rem(lax.axis_index("tgt") + shift, cores) * depth
    slot = lax.broadcasted_iota(jnp.int32, (depth, slots.shape[1]), 0) + base
    taken = jnp.where(slot == slots, 1.0, 0.0).astype(BF16)
    return dot(jnp.concatenate(split(ref[...]), axis=1), taken, ((0,), (0,)))


def own_kernel(cores, slots_ref, held_ref, found_ref):
    blocks, _, size = found_ref.shape
    for b in range(blocks):
        found_ref[b] = found_in(held_ref, slots_ref[:, b * size : (b + 1) * size], 0, cores).astype(BF16)


def make_columns(live_ref, samples_ref, points, columns_v, high_ref, low_ref, sems):
    rows, feat = samples_ref.shape[0], samples_ref.shape[1] // 2
    scale = 0.5 / feat**0.5
    copies = []
    for index, half in enumerate(pieces(rows, HALF_STEP)):
        for at in [pl.ds(half.start + part.start, part.size) for part in pieces(half.size)]:
            base = dot3((samples_ref[at, :feat], samples_ref[at, feat:]), points, ((1,), (0,))) * scale + 1.0
            slot = lax.broadcasted_iota(jnp.int32, (at.size, 1), 0) + at.start
            columns_v[0, at, :], columns_v[1, at, :] = split(jnp.where(slot < live_ref[0], base * base * base, 0.0))
        for kind, ref in enumerate((high_ref, low_ref)):
            copies.append(copy_of(columns_v.at[kind, half], ref.at[half], sems.at[kind, index]))
    return copies


def sum_of(residual, high, low):
    width = residual.shape[1]
    residual = split(residual)
    both = dot(jnp.concatenate(residual, axis=1), high, ((0,), (0,)))
    return both[:width] + both[width:] + dot(residual[0], low, ((0,), (0,)))


def first_kernel(live_ref, residual_ref, samples_ref, slots_ref, found_ref, *refs):
    *held, high_ref, low_ref, total_ref, points_ref, points_v, columns_v, sems = refs
    blocks, _, size = found_ref.shape
    feat = samples_ref.shape[1] // 2
    for b in range(blocks):
        found = found_ref[b].astype(F32)
        for shift, ref in enumerate(held):
            found = found + found_in(ref, slots_ref[:, b * size : (b + 1) * size], shift + 1, len(held) + 1)
        points_v[b, 0], points_v[b, 1] = found[:feat].astype(BF16), found[feat:].astype(BF16)
    points_out = copy_of(points_v, points_ref, sems.at[3, 0])
    copies = make_columns(live_ref, samples_ref, (points_v[0, 0], points_v[0, 1]), columns_v, high_ref, low_ref, sems)
    for index, at in enumerate(pieces(samples_ref.shape[0])):
        term = sum_of(residual_ref[at, :], columns_v[0, at, :], columns_v[1, at, :])
        total_ref[...] = term if index == 0 else total_ref[...] + term
    wait_all(points_out, *copies)


def beside_kernel(block, live_ref, samples_ref, points_ref, inverse_ref, high_ref, low_ref, inverse_v, points_v, columns_v, sems):
    points_in = copy_of(points_ref.at[block + 1], points_v, sems.at[3, 0])
    inverse_in = copy_of(inverse_ref.at[block], inverse_v, sems.at[2, 0])
    points_in.wait()
    copies = make_columns(live_ref, samples_ref, (points_v[0], points_v[1]), columns_v, high_ref, low_ref, sems)
    wait_all(inverse_in, *copies)


def coefs_of(sums_ref, inverse_ref):
    return jnp.concatenate(split(dot3(split(sums_ref[...]), split(inverse_ref[...]), ((1,), (1,))).T), axis=1)


def updated(residual, high, low, coefs):
    width = residual.shape[1]
    both = dot(high, coefs, ((1,), (0,)))
    return residual - (both[:, :width] + both[:, width:] + dot(low, coefs[:, :width], ((1,), (0,))))


def middle_kernel(block, live_ref, sums_ref, inverse_ref, residual_ref, high_ref, low_ref, next_high, next_low, inverses, *refs):
    out_ref, total_ref, inverse_v, coefs_v, residual_v, columns_v, next_v, sems = refs
    parts = pieces(out_ref.shape[0])
    first_in = [
        [
            copy_of(residual_ref.at[at], residual_v.at[at], sems.at[0, i]),
            copy_of(high_ref.at[at], columns_v.at[0, at], sems.at[1, i]),
            copy_of(low_ref.at[at], columns_v.at[1, at], sems.at[2, i]),
        ]
        for i, at in enumerate(parts)
    ]
    next_in = [
        [copy_of(ref.at[at], next_v.at[kind, at], sems.at[3 + kind, i]) for kind, ref in enumerate((next_high, next_low))]
        for i, at in enumerate(parts)
    ]
    inverse_in = copy_of(inverses.at[block + 1], inverse_v, sems.at[5, 0])

    @stage(live_ref)
    def _():
        coefs_v[...] = coefs_of(sums_ref, inverse_ref)

    for copies, at in zip(first_in, parts):
        wait_all(*copies)

        @stage(live_ref)
        def _():
            out_ref[at, :] = updated(residual_v[at, :], columns_v[0, at, :], columns_v[1, at, :], coefs_v[...])

    for copies, at in zip(next_in, parts):
        wait_all(*copies)

        @stage(live_ref)
        def _():
            term = sum_of(out_ref[at, :], next_v[0, at, :], next_v[1, at, :])
            total_ref[...] = term if at.start == 0 else total_ref[...] + term

    inverse_in.wait()


def last_kernel(live_ref, sums_ref, inverse_ref, residual_ref, high_ref, low_ref, out_ref, coefs_v, residual_v, columns_v, sems):
    parts = pieces(out_ref.shape[0])
    columns_in = [
        [copy_of(ref.at[at], columns_v.at[kind, at], sems.at[kind, i]) for kind, ref in enumerate((high_ref, low_ref))]
        for i, at in enumerate(parts)
    ]

    @stage(live_ref)
    def _():
        coefs_v[...] = coefs_of(sums_ref, inverse_ref)

    out = []
    for copies, at in zip(columns_in, parts):
        wait_all(*copies)

        @stage(live_ref)
        def _():
            residual_v[at, :] = updated(residual_ref[at, :], columns_v[0, at, :], columns_v[1, at, :], coefs_v[...])

        out.append(copy_of(residual_v.at[at], out_ref.at[at], sems.at[2, len(out)]))
    wait_all(*out)


SPACES = {"V": pltpu.VMEM, "H": pltpu.HBM, "S": pltpu.SMEM}


def local(kernel, args, places, outs, scratch_shapes, flops, name):
    args = [pltpu.with_memory_space_constraint(a, SPACES[p]) if p != "S" else a for a, p in zip(args, places)]
    moved = sum(a.size * a.dtype.itemsize for a in args)
    made = pl.pallas_call(
        kernel,
        out_shape=[SPACES[p](shape, dtype) for p, shape, dtype in outs],
        in_specs=[pl.BlockSpec(memory_space=SPACES[p]) for p in places],
        out_specs=[pl.BlockSpec(memory_space=SPACES[p]) for p, _, _ in outs],
        scratch_shapes=scratch_shapes,
        cost_estimate=pl.CostEstimate(flops=flops, bytes_accessed=moved, transcendentals=0),
        compiler_params=pltpu.CompilerParams(vmem_limit_bytes=LIMIT),
        name=name,
    )(*args)
    return made if len(outs) > 1 else made[0]


def sum_over_rows(totals, groups, beside):
    order = order_of(groups, SUMS_SEED)
    width, size = totals.shape
    piece = round_up(width, groups) // groups
    padded = jnp.pad(totals, ((0, piece * groups - width), (0, 0))) if piece * groups != width else totals
    got = exchange(padded.reshape(groups, piece, size), order)
    made = None
    if beside is not None:
        got, made = lax.optimization_barrier((got, beside()))
    own = jnp.sum(got, axis=0)
    back = exchange(jnp.broadcast_to(own[None], (groups, piece, size)), order)
    return back.reshape(groups * piece, size)[:width], made


def on_device(groups, cores, counts, samples, targets, point_ids, block_inverse):
    rows_here, feat = samples.shape
    blocks, size = point_ids.shape
    mean = blocks * size / groups
    cap = round_up(max(1, round((mean + 4 * mean**0.5) / cores)), 8)

    order = order_of(groups, POINTS_SEED)
    rows, slots, most, samples_split = local(
        functools.partial(pick_kernel, order, cores, cap),
        (counts, point_ids, samples),
        "SVH",
        [("V", (cap, feat), F32), ("V", (1, blocks * size), jnp.int32), ("S", (1,), jnp.int32), ("V", (rows_here, 2 * feat), BF16)],
        [
            pltpu.VMEM(samples.shape, F32),
            pltpu.VMEM((cap, rows_here), BF16),
            pltpu.SemaphoreType.DMA((len(pieces(rows_here, HALF_STEP)),)),
        ],
        4 * cap * rows_here * feat,
        "pick",
    )

    def general(rows):
        ids = jnp.pad(point_ids.reshape(-1), (0, cores * groups * cap - blocks * size), constant_values=-1)
        ids = lax.dynamic_slice_in_dim(ids, lax.axis_index("tgt") * groups * cap, groups * cap)
        local = ids - lax.axis_index("rows") * rows_here
        owned = (local >= 0) & (local < rows_here)
        taken = jnp.take(samples, jnp.clip(local, 0, rows_here - 1), axis=0)
        taken = jnp.where(owned[:, None], taken, 0.0)
        return jnp.sum(exchange(taken.reshape(groups, cap, feat), order), axis=0)

    rows = lax.cond(most[0] > cap * cores, general, lambda rows: rows, rows)
    got = exchange(jnp.broadcast_to(rows[None], (groups, cap, feat)), order).reshape(groups * cap, feat)
    held = [lax.ppermute(got, "tgt", [((c + shift) % cores, c) for c in range(cores)]) for shift in range(1, cores)]
    found = local(
        functools.partial(own_kernel, cores),
        (slots, got),
        "VV",
        [("V", (blocks, 2 * feat, size), BF16)],
        [],
        4 * groups * cap * feat * blocks * size,
        "own",
    )
    held, found = lax.optimization_barrier((held, found))

    width = targets.shape[1]
    columns_v = pltpu.VMEM((2, rows_here, size), BF16)
    residual_v = pltpu.VMEM((rows_here, width), F32)
    coefs_v = pltpu.VMEM((size, 2 * width), BF16)
    sems = pltpu.SemaphoreType.DMA((6, len(pieces(rows_here))))
    columns_out = [("H", (rows_here, size), BF16)] * 2
    inverse_out = ("V", (size, size), F32)
    totals_out = ("V", (width, size), F32)
    work = 6 * rows_here * size

    residual = targets
    *columns, totals, points = local(
        first_kernel,
        (counts, residual, samples_split, slots, found, *held),
        "SVVVV" + "V" * len(held),
        [*columns_out, totals_out, ("H", (blocks, 2, feat, size), BF16)],
        [pltpu.VMEM((blocks, 2, feat, size), BF16), columns_v, sems],
        work * (feat + width),
        "first",
    )
    for b in range(blocks - 1):

        def beside(b=b, points=points):
            args = (counts, samples_split, points, block_inverse)
            outs = [*columns_out, inverse_out]
            scratch = [pltpu.VMEM((2, feat, size), BF16), columns_v, sems]
            return local(functools.partial(beside_kernel, b), args, "SVHH", outs, scratch, work * feat, "beside")

        sums, (*following, inverse) = sum_over_rows(totals, groups, beside)
        residual, totals, inverse = local(
            functools.partial(middle_kernel, b),
            (counts, sums, inverse, residual, *columns, *following, block_inverse),
            "SVVHHHHHH",
            [("V", (rows_here, width), F32), totals_out, inverse_out],
            [coefs_v, residual_v, columns_v, columns_v, sems],
            2 * work * width,
            "middle",
        )
        columns = following
    sums, _ = sum_over_rows(totals, groups, None)
    return local(
        last_kernel,
        (counts, sums, inverse, residual, *columns),
        "SVVVHH",
        [("H", (rows_here, width), F32)],
        [coefs_v, residual_v, columns_v, sems],
        work * width,
        "last",
    )


def solution(mesh):
    return jax.shard_map(
        functools.partial(on_device, mesh.shape["rows"], mesh.shape["tgt"]),
        mesh=mesh,
        in_specs=(P("rows"), P("rows", None), P("rows", "tgt"), P(), P()),
        out_specs=P("rows", "tgt"),
        check_vma=False,
    )
```

```python
import functools
import random

import jax
import jax.numpy as jnp
from jax import lax
from jax.experimental import pallas as pl
from jax.experimental.pallas import tpu as pltpu
from jax.sharding import PartitionSpec as P

F32 = jnp.float32
BF16 = jnp.bfloat16
ROWS_STEP = 512
HALF_STEP = 1024
LIMIT = 24 * 2**20
POINTS_SEED = 14
SUMS_SEED = 152


def order_of(groups, seed):
    order = list(range(groups))
    random.Random(seed).shuffle(order)
    return order


def exchange(x, order):
    return lax.all_to_all(x, "rows", 0, 0, axis_index_groups=[order])


def round_up(value, unit):
    return -(-value // unit) * unit


def split(x):
    high = x.astype(BF16)
    return high, (x - high.astype(F32)).astype(BF16)


def dot(a, b, dims):
    return lax.dot_general(a, b, (dims, ((), ())), preferred_element_type=F32)


def dot3(a, b, dims):
    return dot(a[0], b[0], dims) + dot(a[0], b[1], dims) + dot(a[1], b[0], dims)


def pieces(rows, step=ROWS_STEP):
    step = min(step, rows)
    return [pl.ds(start, step) for start in range(0, rows, step)]


def copy_of(source, target, sem):
    copy = pltpu.make_async_copy(source, target, sem)
    copy.start()
    return copy


def stage(live_ref):
    return pl.when(live_ref[0] >= 0)


def wait_all(*copies):
    for copy in copies:
        copy.wait()


def pick_kernel(order, cores, cap, live_ref, ids_ref, samples_ref, rows_ref, slots_ref, most_ref, parts_ref, samples_v, chosen_v, sems):
    (rows_here, feat), groups = samples_ref.shape, len(order)
    parts = pieces(rows_here, HALF_STEP)
    copies = [copy_of(samples_ref.at[at], samples_v.at[at], sems.at[i]) for i, at in enumerate(parts)]
    me, core = lax.axis_index("rows"), lax.axis_index("tgt")

    @stage(live_ref)
    def _():
        ids = jnp.concatenate([ids_ref[b : b + 1, :] for b in range(ids_ref.shape[0])], axis=1)
        count = ids.shape[1]
        owner = lax.div(ids, jnp.int32(rows_here))
        local = ids - owner * rows_here
        mine = lax.broadcasted_iota(jnp.int32, (groups, count), 0) == owner
        seen = mine.astype(jnp.int32)
        lane = lax.broadcasted_iota(jnp.int32, (groups, count), 1)
        step = 1
        while step < count:
            seen = seen + jnp.where(lane >= step, pltpu.roll(seen, step, 1), 0)
            step *= 2
        most = jnp.max(seen)
        rank = jnp.sum(jnp.where(mine, seen, 0), axis=0, keepdims=True) - 1
        half = lax.div(rank, jnp.int32(cap))
        turn = jnp.zeros_like(owner)
        for index, device in enumerate(order):
            turn = jnp.where(owner == device, index, turn)
        packed = (half * groups + turn) * cap + (rank - half * cap)
        place = lax.broadcasted_iota(jnp.int32, (1, count), 1)
        slots_ref[...] = jnp.where(most > cap * cores, place, packed)
        most_ref[0] = most

        wanted = lax.broadcasted_iota(jnp.int32, (cap, count), 0) + core * cap
        sent = jnp.sum(jnp.where((wanted == rank) & (owner == me), local, 0), axis=1, keepdims=True)
        chosen_v[...] = jnp.where(lax.broadcasted_iota(jnp.int32, (cap, rows_here), 1) == sent, 1.0, 0.0).astype(BF16)

    for copy, at in zip(copies, parts):
        copy.wait()

        @stage(live_ref)
        def _():
            parts_ref[at, :] = jnp.concatenate(split(samples_v[at, :]), axis=1)
            both = dot(chosen_v[:, at], parts_ref[at, :], ((1,), (0,)))
            found = both[:, :feat] + both[:, feat:]
            rows_ref[...] = found if at.start == 0 else rows_ref[...] + found


def found_in(ref, slots, shift, cores):
    depth = ref.shape[0]
    base = lax.rem(lax.axis_index("tgt") + shift, cores) * depth
    slot = lax.broadcasted_iota(jnp.int32, (depth, slots.shape[1]), 0) + base
    taken = jnp.where(slot == slots, 1.0, 0.0).astype(BF16)
    return dot(jnp.concatenate(split(ref[...]), axis=1), taken, ((0,), (0,)))


def own_kernel(cores, slots_ref, held_ref, found_ref):
    blocks, _, size = found_ref.shape
    for b in range(blocks):
        found_ref[b] = found_in(held_ref, slots_ref[:, b * size : (b + 1) * size], 0, cores).astype(BF16)


def make_columns(live_ref, samples_ref, points, columns_v, high_ref, low_ref, sems):
    rows, feat = samples_ref.shape[0], samples_ref.shape[1] // 2
    scale = 0.5 / feat**0.5
    copies = []
    for index, half in enumerate(pieces(rows, HALF_STEP)):
        for at in [pl.ds(half.start + part.start, part.size) for part in pieces(half.size)]:
            base = dot3((samples_ref[at, :feat], samples_ref[at, feat:]), points, ((1,), (0,))) * scale + 1.0
            slot = lax.broadcasted_iota(jnp.int32, (at.size, 1), 0) + at.start
            columns_v[0, at, :], columns_v[1, at, :] = split(jnp.where(slot < live_ref[0], base * base * base, 0.0))
        for kind, ref in enumerate((high_ref, low_ref)):
            copies.append(copy_of(columns_v.at[kind, half], ref.at[half], sems.at[kind, index]))
    return copies


def sum_of(residual, high, low):
    width = residual.shape[1]
    residual = split(residual)
    both = dot(jnp.concatenate(residual, axis=1), high, ((0,), (0,)))
    return both[:width] + both[width:] + dot(residual[0], low, ((0,), (0,)))


def points_of(found, held, slots):
    total = found.astype(F32)
    for shift, ref in enumerate(held):
        total = total + found_in(ref, slots, shift + 1, len(held) + 1)
    feat = total.shape[0] // 2
    return total[:feat].astype(BF16), total[feat:].astype(BF16)


def first_kernel(cores, live_ref, residual_ref, samples_ref, slots_ref, found_ref, *refs):
    held, refs = refs[: cores - 1], refs[cores - 1 :]
    high_ref, low_ref, total_ref, slots_out, found_out, *held_out, points_v, columns_v, sems = refs
    blocks, _, size = found_ref.shape
    copies = [copy_of(found_ref.at[pl.ds(1, blocks - 1)], found_out, sems.at[3, 0]), copy_of(slots_ref, slots_out, sems.at[3, 1])]
    copies += [copy_of(ref, out, sems.at[4, i]) for i, (ref, out) in enumerate(zip(held, held_out))]
    points_v[0], points_v[1] = points_of(found_ref[0], held, slots_ref[:, :size])
    copies += make_columns(live_ref, samples_ref, (points_v[0], points_v[1]), columns_v, high_ref, low_ref, sems)
    for index, at in enumerate(pieces(samples_ref.shape[0])):
        term = sum_of(residual_ref[at, :], columns_v[0, at, :], columns_v[1, at, :])
        total_ref[...] = term if index == 0 else total_ref[...] + term
    wait_all(*copies)


def beside_kernel(block, cores, live_ref, samples_ref, slots_ref, found_ref, inverse_ref, *refs):
    held, refs = refs[: cores - 1], refs[cores - 1 :]
    high_ref, low_ref, inverse_v, points_v, slots_v, found_v, *held_v, columns_v, sems = refs
    size = found_v.shape[1]
    in_flight = [copy_of(found_ref.at[block], found_v, sems.at[3, 0]), copy_of(slots_ref, slots_v, sems.at[3, 1])]
    in_flight += [copy_of(ref, v, sems.at[4, i]) for i, (ref, v) in enumerate(zip(held, held_v))]
    inverse_in = copy_of(inverse_ref.at[block], inverse_v, sems.at[2, 0])
    wait_all(*in_flight)
    points_v[0], points_v[1] = points_of(found_v[...], held_v, slots_v[:, (block + 1) * size : (block + 2) * size])
    copies = make_columns(live_ref, samples_ref, (points_v[0], points_v[1]), columns_v, high_ref, low_ref, sems)
    wait_all(inverse_in, *copies)


def coefs_of(sums_ref, inverse_ref):
    return jnp.concatenate(split(dot3(split(sums_ref[...]), split(inverse_ref[...]), ((1,), (1,))).T), axis=1)


def updated(residual, high, low, coefs):
    width = residual.shape[1]
    both = dot(high, coefs, ((1,), (0,)))
    return residual - (both[:, :width] + both[:, width:] + dot(low, coefs[:, :width], ((1,), (0,))))


def middle_kernel(block, live_ref, sums_ref, inverse_ref, residual_ref, high_ref, low_ref, next_high, next_low, inverses, *refs):
    out_ref, total_ref, inverse_v, coefs_v, residual_v, columns_v, next_v, sems = refs
    parts = pieces(out_ref.shape[0])
    first_in = [
        [
            copy_of(residual_ref.at[at], residual_v.at[at], sems.at[0, i]),
            copy_of(high_ref.at[at], columns_v.at[0, at], sems.at[1, i]),
            copy_of(low_ref.at[at], columns_v.at[1, at], sems.at[2, i]),
        ]
        for i, at in enumerate(parts)
    ]
    next_in = [
        [copy_of(ref.at[at], next_v.at[kind, at], sems.at[3 + kind, i]) for kind, ref in enumerate((next_high, next_low))]
        for i, at in enumerate(parts)
    ]
    inverse_in = copy_of(inverses.at[block + 1], inverse_v, sems.at[5, 0])

    @stage(live_ref)
    def _():
        coefs_v[...] = coefs_of(sums_ref, inverse_ref)

    for copies, at in zip(first_in, parts):
        wait_all(*copies)

        @stage(live_ref)
        def _():
            out_ref[at, :] = updated(residual_v[at, :], columns_v[0, at, :], columns_v[1, at, :], coefs_v[...])

    for copies, at in zip(next_in, parts):
        wait_all(*copies)

        @stage(live_ref)
        def _():
            term = sum_of(out_ref[at, :], next_v[0, at, :], next_v[1, at, :])
            total_ref[...] = term if at.start == 0 else total_ref[...] + term

    inverse_in.wait()


def last_kernel(live_ref, sums_ref, inverse_ref, residual_ref, high_ref, low_ref, out_ref, coefs_v, residual_v, columns_v, sems):
    parts = pieces(out_ref.shape[0])
    columns_in = [
        [copy_of(ref.at[at], columns_v.at[kind, at], sems.at[kind, i]) for kind, ref in enumerate((high_ref, low_ref))]
        for i, at in enumerate(parts)
    ]

    @stage(live_ref)
    def _():
        coefs_v[...] = coefs_of(sums_ref, inverse_ref)

    out = []
    for copies, at in zip(columns_in, parts):
        wait_all(*copies)

        @stage(live_ref)
        def _():
            residual_v[at, :] = updated(residual_ref[at, :], columns_v[0, at, :], columns_v[1, at, :], coefs_v[...])

        out.append(copy_of(residual_v.at[at], out_ref.at[at], sems.at[2, len(out)]))
    wait_all(*out)


SPACES = {"V": pltpu.VMEM, "H": pltpu.HBM, "S": pltpu.SMEM}


def local(kernel, args, places, outs, scratch_shapes, flops, name):
    args = [pltpu.with_memory_space_constraint(a, SPACES[p]) if p != "S" else a for a, p in zip(args, places)]
    moved = sum(a.size * a.dtype.itemsize for a in args)
    made = pl.pallas_call(
        kernel,
        out_shape=[SPACES[p](shape, dtype) for p, shape, dtype in outs],
        in_specs=[pl.BlockSpec(memory_space=SPACES[p]) for p in places],
        out_specs=[pl.BlockSpec(memory_space=SPACES[p]) for p, _, _ in outs],
        scratch_shapes=scratch_shapes,
        cost_estimate=pl.CostEstimate(flops=flops, bytes_accessed=moved, transcendentals=0),
        compiler_params=pltpu.CompilerParams(vmem_limit_bytes=LIMIT),
        name=name,
    )(*args)
    return made if len(outs) > 1 else made[0]


def sum_over_rows(totals, groups, beside):
    order = order_of(groups, SUMS_SEED)
    width, size = totals.shape
    piece = round_up(width, groups) // groups
    padded = jnp.pad(totals, ((0, piece * groups - width), (0, 0))) if piece * groups != width else totals
    got = exchange(padded.reshape(groups, piece, size), order)
    made = None
    if beside is not None:
        got, made = lax.optimization_barrier((got, beside()))
    own = jnp.sum(got, axis=0)
    back = exchange(jnp.broadcast_to(own[None], (groups, piece, size)), order)
    return back.reshape(groups * piece, size)[:width], made


def on_device(groups, cores, counts, samples, targets, point_ids, block_inverse):
    rows_here, feat = samples.shape
    blocks, size = point_ids.shape
    mean = blocks * size / groups
    cap = round_up(max(1, round((mean + 4 * mean**0.5) / cores)), 8)

    order = order_of(groups, POINTS_SEED)
    rows, slots, most, samples_split = local(
        functools.partial(pick_kernel, order, cores, cap),
        (counts, point_ids, samples),
        "SVH",
        [("V", (cap, feat), F32), ("V", (1, blocks * size), jnp.int32), ("S", (1,), jnp.int32), ("V", (rows_here, 2 * feat), BF16)],
        [
            pltpu.VMEM(samples.shape, F32),
            pltpu.VMEM((cap, rows_here), BF16),
            pltpu.SemaphoreType.DMA((len(pieces(rows_here, HALF_STEP)),)),
        ],
        4 * cap * rows_here * feat,
        "pick",
    )

    def general(rows):
        ids = jnp.pad(point_ids.reshape(-1), (0, cores * groups * cap - blocks * size), constant_values=-1)
        ids = lax.dynamic_slice_in_dim(ids, lax.axis_index("tgt") * groups * cap, groups * cap)
        local = ids - lax.axis_index("rows") * rows_here
        owned = (local >= 0) & (local < rows_here)
        taken = jnp.take(samples, jnp.clip(local, 0, rows_here - 1), axis=0)
        taken = jnp.where(owned[:, None], taken, 0.0)
        return jnp.sum(exchange(taken.reshape(groups, cap, feat), order), axis=0)

    rows = lax.cond(most[0] > cap * cores, general, lambda rows: rows, rows)
    got = exchange(jnp.broadcast_to(rows[None], (groups, cap, feat)), order).reshape(groups * cap, feat)
    held = [lax.ppermute(got, "tgt", [((c + shift) % cores, c) for c in range(cores)]) for shift in range(1, cores)]
    found = local(
        functools.partial(own_kernel, cores),
        (slots, got),
        "VV",
        [("V", (blocks, 2 * feat, size), BF16)],
        [],
        4 * groups * cap * feat * blocks * size,
        "own",
    )
    held, found = lax.optimization_barrier((held, found))

    width = targets.shape[1]
    columns_v = pltpu.VMEM((2, rows_here, size), BF16)
    residual_v = pltpu.VMEM((rows_here, width), F32)
    coefs_v = pltpu.VMEM((size, 2 * width), BF16)
    sems = pltpu.SemaphoreType.DMA((6, max(cores, len(pieces(rows_here)))))
    columns_out = [("H", (rows_here, size), BF16)] * 2
    inverse_out = ("V", (size, size), F32)
    totals_out = ("V", (width, size), F32)
    work = 6 * rows_here * size

    residual = targets
    points_v = pltpu.VMEM((2, feat, size), BF16)
    high, low, totals, slots_out, found, *held = local(
        functools.partial(first_kernel, cores),
        (counts, residual, samples_split, slots, found, *held),
        "SVVVV" + "V" * len(held),
        [
            *columns_out,
            totals_out,
            ("H", slots.shape, jnp.int32),
            ("H", (blocks - 1, 2 * feat, size), BF16),
            *[("H", h.shape, F32) for h in held],
        ],
        [points_v, columns_v, sems],
        work * (feat + width),
        "first",
    )
    columns = [high, low]
    for b in range(blocks - 1):

        def beside(b=b):
            return local(
                functools.partial(beside_kernel, b, cores),
                (counts, samples_split, slots_out, found, block_inverse, *held),
                "SVHHH" + "H" * len(held),
                [*columns_out, inverse_out],
                [
                    points_v,
                    pltpu.VMEM(slots.shape, jnp.int32),
                    pltpu.VMEM((2 * feat, size), BF16),
                    *[pltpu.VMEM(h.shape, F32) for h in held],
                    columns_v,
                    sems,
                ],
                work * feat,
                "beside",
            )

        sums, (*following, inverse) = sum_over_rows(totals, groups, beside)
        residual, totals, inverse = local(
            functools.partial(middle_kernel, b),
            (counts, sums, inverse, residual, *columns, *following, block_inverse),
            "SVVHHHHHH",
            [("V", (rows_here, width), F32), totals_out, inverse_out],
            [coefs_v, residual_v, columns_v, columns_v, sems],
            2 * work * width,
            "middle",
        )
        columns = following
    sums, _ = sum_over_rows(totals, groups, None)
    return local(
        last_kernel,
        (counts, sums, inverse, residual, *columns),
        "SVVVHH",
        [("H", (rows_here, width), F32)],
        [coefs_v, residual_v, columns_v, sems],
        work * width,
        "last",
    )


def solution(mesh):
    return jax.shard_map(
        functools.partial(on_device, mesh.shape["rows"], mesh.shape["tgt"]),
        mesh=mesh,
        in_specs=(P("rows"), P("rows", None), P("rows", "tgt"), P(), P()),
        out_specs=P("rows", "tgt"),
        check_vma=False,
    )
```

```python
import functools
import random

import jax
import jax.numpy as jnp
from jax import lax
from jax.experimental import pallas as pl
from jax.experimental.pallas import tpu as pltpu
from jax.sharding import PartitionSpec as P

F32 = jnp.float32
BF16 = jnp.bfloat16
ROWS_STEP = 512
HALF_STEP = 1024
LIMIT = 24 * 2**20
POINTS_SEED = 14
SUMS_SEED = 152


def order_of(groups, seed):
    order = list(range(groups))
    random.Random(seed).shuffle(order)
    return order


def exchange(x, order):
    return lax.all_to_all(x, "rows", 0, 0, axis_index_groups=[order])


def round_up(value, unit):
    return -(-value // unit) * unit


def split(x):
    high = x.astype(BF16)
    return high, (x - high.astype(F32)).astype(BF16)


def dot(a, b, dims):
    return lax.dot_general(a, b, (dims, ((), ())), preferred_element_type=F32)


def dot3(a, b, dims):
    return dot(a[0], b[0], dims) + dot(a[0], b[1], dims) + dot(a[1], b[0], dims)


def pieces(rows, step=ROWS_STEP):
    step = min(step, rows)
    return [pl.ds(start, step) for start in range(0, rows, step)]


def copy_of(source, target, sem):
    copy = pltpu.make_async_copy(source, target, sem)
    copy.start()
    return copy


def stage(live_ref):
    return pl.when(live_ref[0] >= 0)


def wait_all(*copies):
    for copy in copies:
        copy.wait()


def pick_kernel(order, cores, caps, live_ref, ids_ref, samples_ref, rows_ref, slots_ref, most_ref, samples_v, chosen_v, sems):
    (rows_here, feat), groups = samples_ref.shape, len(order)
    parts = pieces(rows_here, HALF_STEP)
    copies = [copy_of(samples_ref.at[at], samples_v.at[at], sems.at[i]) for i, at in enumerate(parts)]
    me, core = lax.axis_index("rows"), lax.axis_index("tgt")

    @stage(live_ref)
    def _():
        ids = jnp.concatenate([ids_ref[b : b + 1, :] for b in range(ids_ref.shape[0])], axis=1)
        count = ids.shape[1]
        owner = lax.div(ids, jnp.int32(rows_here))
        local = ids - owner * rows_here
        mine = lax.broadcasted_iota(jnp.int32, (groups, count), 0) == owner
        seen = mine.astype(jnp.int32)
        lane = lax.broadcasted_iota(jnp.int32, (groups, count), 1)
        step = 1
        while step < count:
            seen = seen + jnp.where(lane >= step, pltpu.roll(seen, step, 1), 0)
            step *= 2
        most = jnp.max(seen)
        rank = jnp.sum(jnp.where(mine, seen, 0), axis=0, keepdims=True) - 1
        cap = jnp.int32(caps[-1])
        for less in caps[-2::-1]:
            cap = jnp.where(most <= less * cores, less, cap)
        half = lax.div(rank, cap)
        turn = jnp.zeros_like(owner)
        for index, device in enumerate(order):
            turn = jnp.where(owner == device, index, turn)
        packed = half * (groups * caps[-1]) + turn * cap + (rank - half * cap)
        place = lax.broadcasted_iota(jnp.int32, (1, count), 1)
        slots_ref[...] = jnp.where(most > caps[-1] * cores, place, packed)
        most_ref[0] = most

        wanted = lax.broadcasted_iota(jnp.int32, (caps[-1], count), 0) + core * cap
        sent = jnp.sum(jnp.where((wanted == rank) & (owner == me), local, 0), axis=1, keepdims=True)
        chosen_v[...] = jnp.where(lax.broadcasted_iota(jnp.int32, (caps[-1], rows_here), 1) == sent, 1.0, 0.0).astype(BF16)

    for copy, at in zip(copies, parts):
        copy.wait()

        @stage(live_ref)
        def _():
            both = dot(chosen_v[:, at], jnp.concatenate(split(samples_v[at, :]), axis=1), ((1,), (0,)))
            found = both[:, :feat] + both[:, feat:]
            rows_ref[...] = found if at.start == 0 else rows_ref[...] + found


def owned_kernel(local_ref, samples_ref, out_ref, samples_v, sems):
    copy_of(samples_ref, samples_v, sems.at[0]).wait()
    rows, feat = samples_v.shape
    parts = jnp.concatenate(split(samples_v[...]), axis=1)
    for at in pieces(local_ref.shape[0], 128):
        chosen = lax.broadcasted_iota(jnp.int32, (at.size, rows), 1) == local_ref[at, :]
        both = dot(jnp.where(chosen, 1.0, 0.0).astype(BF16), parts, ((1,), (0,)))
        out_ref[at, :] = both[:, :feat] + both[:, feat:]


def found_in(ref, slots, shift, cores):
    depth = ref.shape[0]
    base = lax.rem(lax.axis_index("tgt") + shift, cores) * depth
    slot = lax.broadcasted_iota(jnp.int32, (depth, slots.shape[1]), 0) + base
    taken = jnp.where(slot == slots, 1.0, 0.0).astype(BF16)
    return dot(jnp.concatenate(split(ref[...]), axis=1), taken, ((0,), (0,)))


def own_kernel(cores, live_ref, slots_ref, held_ref, samples_ref, found_ref, samples_v, sems):
    blocks, _, size = found_ref.shape
    samples_in = copy_of(samples_ref, samples_v, sems.at[0])

    @stage(live_ref)
    def _():
        for b in range(blocks):
            found_ref[b] = found_in(held_ref, slots_ref[:, b * size : (b + 1) * size], 0, cores).astype(BF16)

    samples_in.wait()


def make_columns(live_ref, samples_ref, points, columns_v, high_ref, low_ref, sems):
    rows, feat = samples_ref.shape
    scale = 0.5 / feat**0.5
    copies = []
    for index, half in enumerate(pieces(rows, HALF_STEP)):
        for at in [pl.ds(half.start + part.start, part.size) for part in pieces(half.size)]:
            base = dot3(split(samples_ref[at, :]), points, ((1,), (0,))) * scale + 1.0
            slot = lax.broadcasted_iota(jnp.int32, (at.size, 1), 0) + at.start
            columns_v[0, at, :], columns_v[1, at, :] = split(jnp.where(slot < live_ref[0], base * base * base, 0.0))
        for kind, ref in enumerate((high_ref, low_ref)):
            copies.append(copy_of(columns_v.at[kind, half], ref.at[half], sems.at[kind, index]))
    return copies


def sum_of(residual, high, low):
    width = residual.shape[1]
    residual = split(residual)
    both = dot(jnp.concatenate(residual, axis=1), high, ((0,), (0,)))
    return both[:width] + both[width:] + dot(residual[0], low, ((0,), (0,)))


def points_of(found, held, slots):
    total = found.astype(F32)
    for shift, ref in enumerate(held):
        total = total + found_in(ref, slots, shift + 1, len(held) + 1)
    feat = total.shape[0] // 2
    return total[:feat].astype(BF16), total[feat:].astype(BF16)


def first_kernel(cores, live_ref, residual_ref, samples_ref, slots_ref, found_ref, *refs):
    held, refs = refs[: cores - 1], refs[cores - 1 :]
    high_ref, low_ref, total_ref, slots_out, found_out, *held_out, points_v, columns_v, sems = refs
    blocks, _, size = found_ref.shape
    copies = [copy_of(found_ref.at[pl.ds(1, blocks - 1)], found_out, sems.at[3, 0]), copy_of(slots_ref, slots_out, sems.at[3, 1])]
    copies += [copy_of(ref, out, sems.at[4, i]) for i, (ref, out) in enumerate(zip(held, held_out))]
    points_v[0], points_v[1] = points_of(found_ref[0], held, slots_ref[:, :size])
    copies += make_columns(live_ref, samples_ref, (points_v[0], points_v[1]), columns_v, high_ref, low_ref, sems)
    for index, at in enumerate(pieces(samples_ref.shape[0])):
        term = sum_of(residual_ref[at, :], columns_v[0, at, :], columns_v[1, at, :])
        total_ref[...] = term if index == 0 else total_ref[...] + term
    wait_all(*copies)


def beside_kernel(block, cores, live_ref, samples_ref, slots_ref, found_ref, inverse_ref, *refs):
    held, refs = refs[: cores - 1], refs[cores - 1 :]
    high_ref, low_ref, inverse_v, samples_v, points_v, slots_v, found_v, *held_v, columns_v, sems = refs
    size = found_v.shape[1]
    in_flight = [copy_of(found_ref.at[block], found_v, sems.at[3, 0]), copy_of(slots_ref, slots_v, sems.at[3, 1])]
    in_flight += [copy_of(ref, v, sems.at[4, i]) for i, (ref, v) in enumerate(zip(held, held_v))]
    samples_in = copy_of(samples_ref, samples_v, sems.at[2, 1])
    inverse_in = copy_of(inverse_ref.at[block], inverse_v, sems.at[2, 0])
    wait_all(*in_flight, samples_in)
    points_v[0], points_v[1] = points_of(found_v[...], held_v, slots_v[:, (block + 1) * size : (block + 2) * size])
    copies = make_columns(live_ref, samples_v, (points_v[0], points_v[1]), columns_v, high_ref, low_ref, sems)
    wait_all(inverse_in, *copies)


def coefs_of(sums_ref, inverse_ref):
    return jnp.concatenate(split(dot3(split(sums_ref[...]), split(inverse_ref[...]), ((1,), (1,))).T), axis=1)


def updated(residual, high, low, coefs):
    width = residual.shape[1]
    both = dot(high, coefs, ((1,), (0,)))
    return residual - (both[:, :width] + both[:, width:] + dot(low, coefs[:, :width], ((1,), (0,))))


def middle_kernel(block, live_ref, sums_ref, inverse_ref, residual_ref, high_ref, low_ref, next_high, next_low, inverses, *refs):
    out_ref, total_ref, inverse_v, coefs_v, residual_v, columns_v, next_v, sems = refs
    parts = pieces(out_ref.shape[0])
    first_in = [
        [
            copy_of(residual_ref.at[at], residual_v.at[at], sems.at[0, i]),
            copy_of(high_ref.at[at], columns_v.at[0, at], sems.at[1, i]),
            copy_of(low_ref.at[at], columns_v.at[1, at], sems.at[2, i]),
        ]
        for i, at in enumerate(parts)
    ]
    next_in = [
        [copy_of(ref.at[at], next_v.at[kind, at], sems.at[3 + kind, i]) for kind, ref in enumerate((next_high, next_low))]
        for i, at in enumerate(parts)
    ]
    inverse_in = copy_of(inverses.at[block + 1], inverse_v, sems.at[5, 0])

    @stage(live_ref)
    def _():
        coefs_v[...] = coefs_of(sums_ref, inverse_ref)

    for copies, at in zip(first_in, parts):
        wait_all(*copies)

        @stage(live_ref)
        def _():
            out_ref[at, :] = updated(residual_v[at, :], columns_v[0, at, :], columns_v[1, at, :], coefs_v[...])

    for copies, at in zip(next_in, parts):
        wait_all(*copies)

        @stage(live_ref)
        def _():
            term = sum_of(out_ref[at, :], next_v[0, at, :], next_v[1, at, :])
            total_ref[...] = term if at.start == 0 else total_ref[...] + term

    inverse_in.wait()


def last_kernel(live_ref, sums_ref, inverse_ref, residual_ref, high_ref, low_ref, out_ref, coefs_v, residual_v, columns_v, sems):
    parts = pieces(out_ref.shape[0])
    columns_in = [
        [copy_of(ref.at[at], columns_v.at[kind, at], sems.at[kind, i]) for kind, ref in enumerate((high_ref, low_ref))]
        for i, at in enumerate(parts)
    ]

    @stage(live_ref)
    def _():
        coefs_v[...] = coefs_of(sums_ref, inverse_ref)

    out = []
    for copies, at in zip(columns_in, parts):
        wait_all(*copies)

        @stage(live_ref)
        def _():
            residual_v[at, :] = updated(residual_ref[at, :], columns_v[0, at, :], columns_v[1, at, :], coefs_v[...])

        out.append(copy_of(residual_v.at[at], out_ref.at[at], sems.at[2, len(out)]))
    wait_all(*out)


SPACES = {"V": pltpu.VMEM, "H": pltpu.HBM, "S": pltpu.SMEM}


def local(kernel, args, places, outs, scratch_shapes, flops, name):
    args = [pltpu.with_memory_space_constraint(a, SPACES[p]) if p != "S" else a for a, p in zip(args, places)]
    moved = sum(a.size * a.dtype.itemsize for a in args)
    made = pl.pallas_call(
        kernel,
        out_shape=[SPACES[p](shape, dtype) for p, shape, dtype in outs],
        in_specs=[pl.BlockSpec(memory_space=SPACES[p]) for p in places],
        out_specs=[pl.BlockSpec(memory_space=SPACES[p]) for p, _, _ in outs],
        scratch_shapes=scratch_shapes,
        cost_estimate=pl.CostEstimate(flops=flops, bytes_accessed=moved, transcendentals=0),
        compiler_params=pltpu.CompilerParams(vmem_limit_bytes=LIMIT),
        name=name,
    )(*args)
    return made if len(outs) > 1 else made[0]


def sum_over_rows(totals, groups, beside):
    order = order_of(groups, SUMS_SEED)
    width, size = totals.shape
    piece = round_up(width, groups) // groups
    padded = jnp.pad(totals, ((0, piece * groups - width), (0, 0))) if piece * groups != width else totals
    got = exchange(padded.reshape(groups, piece, size), order)
    made = None
    if beside is not None:
        got, made = lax.optimization_barrier((got, beside()))
    own = jnp.sum(got, axis=0)
    back = exchange(jnp.broadcast_to(own[None], (groups, piece, size)), order)
    return back.reshape(groups * piece, size)[:width], made


def on_device(groups, cores, counts, samples, targets, point_ids, block_inverse):
    rows_here, feat = samples.shape
    blocks, size = point_ids.shape
    mean = blocks * size / groups
    caps = sorted({round_up(max(1, round((mean + spread * mean**0.5) / cores)), 8) for spread in (2, 4)})
    cap = caps[-1]

    order = order_of(groups, POINTS_SEED)
    rows, slots, most = local(
        functools.partial(pick_kernel, order, cores, caps),
        (counts, point_ids, samples),
        "SVH",
        [("V", (cap, feat), F32), ("V", (1, blocks * size), jnp.int32), ("S", (1,), jnp.int32)],
        [
            pltpu.VMEM(samples.shape, F32),
            pltpu.VMEM((cap, rows_here), BF16),
            pltpu.SemaphoreType.DMA((len(pieces(rows_here, HALF_STEP)),)),
        ],
        4 * cap * rows_here * feat,
        "pick",
    )

    def general(rows):
        ids = jnp.pad(point_ids.reshape(-1), (0, cores * groups * cap - blocks * size), constant_values=-1)
        ids = lax.dynamic_slice_in_dim(ids, lax.axis_index("tgt") * groups * cap, groups * cap)
        here = ids - lax.axis_index("rows") * rows_here
        taken = local(
            owned_kernel,
            (here[:, None], samples),
            "VH",
            [("V", (groups * cap, feat), F32)],
            [pltpu.VMEM(samples.shape, F32), pltpu.SemaphoreType.DMA((1,))],
            4 * groups * cap * rows_here * feat,
            "owned",
        )
        return jnp.sum(exchange(taken.reshape(groups, cap, feat), order), axis=0)

    def gather(rows, count=cap):
        sent = jnp.broadcast_to(rows[None, :count], (groups, count, feat))
        got = exchange(sent, order).reshape(groups * count, feat)
        return got if count == cap else jnp.pad(got, ((0, groups * (cap - count)), (0, 0)))

    choices = [functools.partial(gather, count=count) for count in caps] + [lambda rows: gather(general(rows))]
    got = lax.switch(sum((most[0] > count * cores).astype(jnp.int32) for count in caps), choices, rows)
    held = [lax.ppermute(got, "tgt", [((c + shift) % cores, c) for c in range(cores)]) for shift in range(1, cores)]
    found, samples_v = local(
        functools.partial(own_kernel, cores),
        (counts, slots, got, samples),
        "SVVH",
        [("V", (blocks, 2 * feat, size), BF16), ("V", samples.shape, F32)],
        [pltpu.SemaphoreType.DMA((1,))],
        4 * groups * cap * feat * blocks * size,
        "own",
    )
    held, found = lax.optimization_barrier((held, found))

    width = targets.shape[1]
    columns_v = pltpu.VMEM((2, rows_here, size), BF16)
    residual_v = pltpu.VMEM((rows_here, width), F32)
    coefs_v = pltpu.VMEM((size, 2 * width), BF16)
    sems = pltpu.SemaphoreType.DMA((6, max(cores, len(pieces(rows_here)))))
    columns_out = [("H", (rows_here, size), BF16)] * 2
    inverse_out = ("V", (size, size), F32)
    totals_out = ("V", (width, size), F32)
    work = 6 * rows_here * size

    residual = targets
    points_v = pltpu.VMEM((2, feat, size), BF16)
    high, low, totals, slots_out, found, *held = local(
        functools.partial(first_kernel, cores),
        (counts, residual, samples_v, slots, found, *held),
        "SVVVV" + "V" * len(held),
        [
            *columns_out,
            totals_out,
            ("H", slots.shape, jnp.int32),
            ("H", (blocks - 1, 2 * feat, size), BF16),
            *[("H", h.shape, F32) for h in held],
        ],
        [points_v, columns_v, sems],
        work * (feat + width),
        "first",
    )
    columns = [high, low]
    for b in range(blocks - 1):

        def beside(b=b):
            return local(
                functools.partial(beside_kernel, b, cores),
                (counts, samples, slots_out, found, block_inverse, *held),
                "SHHHH" + "H" * len(held),
                [*columns_out, inverse_out],
                [
                    pltpu.VMEM(samples.shape, F32),
                    points_v,
                    pltpu.VMEM(slots.shape, jnp.int32),
                    pltpu.VMEM((2 * feat, size), BF16),
                    *[pltpu.VMEM(h.shape, F32) for h in held],
                    columns_v,
                    sems,
                ],
                work * feat,
                "beside",
            )

        sums, (*following, inverse) = sum_over_rows(totals, groups, beside)
        residual, totals, inverse = local(
            functools.partial(middle_kernel, b),
            (counts, sums, inverse, residual, *columns, *following, block_inverse),
            "SVVHHHHHH",
            [("V", (rows_here, width), F32), totals_out, inverse_out],
            [coefs_v, residual_v, columns_v, columns_v, sems],
            2 * work * width,
            "middle",
        )
        columns = following
    sums, _ = sum_over_rows(totals, groups, None)
    return local(
        last_kernel,
        (counts, sums, inverse, residual, *columns),
        "SVVVHH",
        [("H", (rows_here, width), F32)],
        [coefs_v, residual_v, columns_v, sems],
        work * width,
        "last",
    )


def solution(mesh):
    return jax.shard_map(
        functools.partial(on_device, mesh.shape["rows"], mesh.shape["tgt"]),
        mesh=mesh,
        in_specs=(P("rows"), P("rows", None), P("rows", "tgt"), P(), P()),
        out_specs=P("rows", "tgt"),
        check_vma=False,
    )
```

```python
import functools
import random

import jax
import jax.numpy as jnp
from jax import lax
from jax.experimental import pallas as pl
from jax.experimental.pallas import tpu as pltpu
from jax.sharding import PartitionSpec as P

F32 = jnp.float32
BF16 = jnp.bfloat16
ROWS_STEP = 512
HALF_STEP = 1024
LIMIT = 24 * 2**20
POINTS_SEED = 14
SUMS_SEED = 152


def order_of(groups, seed):
    order = list(range(groups))
    random.Random(seed).shuffle(order)
    return order


def exchange(x, order):
    return lax.all_to_all(x, "rows", 0, 0, axis_index_groups=[order])


def round_up(value, unit):
    return -(-value // unit) * unit


def split(x):
    high = x.astype(BF16)
    return high, (x - high.astype(F32)).astype(BF16)


def dot(a, b, dims):
    return lax.dot_general(a, b, (dims, ((), ())), preferred_element_type=F32)


def dot3(a, b, dims):
    return dot(a[0], b[0], dims) + dot(a[0], b[1], dims) + dot(a[1], b[0], dims)


def pieces(rows, step=ROWS_STEP):
    step = min(step, rows)
    return [pl.ds(start, step) for start in range(0, rows, step)]


def copy_of(source, target, sem):
    copy = pltpu.make_async_copy(source, target, sem)
    copy.start()
    return copy


def stage(live_ref):
    return pl.when(live_ref[0] >= 0)


def wait_all(*copies):
    for copy in copies:
        copy.wait()


def pick_kernel(order, cores, caps, live_ref, ids_ref, samples_ref, rows_ref, slots_ref, most_ref, samples_v, chosen_v, sems):
    (rows_here, feat), groups = samples_ref.shape, len(order)
    parts = pieces(rows_here, HALF_STEP)
    copies = [copy_of(samples_ref.at[at], samples_v.at[at], sems.at[i]) for i, at in enumerate(parts)]
    me, core = lax.axis_index("rows"), lax.axis_index("tgt")

    @stage(live_ref)
    def _():
        ids = jnp.concatenate([ids_ref[b : b + 1, :] for b in range(ids_ref.shape[0])], axis=1)
        count = ids.shape[1]
        owner = lax.div(ids, jnp.int32(rows_here))
        local = ids - owner * rows_here
        mine = lax.broadcasted_iota(jnp.int32, (groups, count), 0) == owner
        seen = mine.astype(jnp.int32)
        lane = lax.broadcasted_iota(jnp.int32, (groups, count), 1)
        step = 1
        while step < count:
            seen = seen + jnp.where(lane >= step, pltpu.roll(seen, step, 1), 0)
            step *= 2
        most = jnp.max(seen)
        rank = jnp.sum(jnp.where(mine, seen, 0), axis=0, keepdims=True) - 1
        cap = jnp.int32(caps[-1])
        for less in caps[-2::-1]:
            cap = jnp.where(most <= less * cores, less, cap)
        half = lax.div(rank, cap)
        turn = jnp.zeros_like(owner)
        for index, device in enumerate(order):
            turn = jnp.where(owner == device, index, turn)
        packed = half * (groups * caps[-1]) + turn * cap + (rank - half * cap)
        place = lax.broadcasted_iota(jnp.int32, (1, count), 1)
        slots_ref[...] = jnp.where(most > caps[-1] * cores, place, packed)
        most_ref[0] = most

        wanted = lax.broadcasted_iota(jnp.int32, (caps[-1], count), 0) + core * cap
        sent = jnp.sum(jnp.where((wanted == rank) & (owner == me), local, 0), axis=1, keepdims=True)
        chosen_v[...] = jnp.where(lax.broadcasted_iota(jnp.int32, (caps[-1], rows_here), 1) == sent, 1.0, 0.0).astype(BF16)

    for copy, at in zip(copies, parts):
        copy.wait()

        @stage(live_ref)
        def _():
            both = dot(chosen_v[:, at], jnp.concatenate(split(samples_v[at, :]), axis=1), ((1,), (0,)))
            found = both[:, :feat] + both[:, feat:]
            rows_ref[...] = found if at.start == 0 else rows_ref[...] + found


def owned_kernel(local_ref, samples_ref, out_ref, samples_v, sems):
    copy_of(samples_ref, samples_v, sems.at[0]).wait()
    rows, feat = samples_v.shape
    parts = jnp.concatenate(split(samples_v[...]), axis=1)
    for at in pieces(local_ref.shape[0], 128):
        chosen = lax.broadcasted_iota(jnp.int32, (at.size, rows), 1) == local_ref[at, :]
        both = dot(jnp.where(chosen, 1.0, 0.0).astype(BF16), parts, ((1,), (0,)))
        out_ref[at, :] = both[:, :feat] + both[:, feat:]


def found_in(ref, slots, shift, cores):
    depth = ref.shape[0]
    base = lax.rem(lax.axis_index("tgt") + shift, cores) * depth
    slot = lax.broadcasted_iota(jnp.int32, (depth, slots.shape[1]), 0) + base
    taken = jnp.where(slot == slots, 1.0, 0.0).astype(BF16)
    return dot(jnp.concatenate(split(ref[...]), axis=1), taken, ((0,), (0,)))


def own_kernel(cores, live_ref, slots_ref, held_ref, samples_ref, found_ref, parts_ref, samples_v, sems):
    blocks, _, size = found_ref.shape
    samples_in = copy_of(samples_ref, samples_v, sems.at[0])

    @stage(live_ref)
    def _():
        for b in range(blocks):
            found_ref[b] = found_in(held_ref, slots_ref[:, b * size : (b + 1) * size], 0, cores).astype(BF16)

    samples_in.wait()
    parts_ref[...] = jnp.concatenate(split(samples_v[...]), axis=1)


def make_columns(live_ref, samples_ref, points, columns_v, high_ref, low_ref, sems):
    rows, feat = samples_ref.shape[0], samples_ref.shape[1] // 2
    scale = 0.5 / feat**0.5
    copies = []
    for index, half in enumerate(pieces(rows, HALF_STEP)):
        for at in [pl.ds(half.start + part.start, part.size) for part in pieces(half.size)]:
            base = dot3((samples_ref[at, :feat], samples_ref[at, feat:]), points, ((1,), (0,))) * scale + 1.0
            slot = lax.broadcasted_iota(jnp.int32, (at.size, 1), 0) + at.start
            columns_v[0, at, :], columns_v[1, at, :] = split(jnp.where(slot < live_ref[0], base * base * base, 0.0))
        for kind, ref in enumerate((high_ref, low_ref)):
            copies.append(copy_of(columns_v.at[kind, half], ref.at[half], sems.at[kind, index]))
    return copies


def sum_of(residual, high, low):
    width = residual.shape[1]
    residual = split(residual)
    both = dot(jnp.concatenate(residual, axis=1), high, ((0,), (0,)))
    return both[:width] + both[width:] + dot(residual[0], low, ((0,), (0,)))


def points_of(found, held, slots):
    total = found.astype(F32)
    for shift, ref in enumerate(held):
        total = total + found_in(ref, slots, shift + 1, len(held) + 1)
    feat = total.shape[0] // 2
    return total[:feat].astype(BF16), total[feat:].astype(BF16)


def first_kernel(cores, live_ref, residual_ref, samples_ref, slots_ref, found_ref, *refs):
    held, refs = refs[: cores - 1], refs[cores - 1 :]
    high_ref, low_ref, total_ref, slots_out, found_out, *held_out, points_v, columns_v, sems = refs
    blocks, _, size = found_ref.shape
    copies = [copy_of(found_ref.at[pl.ds(1, blocks - 1)], found_out, sems.at[3, 0]), copy_of(slots_ref, slots_out, sems.at[3, 1])]
    copies += [copy_of(ref, out, sems.at[4, i]) for i, (ref, out) in enumerate(zip(held, held_out))]
    points_v[0], points_v[1] = points_of(found_ref[0], held, slots_ref[:, :size])
    copies += make_columns(live_ref, samples_ref, (points_v[0], points_v[1]), columns_v, high_ref, low_ref, sems)
    for index, at in enumerate(pieces(samples_ref.shape[0])):
        term = sum_of(residual_ref[at, :], columns_v[0, at, :], columns_v[1, at, :])
        total_ref[...] = term if index == 0 else total_ref[...] + term
    wait_all(*copies)


def beside_kernel(block, cores, live_ref, samples_ref, slots_ref, found_ref, inverse_ref, *refs):
    held, refs = refs[: cores - 1], refs[cores - 1 :]
    high_ref, low_ref, inverse_v, samples_v, points_v, slots_v, found_v, *held_v, columns_v, sems = refs
    size = found_v.shape[1]
    in_flight = [copy_of(found_ref.at[block], found_v, sems.at[3, 0]), copy_of(slots_ref, slots_v, sems.at[3, 1])]
    in_flight += [copy_of(ref, v, sems.at[4, i]) for i, (ref, v) in enumerate(zip(held, held_v))]
    in_flight.append(copy_of(samples_ref, samples_v, sems.at[2, 1]))
    inverse_in = copy_of(inverse_ref.at[block], inverse_v, sems.at[2, 0])
    wait_all(*in_flight)
    points_v[0], points_v[1] = points_of(found_v[...], held_v, slots_v[:, (block + 1) * size : (block + 2) * size])
    copies = make_columns(live_ref, samples_v, (points_v[0], points_v[1]), columns_v, high_ref, low_ref, sems)
    wait_all(inverse_in, *copies)


def coefs_of(sums_ref, inverse_ref):
    return jnp.concatenate(split(dot3(split(sums_ref[...]), split(inverse_ref[...]), ((1,), (1,))).T), axis=1)


def updated(residual, high, low, coefs):
    width = residual.shape[1]
    both = dot(high, coefs, ((1,), (0,)))
    return residual - (both[:, :width] + both[:, width:] + dot(low, coefs[:, :width], ((1,), (0,))))


def middle_kernel(block, live_ref, sums_ref, inverse_ref, residual_ref, high_ref, low_ref, next_high, next_low, inverses, *refs):
    out_ref, total_ref, inverse_v, coefs_v, residual_v, columns_v, next_v, sems = refs
    parts = pieces(out_ref.shape[0])
    first_in = [
        [
            copy_of(residual_ref.at[at], residual_v.at[at], sems.at[0, i]),
            copy_of(high_ref.at[at], columns_v.at[0, at], sems.at[1, i]),
            copy_of(low_ref.at[at], columns_v.at[1, at], sems.at[2, i]),
        ]
        for i, at in enumerate(parts)
    ]
    next_in = [
        [copy_of(ref.at[at], next_v.at[kind, at], sems.at[3 + kind, i]) for kind, ref in enumerate((next_high, next_low))]
        for i, at in enumerate(parts)
    ]
    inverse_in = copy_of(inverses.at[block + 1], inverse_v, sems.at[5, 0])

    @stage(live_ref)
    def _():
        coefs_v[...] = coefs_of(sums_ref, inverse_ref)

    for copies, at in zip(first_in, parts):
        wait_all(*copies)

        @stage(live_ref)
        def _():
            out_ref[at, :] = updated(residual_v[at, :], columns_v[0, at, :], columns_v[1, at, :], coefs_v[...])

    for copies, at in zip(next_in, parts):
        wait_all(*copies)

        @stage(live_ref)
        def _():
            term = sum_of(out_ref[at, :], next_v[0, at, :], next_v[1, at, :])
            total_ref[...] = term if at.start == 0 else total_ref[...] + term

    inverse_in.wait()


def last_kernel(live_ref, sums_ref, inverse_ref, residual_ref, high_ref, low_ref, out_ref, coefs_v, residual_v, columns_v, sems):
    parts = pieces(out_ref.shape[0])
    columns_in = [
        [copy_of(ref.at[at], columns_v.at[kind, at], sems.at[kind, i]) for kind, ref in enumerate((high_ref, low_ref))]
        for i, at in enumerate(parts)
    ]

    @stage(live_ref)
    def _():
        coefs_v[...] = coefs_of(sums_ref, inverse_ref)

    out = []
    for copies, at in zip(columns_in, parts):
        wait_all(*copies)

        @stage(live_ref)
        def _():
            residual_v[at, :] = updated(residual_ref[at, :], columns_v[0, at, :], columns_v[1, at, :], coefs_v[...])

        out.append(copy_of(residual_v.at[at], out_ref.at[at], sems.at[2, len(out)]))
    wait_all(*out)


SPACES = {"V": pltpu.VMEM, "H": pltpu.HBM, "S": pltpu.SMEM}


def local(kernel, args, places, outs, scratch_shapes, flops, name):
    args = [pltpu.with_memory_space_constraint(a, SPACES[p]) if p != "S" else a for a, p in zip(args, places)]
    moved = sum(a.size * a.dtype.itemsize for a in args)
    made = pl.pallas_call(
        kernel,
        out_shape=[SPACES[p](shape, dtype) for p, shape, dtype in outs],
        in_specs=[pl.BlockSpec(memory_space=SPACES[p]) for p in places],
        out_specs=[pl.BlockSpec(memory_space=SPACES[p]) for p, _, _ in outs],
        scratch_shapes=scratch_shapes,
        cost_estimate=pl.CostEstimate(flops=flops, bytes_accessed=moved, transcendentals=0),
        compiler_params=pltpu.CompilerParams(vmem_limit_bytes=LIMIT),
        name=name,
    )(*args)
    return made if len(outs) > 1 else made[0]


def sum_over_rows(totals, groups, beside):
    order = order_of(groups, SUMS_SEED)
    width, size = totals.shape
    piece = round_up(width, groups) // groups
    padded = jnp.pad(totals, ((0, piece * groups - width), (0, 0))) if piece * groups != width else totals
    got = exchange(padded.reshape(groups, piece, size), order)
    made = None
    if beside is not None:
        got, made = lax.optimization_barrier((got, beside()))
    own = jnp.sum(got, axis=0)
    back = exchange(jnp.broadcast_to(own[None], (groups, piece, size)), order)
    return back.reshape(groups * piece, size)[:width], made


def on_device(groups, cores, counts, samples, targets, point_ids, block_inverse):
    rows_here, feat = samples.shape
    blocks, size = point_ids.shape
    mean = blocks * size / groups
    caps = sorted({round_up(max(1, round((mean + spread * mean**0.5) / cores)), 8) for spread in (2, 4)})
    cap = caps[-1]

    order = order_of(groups, POINTS_SEED)
    rows, slots, most = local(
        functools.partial(pick_kernel, order, cores, caps),
        (counts, point_ids, samples),
        "SVH",
        [("V", (cap, feat), F32), ("V", (1, blocks * size), jnp.int32), ("S", (1,), jnp.int32)],
        [
            pltpu.VMEM(samples.shape, F32),
            pltpu.VMEM((cap, rows_here), BF16),
            pltpu.SemaphoreType.DMA((len(pieces(rows_here, HALF_STEP)),)),
        ],
        4 * cap * rows_here * feat,
        "pick",
    )

    def general(rows):
        ids = jnp.pad(point_ids.reshape(-1), (0, cores * groups * cap - blocks * size), constant_values=-1)
        ids = lax.dynamic_slice_in_dim(ids, lax.axis_index("tgt") * groups * cap, groups * cap)
        here = ids - lax.axis_index("rows") * rows_here
        taken = local(
            owned_kernel,
            (here[:, None], samples),
            "VH",
            [("V", (groups * cap, feat), F32)],
            [pltpu.VMEM(samples.shape, F32), pltpu.SemaphoreType.DMA((1,))],
            4 * groups * cap * rows_here * feat,
            "owned",
        )
        return jnp.sum(exchange(taken.reshape(groups, cap, feat), order), axis=0)

    def gather(rows, count=cap):
        sent = jnp.broadcast_to(rows[None, :count], (groups, count, feat))
        got = exchange(sent, order).reshape(groups * count, feat)
        return got if count == cap else jnp.pad(got, ((0, groups * (cap - count)), (0, 0)))

    choices = [functools.partial(gather, count=count) for count in caps] + [lambda rows: gather(general(rows))]
    got = lax.switch(sum((most[0] > count * cores).astype(jnp.int32) for count in caps), choices, rows)
    held = [lax.ppermute(got, "tgt", [((c + shift) % cores, c) for c in range(cores)]) for shift in range(1, cores)]
    found, samples_split = local(
        functools.partial(own_kernel, cores),
        (counts, slots, got, samples),
        "SVVH",
        [("V", (blocks, 2 * feat, size), BF16), ("V", (rows_here, 2 * feat), BF16)],
        [pltpu.VMEM(samples.shape, F32), pltpu.SemaphoreType.DMA((1,))],
        4 * groups * cap * feat * blocks * size,
        "own",
    )
    held, found = lax.optimization_barrier((held, found))

    width = targets.shape[1]
    columns_v = pltpu.VMEM((2, rows_here, size), BF16)
    residual_v = pltpu.VMEM((rows_here, width), F32)
    coefs_v = pltpu.VMEM((size, 2 * width), BF16)
    sems = pltpu.SemaphoreType.DMA((6, max(cores, len(pieces(rows_here)))))
    columns_out = [("H", (rows_here, size), BF16)] * 2
    inverse_out = ("V", (size, size), F32)
    totals_out = ("V", (width, size), F32)
    work = 6 * rows_here * size

    residual = targets
    points_v = pltpu.VMEM((2, feat, size), BF16)
    high, low, totals, slots_out, found, *held = local(
        functools.partial(first_kernel, cores),
        (counts, residual, samples_split, slots, found, *held),
        "SVVVV" + "V" * len(held),
        [
            *columns_out,
            totals_out,
            ("H", slots.shape, jnp.int32),
            ("H", (blocks - 1, 2 * feat, size), BF16),
            *[("H", h.shape, F32) for h in held],
        ],
        [points_v, columns_v, sems],
        work * (feat + width),
        "first",
    )
    columns = [high, low]
    for b in range(blocks - 1):

        def beside(b=b):
            return local(
                functools.partial(beside_kernel, b, cores),
                (counts, samples_split, slots_out, found, block_inverse, *held),
                "SHHHH" + "H" * len(held),
                [*columns_out, inverse_out],
                [
                    pltpu.VMEM((rows_here, 2 * feat), BF16),
                    points_v,
                    pltpu.VMEM(slots.shape, jnp.int32),
                    pltpu.VMEM((2 * feat, size), BF16),
                    *[pltpu.VMEM(h.shape, F32) for h in held],
                    columns_v,
                    sems,
                ],
                work * feat,
                "beside",
            )

        sums, (*following, inverse) = sum_over_rows(totals, groups, beside)
        residual, totals, inverse = local(
            functools.partial(middle_kernel, b),
            (counts, sums, inverse, residual, *columns, *following, block_inverse),
            "SVVHHHHHH",
            [("V", (rows_here, width), F32), totals_out, inverse_out],
            [coefs_v, residual_v, columns_v, columns_v, sems],
            2 * work * width,
            "middle",
        )
        columns = following
    sums, _ = sum_over_rows(totals, groups, None)
    return local(
        last_kernel,
        (counts, sums, inverse, residual, *columns),
        "SVVVHH",
        [("H", (rows_here, width), F32)],
        [coefs_v, residual_v, columns_v, sems],
        work * width,
        "last",
    )


def solution(mesh):
    return jax.shard_map(
        functools.partial(on_device, mesh.shape["rows"], mesh.shape["tgt"]),
        mesh=mesh,
        in_specs=(P("rows"), P("rows", None), P("rows", "tgt"), P(), P()),
        out_specs=P("rows", "tgt"),
        check_vma=False,
    )
```

```python
import functools
import random

import jax
import jax.numpy as jnp
from jax import lax
from jax.experimental import pallas as pl
from jax.experimental.pallas import tpu as pltpu
from jax.sharding import PartitionSpec as P

F32 = jnp.float32
BF16 = jnp.bfloat16
ROWS_STEP = 512
HALF_STEP = 1024
LIMIT = 24 * 2**20
POINTS_SEED = 14
SUMS_SEED = 152


def order_of(groups, seed):
    order = list(range(groups))
    random.Random(seed).shuffle(order)
    return order


def exchange(x, order):
    return lax.all_to_all(x, "rows", 0, 0, axis_index_groups=[order])


def round_up(value, unit):
    return -(-value // unit) * unit


def split(x):
    high = x.astype(BF16)
    return high, (x - high.astype(F32)).astype(BF16)


def dot(a, b, dims):
    return lax.dot_general(a, b, (dims, ((), ())), preferred_element_type=F32)


def dot3(a, b, dims):
    return dot(a[0], b[0], dims) + dot(a[0], b[1], dims) + dot(a[1], b[0], dims)


def pieces(rows, step=ROWS_STEP):
    step = min(step, rows)
    return [pl.ds(start, step) for start in range(0, rows, step)]


def copy_of(source, target, sem):
    copy = pltpu.make_async_copy(source, target, sem)
    copy.start()
    return copy


def stage(live_ref):
    return pl.when(live_ref[0] >= 0)


def wait_all(*copies):
    for copy in copies:
        copy.wait()


def pick_kernel(order, cores, caps, live_ref, ids_ref, samples_ref, rows_ref, slots_ref, most_ref, samples_v, chosen_v, sems):
    (rows_here, feat), groups = samples_ref.shape, len(order)
    parts = pieces(rows_here, HALF_STEP)
    copies = [copy_of(samples_ref.at[at], samples_v.at[at], sems.at[i]) for i, at in enumerate(parts)]
    me, core = lax.axis_index("rows"), lax.axis_index("tgt")

    @stage(live_ref)
    def _():
        ids = jnp.concatenate([ids_ref[b : b + 1, :] for b in range(ids_ref.shape[0])], axis=1)
        count = ids.shape[1]
        owner = lax.div(ids, jnp.int32(rows_here))
        local = ids - owner * rows_here
        mine = lax.broadcasted_iota(jnp.int32, (groups, count), 0) == owner
        seen = mine.astype(jnp.int32)
        lane = lax.broadcasted_iota(jnp.int32, (groups, count), 1)
        step = 1
        while step < count:
            seen = seen + jnp.where(lane >= step, pltpu.roll(seen, step, 1), 0)
            step *= 2
        most = jnp.max(seen)
        rank = jnp.sum(jnp.where(mine, seen, 0), axis=0, keepdims=True) - 1
        cap = jnp.int32(caps[-1])
        for less in caps[-2::-1]:
            cap = jnp.where(most <= less * cores, less, cap)
        half = lax.div(rank, cap)
        turn = jnp.zeros_like(owner)
        for index, device in enumerate(order):
            turn = jnp.where(owner == device, index, turn)
        packed = half * (groups * caps[-1]) + turn * cap + (rank - half * cap)
        place = lax.broadcasted_iota(jnp.int32, (1, count), 1)
        slots_ref[...] = jnp.where(most > caps[-1] * cores, place, packed)
        most_ref[0] = most

        wanted = lax.broadcasted_iota(jnp.int32, (caps[-1], count), 0) + core * cap
        sent = jnp.sum(jnp.where((wanted == rank) & (owner == me), local, 0), axis=1, keepdims=True)
        chosen_v[...] = jnp.where(lax.broadcasted_iota(jnp.int32, (caps[-1], rows_here), 1) == sent, 1.0, 0.0).astype(BF16)

    for copy, at in zip(copies, parts):
        copy.wait()

        @stage(live_ref)
        def _():
            both = dot(chosen_v[:, at], jnp.concatenate(split(samples_v[at, :]), axis=1), ((1,), (0,)))
            found = both[:, :feat] + both[:, feat:]
            rows_ref[...] = found if at.start == 0 else rows_ref[...] + found


def owned_kernel(local_ref, samples_ref, out_ref, samples_v, sems):
    copy_of(samples_ref, samples_v, sems.at[0]).wait()
    rows, feat = samples_v.shape
    parts = jnp.concatenate(split(samples_v[...]), axis=1)
    for at in pieces(local_ref.shape[0], 128):
        chosen = lax.broadcasted_iota(jnp.int32, (at.size, rows), 1) == local_ref[at, :]
        both = dot(jnp.where(chosen, 1.0, 0.0).astype(BF16), parts, ((1,), (0,)))
        out_ref[at, :] = both[:, :feat] + both[:, feat:]


def found_in(ref, slots, shift, cores):
    depth = ref.shape[0]
    base = lax.rem(lax.axis_index("tgt") + shift, cores) * depth
    slot = lax.broadcasted_iota(jnp.int32, (depth, slots.shape[1]), 0) + base
    taken = jnp.where(slot == slots, 1.0, 0.0).astype(BF16)
    return dot(jnp.concatenate(split(ref[...]), axis=1), taken, ((0,), (0,)))


def own_kernel(cores, live_ref, slots_ref, held_ref, samples_ref, found_ref, parts_ref, samples_v, sems):
    blocks, _, size = found_ref.shape
    samples_in = copy_of(samples_ref, samples_v, sems.at[0])

    @stage(live_ref)
    def _():
        for b in range(blocks):
            found_ref[b] = found_in(held_ref, slots_ref[:, b * size : (b + 1) * size], 0, cores).astype(BF16)

    samples_in.wait()
    parts_ref[...] = jnp.concatenate(split(samples_v[...]), axis=1)


def make_columns(live_ref, samples_ref, points, columns_v, high_ref, low_ref, sems):
    rows, feat = samples_ref.shape[0], samples_ref.shape[1] // 2
    scale = 0.5 / feat**0.5
    copies = []
    for index, half in enumerate(pieces(rows, HALF_STEP)):
        for at in [pl.ds(half.start + part.start, part.size) for part in pieces(half.size)]:
            base = dot3((samples_ref[at, :feat], samples_ref[at, feat:]), points, ((1,), (0,))) * scale + 1.0
            slot = lax.broadcasted_iota(jnp.int32, (at.size, 1), 0) + at.start
            columns_v[0, at, :], columns_v[1, at, :] = split(jnp.where(slot < live_ref[0], base * base * base, 0.0))
        for kind, ref in enumerate((high_ref, low_ref)):
            copies.append(copy_of(columns_v.at[kind, half], ref.at[half], sems.at[kind, index]))
    return copies


def sum_of(residual, high, low):
    width = residual.shape[1]
    residual = split(residual)
    both = dot(jnp.concatenate(residual, axis=1), high, ((0,), (0,)))
    return both[:width] + both[width:] + dot(residual[0], low, ((0,), (0,)))


def points_of(found, held, slots):
    total = found.astype(F32)
    for shift, ref in enumerate(held):
        total = total + found_in(ref, slots, shift + 1, len(held) + 1)
    feat = total.shape[0] // 2
    return total[:feat].astype(BF16), total[feat:].astype(BF16)


def first_kernel(cores, live_ref, residual_ref, samples_ref, slots_ref, found_ref, *refs):
    held, refs = refs[: cores - 1], refs[cores - 1 :]
    high_ref, low_ref, total_ref, slots_out, found_out, *held_out, points_v, columns_v, sems = refs
    blocks, _, size = found_ref.shape
    copies = [copy_of(found_ref.at[pl.ds(1, blocks - 1)], found_out, sems.at[3, 0]), copy_of(slots_ref, slots_out, sems.at[3, 1])]
    copies += [copy_of(ref, out, sems.at[4, i]) for i, (ref, out) in enumerate(zip(held, held_out))]
    points_v[0], points_v[1] = points_of(found_ref[0], held, slots_ref[:, :size])
    copies += make_columns(live_ref, samples_ref, (points_v[0], points_v[1]), columns_v, high_ref, low_ref, sems)
    for index, at in enumerate(pieces(samples_ref.shape[0])):
        term = sum_of(residual_ref[at, :], columns_v[0, at, :], columns_v[1, at, :])
        total_ref[...] = term if index == 0 else total_ref[...] + term
    wait_all(*copies)


def beside_kernel(block, cores, live_ref, samples_ref, slots_ref, found_ref, inverse_ref, *refs):
    held, refs = refs[: cores - 1], refs[cores - 1 :]
    high_ref, low_ref, inverse_v, samples_v, points_v, slots_v, found_v, *held_v, columns_v, sems = refs
    size = found_v.shape[1]
    in_flight = [copy_of(found_ref.at[block], found_v, sems.at[3, 0]), copy_of(slots_ref, slots_v, sems.at[3, 1])]
    in_flight += [copy_of(ref, v, sems.at[4, i]) for i, (ref, v) in enumerate(zip(held, held_v))]
    samples_in = copy_of(samples_ref, samples_v, sems.at[2, 1])
    inverse_in = copy_of(inverse_ref.at[block], inverse_v, sems.at[2, 0])
    wait_all(*in_flight)

    @stage(live_ref)
    def _():
        points_v[0], points_v[1] = points_of(found_v[...], held_v, slots_v[:, (block + 1) * size : (block + 2) * size])

    samples_in.wait()
    copies = make_columns(live_ref, samples_v, (points_v[0], points_v[1]), columns_v, high_ref, low_ref, sems)
    wait_all(inverse_in, *copies)


def coefs_of(sums_ref, inverse_ref):
    return jnp.concatenate(split(dot3(split(sums_ref[...]), split(inverse_ref[...]), ((1,), (1,))).T), axis=1)


def updated(residual, high, low, coefs):
    width = residual.shape[1]
    both = dot(high, coefs, ((1,), (0,)))
    return residual - (both[:, :width] + both[:, width:] + dot(low, coefs[:, :width], ((1,), (0,))))


def middle_kernel(block, live_ref, sums_ref, inverse_ref, residual_ref, high_ref, low_ref, next_high, next_low, inverses, *refs):
    out_ref, total_ref, inverse_v, coefs_v, residual_v, columns_v, next_v, sems = refs
    parts = pieces(out_ref.shape[0])
    first_in = [
        [
            copy_of(residual_ref.at[at], residual_v.at[at], sems.at[0, i]),
            copy_of(high_ref.at[at], columns_v.at[0, at], sems.at[1, i]),
            copy_of(low_ref.at[at], columns_v.at[1, at], sems.at[2, i]),
        ]
        for i, at in enumerate(parts)
    ]
    next_in = [
        [copy_of(ref.at[at], next_v.at[kind, at], sems.at[3 + kind, i]) for kind, ref in enumerate((next_high, next_low))]
        for i, at in enumerate(parts)
    ]
    inverse_in = copy_of(inverses.at[block + 1], inverse_v, sems.at[5, 0])

    @stage(live_ref)
    def _():
        coefs_v[...] = coefs_of(sums_ref, inverse_ref)

    for copies, at in zip(first_in, parts):
        wait_all(*copies)

        @stage(live_ref)
        def _():
            out_ref[at, :] = updated(residual_v[at, :], columns_v[0, at, :], columns_v[1, at, :], coefs_v[...])

    for copies, at in zip(next_in, parts):
        wait_all(*copies)

        @stage(live_ref)
        def _():
            term = sum_of(out_ref[at, :], next_v[0, at, :], next_v[1, at, :])
            total_ref[...] = term if at.start == 0 else total_ref[...] + term

    inverse_in.wait()


def last_kernel(live_ref, sums_ref, inverse_ref, residual_ref, high_ref, low_ref, out_ref, coefs_v, residual_v, columns_v, sems):
    parts = pieces(out_ref.shape[0])
    columns_in = [
        [copy_of(ref.at[at], columns_v.at[kind, at], sems.at[kind, i]) for kind, ref in enumerate((high_ref, low_ref))]
        for i, at in enumerate(parts)
    ]

    @stage(live_ref)
    def _():
        coefs_v[...] = coefs_of(sums_ref, inverse_ref)

    out = []
    for copies, at in zip(columns_in, parts):
        wait_all(*copies)

        @stage(live_ref)
        def _():
            residual_v[at, :] = updated(residual_ref[at, :], columns_v[0, at, :], columns_v[1, at, :], coefs_v[...])

        out.append(copy_of(residual_v.at[at], out_ref.at[at], sems.at[2, len(out)]))
    wait_all(*out)


SPACES = {"V": pltpu.VMEM, "H": pltpu.HBM, "S": pltpu.SMEM}


def local(kernel, args, places, outs, scratch_shapes, flops, name):
    args = [pltpu.with_memory_space_constraint(a, SPACES[p]) if p != "S" else a for a, p in zip(args, places)]
    moved = sum(a.size * a.dtype.itemsize for a in args)
    made = pl.pallas_call(
        kernel,
        out_shape=[SPACES[p](shape, dtype) for p, shape, dtype in outs],
        in_specs=[pl.BlockSpec(memory_space=SPACES[p]) for p in places],
        out_specs=[pl.BlockSpec(memory_space=SPACES[p]) for p, _, _ in outs],
        scratch_shapes=scratch_shapes,
        cost_estimate=pl.CostEstimate(flops=flops, bytes_accessed=moved, transcendentals=0),
        compiler_params=pltpu.CompilerParams(vmem_limit_bytes=LIMIT),
        name=name,
    )(*args)
    return made if len(outs) > 1 else made[0]


def sum_over_rows(totals, groups, beside):
    order = order_of(groups, SUMS_SEED)
    width, size = totals.shape
    piece = round_up(width, groups) // groups
    padded = jnp.pad(totals, ((0, piece * groups - width), (0, 0))) if piece * groups != width else totals
    got = exchange(padded.reshape(groups, piece, size), order)
    made = None
    if beside is not None:
        got, made = lax.optimization_barrier((got, beside()))
    own = jnp.sum(got, axis=0)
    back = exchange(jnp.broadcast_to(own[None], (groups, piece, size)), order)
    return back.reshape(groups * piece, size)[:width], made


def on_device(groups, cores, counts, samples, targets, point_ids, block_inverse):
    rows_here, feat = samples.shape
    blocks, size = point_ids.shape
    mean = blocks * size / groups
    caps = sorted({round_up(max(1, round((mean + spread * mean**0.5) / cores)), 8) for spread in (2, 4)})
    cap = caps[-1]

    order = order_of(groups, POINTS_SEED)
    rows, slots, most = local(
        functools.partial(pick_kernel, order, cores, caps),
        (counts, point_ids, samples),
        "SVH",
        [("V", (cap, feat), F32), ("V", (1, blocks * size), jnp.int32), ("S", (1,), jnp.int32)],
        [
            pltpu.VMEM(samples.shape, F32),
            pltpu.VMEM((cap, rows_here), BF16),
            pltpu.SemaphoreType.DMA((len(pieces(rows_here, HALF_STEP)),)),
        ],
        4 * cap * rows_here * feat,
        "pick",
    )

    def general(rows):
        ids = jnp.pad(point_ids.reshape(-1), (0, cores * groups * cap - blocks * size), constant_values=-1)
        ids = lax.dynamic_slice_in_dim(ids, lax.axis_index("tgt") * groups * cap, groups * cap)
        here = ids - lax.axis_index("rows") * rows_here
        taken = local(
            owned_kernel,
            (here[:, None], samples),
            "VH",
            [("V", (groups * cap, feat), F32)],
            [pltpu.VMEM(samples.shape, F32), pltpu.SemaphoreType.DMA((1,))],
            4 * groups * cap * rows_here * feat,
            "owned",
        )
        return jnp.sum(exchange(taken.reshape(groups, cap, feat), order), axis=0)

    def gather(rows, count=cap):
        sent = jnp.broadcast_to(rows[None, :count], (groups, count, feat))
        got = exchange(sent, order).reshape(groups * count, feat)
        return got if count == cap else jnp.pad(got, ((0, groups * (cap - count)), (0, 0)))

    choices = [functools.partial(gather, count=count) for count in caps] + [lambda rows: gather(general(rows))]
    got = lax.switch(sum((most[0] > count * cores).astype(jnp.int32) for count in caps), choices, rows)
    held = [lax.ppermute(got, "tgt", [((c + shift) % cores, c) for c in range(cores)]) for shift in range(1, cores)]
    found, samples_split = local(
        functools.partial(own_kernel, cores),
        (counts, slots, got, samples),
        "SVVH",
        [("V", (blocks, 2 * feat, size), BF16), ("V", (rows_here, 2 * feat), BF16)],
        [pltpu.VMEM(samples.shape, F32), pltpu.SemaphoreType.DMA((1,))],
        4 * groups * cap * feat * blocks * size,
        "own",
    )
    held, found = lax.optimization_barrier((held, found))

    width = targets.shape[1]
    columns_v = pltpu.VMEM((2, rows_here, size), BF16)
    residual_v = pltpu.VMEM((rows_here, width), F32)
    coefs_v = pltpu.VMEM((size, 2 * width), BF16)
    sems = pltpu.SemaphoreType.DMA((6, max(cores, len(pieces(rows_here)))))
    columns_out = [("H", (rows_here, size), BF16)] * 2
    inverse_out = ("V", (size, size), F32)
    totals_out = ("V", (width, size), F32)
    work = 6 * rows_here * size

    residual = targets
    points_v = pltpu.VMEM((2, feat, size), BF16)
    high, low, totals, slots_out, found, *held = local(
        functools.partial(first_kernel, cores),
        (counts, residual, samples_split, slots, found, *held),
        "SVVVV" + "V" * len(held),
        [
            *columns_out,
            totals_out,
            ("H", slots.shape, jnp.int32),
            ("H", (blocks - 1, 2 * feat, size), BF16),
            *[("H", h.shape, F32) for h in held],
        ],
        [points_v, columns_v, sems],
        work * (feat + width),
        "first",
    )
    columns = [high, low]
    for b in range(blocks - 1):

        def beside(b=b):
            return local(
                functools.partial(beside_kernel, b, cores),
                (counts, samples_split, slots_out, found, block_inverse, *held),
                "SHHHH" + "H" * len(held),
                [*columns_out, inverse_out],
                [
                    pltpu.VMEM((rows_here, 2 * feat), BF16),
                    points_v,
                    pltpu.VMEM(slots.shape, jnp.int32),
                    pltpu.VMEM((2 * feat, size), BF16),
                    *[pltpu.VMEM(h.shape, F32) for h in held],
                    columns_v,
                    sems,
                ],
                work * feat,
                "beside",
            )

        sums, (*following, inverse) = sum_over_rows(totals, groups, beside)
        residual, totals, inverse = local(
            functools.partial(middle_kernel, b),
            (counts, sums, inverse, residual, *columns, *following, block_inverse),
            "SVVHHHHHH",
            [("V", (rows_here, width), F32), totals_out, inverse_out],
            [coefs_v, residual_v, columns_v, columns_v, sems],
            2 * work * width,
            "middle",
        )
        columns = following
    sums, _ = sum_over_rows(totals, groups, None)
    return local(
        last_kernel,
        (counts, sums, inverse, residual, *columns),
        "SVVVHH",
        [("H", (rows_here, width), F32)],
        [coefs_v, residual_v, columns_v, sems],
        work * width,
        "last",
    )


def solution(mesh):
    return jax.shard_map(
        functools.partial(on_device, mesh.shape["rows"], mesh.shape["tgt"]),
        mesh=mesh,
        in_specs=(P("rows"), P("rows", None), P("rows", "tgt"), P(), P()),
        out_specs=P("rows", "tgt"),
        check_vma=False,
    )
```

```python
import functools
import random

import jax
import jax.numpy as jnp
from jax import lax
from jax.experimental import pallas as pl
from jax.experimental.pallas import tpu as pltpu
from jax.sharding import PartitionSpec as P

F32 = jnp.float32
BF16 = jnp.bfloat16
ROWS_STEP = 512
HALF_STEP = 1024
LIMIT = 24 * 2**20
POINTS_SEED = 14
SUMS_SEED = 152


def order_of(groups, seed):
    order = list(range(groups))
    random.Random(seed).shuffle(order)
    return order


def exchange(x, order):
    return lax.all_to_all(x, "rows", 0, 0, axis_index_groups=[order])


def round_up(value, unit):
    return -(-value // unit) * unit


def split(x):
    high = x.astype(BF16)
    return high, (x - high.astype(F32)).astype(BF16)


def dot(a, b, dims):
    return lax.dot_general(a, b, (dims, ((), ())), preferred_element_type=F32)


def dot3(a, b, dims):
    return dot(a[0], b[0], dims) + dot(a[0], b[1], dims) + dot(a[1], b[0], dims)


def pieces(rows, step=ROWS_STEP):
    step = min(step, rows)
    return [pl.ds(start, step) for start in range(0, rows, step)]


def copy_of(source, target, sem):
    copy = pltpu.make_async_copy(source, target, sem)
    copy.start()
    return copy


def stage(live_ref):
    return pl.when(live_ref[0] >= 0)


def wait_all(*copies):
    for copy in copies:
        copy.wait()


def pick_kernel(order, cores, caps, live_ref, ids_ref, samples_ref, rows_ref, slots_ref, most_ref, samples_v, chosen_v, sems):
    (rows_here, feat), groups = samples_ref.shape, len(order)
    parts = pieces(rows_here, HALF_STEP)
    copies = [copy_of(samples_ref.at[at], samples_v.at[at], sems.at[i]) for i, at in enumerate(parts)]
    me, core = lax.axis_index("rows"), lax.axis_index("tgt")

    @stage(live_ref)
    def _():
        ids = jnp.concatenate([ids_ref[b : b + 1, :] for b in range(ids_ref.shape[0])], axis=1)
        count = ids.shape[1]
        owner = lax.div(ids, jnp.int32(rows_here))
        local = ids - owner * rows_here
        mine = lax.broadcasted_iota(jnp.int32, (groups, count), 0) == owner
        seen = mine.astype(jnp.int32)
        lane = lax.broadcasted_iota(jnp.int32, (groups, count), 1)
        step = 1
        while step < count:
            seen = seen + jnp.where(lane >= step, pltpu.roll(seen, step, 1), 0)
            step *= 2
        most = jnp.max(seen)
        rank = jnp.sum(jnp.where(mine, seen, 0), axis=0, keepdims=True) - 1
        cap = jnp.int32(caps[-1])
        for less in caps[-2::-1]:
            cap = jnp.where(most <= less * cores, less, cap)
        half = lax.div(rank, cap)
        turn = jnp.zeros_like(owner)
        for index, device in enumerate(order):
            turn = jnp.where(owner == device, index, turn)
        packed = half * (groups * caps[-1]) + turn * cap + (rank - half * cap)
        place = lax.broadcasted_iota(jnp.int32, (1, count), 1)
        slots_ref[...] = jnp.where(most > caps[-1] * cores, place, packed)
        most_ref[0] = most

        wanted = lax.broadcasted_iota(jnp.int32, (caps[-1], count), 0) + core * cap
        sent = jnp.sum(jnp.where((wanted == rank) & (owner == me), local, 0), axis=1, keepdims=True)
        chosen_v[...] = jnp.where(lax.broadcasted_iota(jnp.int32, (caps[-1], rows_here), 1) == sent, 1.0, 0.0).astype(BF16)

    for copy, at in zip(copies, parts):
        copy.wait()

        @stage(live_ref)
        def _():
            both = dot(chosen_v[:, at], jnp.concatenate(split(samples_v[at, :]), axis=1), ((1,), (0,)))
            found = both[:, :feat] + both[:, feat:]
            rows_ref[...] = found if at.start == 0 else rows_ref[...] + found


def owned_kernel(local_ref, samples_ref, out_ref, samples_v, sems):
    copy_of(samples_ref, samples_v, sems.at[0]).wait()
    rows, feat = samples_v.shape
    parts = jnp.concatenate(split(samples_v[...]), axis=1)
    for at in pieces(local_ref.shape[0], 128):
        chosen = lax.broadcasted_iota(jnp.int32, (at.size, rows), 1) == local_ref[at, :]
        both = dot(jnp.where(chosen, 1.0, 0.0).astype(BF16), parts, ((1,), (0,)))
        out_ref[at, :] = both[:, :feat] + both[:, feat:]


def found_in(ref, slots, shift, cores):
    depth = ref.shape[0]
    base = lax.rem(lax.axis_index("tgt") + shift, cores) * depth
    slot = lax.broadcasted_iota(jnp.int32, (depth, slots.shape[1]), 0) + base
    taken = jnp.where(slot == slots, 1.0, 0.0).astype(BF16)
    return dot(jnp.concatenate(split(ref[...]), axis=1), taken, ((0,), (0,)))


def own_kernel(cores, live_ref, slots_ref, held_ref, samples_ref, found_ref, parts_ref, samples_v, sems):
    blocks, _, size = found_ref.shape
    samples_in = copy_of(samples_ref, samples_v, sems.at[0])

    @stage(live_ref)
    def _():
        for b in range(blocks):
            found_ref[b] = found_in(held_ref, slots_ref[:, b * size : (b + 1) * size], 0, cores).astype(BF16)

    samples_in.wait()
    parts_ref[...] = jnp.concatenate(split(samples_v[...]), axis=1)


def make_columns(live_ref, samples_ref, points, columns_v, high_ref, low_ref, sems):
    rows, feat = samples_ref.shape[0], samples_ref.shape[1] // 2
    scale = 0.5 / feat**0.5
    copies = []
    for index, half in enumerate(pieces(rows, HALF_STEP)):
        for at in [pl.ds(half.start + part.start, part.size) for part in pieces(half.size)]:
            base = dot3((samples_ref[at, :feat], samples_ref[at, feat:]), points, ((1,), (0,))) * scale + 1.0
            slot = lax.broadcasted_iota(jnp.int32, (at.size, 1), 0) + at.start
            columns_v[0, at, :], columns_v[1, at, :] = split(jnp.where(slot < live_ref[0], base * base * base, 0.0))
        for kind, ref in enumerate((high_ref, low_ref)):
            copies.append(copy_of(columns_v.at[kind, half], ref.at[half], sems.at[kind, index]))
    return copies


def sum_of(residual, high, low):
    width = residual.shape[1]
    residual = split(residual)
    both = dot(jnp.concatenate(residual, axis=1), high, ((0,), (0,)))
    return both[:width] + both[width:] + dot(residual[0], low, ((0,), (0,)))


def points_of(found, held, slots):
    total = found.astype(F32)
    for shift, ref in enumerate(held):
        total = total + found_in(ref, slots, shift + 1, len(held) + 1)
    feat = total.shape[0] // 2
    return total[:feat].astype(BF16), total[feat:].astype(BF16)


def first_kernel(cores, live_ref, residual_ref, samples_ref, slots_ref, found_ref, *refs):
    held, refs = refs[: cores - 1], refs[cores - 1 :]
    high_ref, low_ref, total_ref, slots_out, found_out, *held_out, points_v, columns_v, sems = refs
    blocks, _, size = found_ref.shape
    copies = [copy_of(found_ref.at[pl.ds(1, blocks - 1)], found_out, sems.at[3, 0]), copy_of(slots_ref, slots_out, sems.at[3, 1])]
    copies += [copy_of(ref, out, sems.at[4, i]) for i, (ref, out) in enumerate(zip(held, held_out))]
    points_v[0], points_v[1] = points_of(found_ref[0], held, slots_ref[:, :size])
    copies += make_columns(live_ref, samples_ref, (points_v[0], points_v[1]), columns_v, high_ref, low_ref, sems)
    for index, at in enumerate(pieces(samples_ref.shape[0])):
        term = sum_of(residual_ref[at, :], columns_v[0, at, :], columns_v[1, at, :])
        total_ref[...] = term if index == 0 else total_ref[...] + term
    wait_all(*copies)


def beside_kernel(block, cores, live_ref, samples_ref, slots_ref, found_ref, inverse_ref, *refs):
    held, refs = refs[: cores - 1], refs[cores - 1 :]
    high_ref, low_ref, inverse_v, samples_v, points_v, slots_v, found_v, *held_v, columns_v, sems = refs
    size = found_v.shape[1]
    in_flight = [copy_of(found_ref.at[block], found_v, sems.at[3, 0]), copy_of(slots_ref, slots_v, sems.at[3, 1])]
    in_flight += [copy_of(ref, v, sems.at[4, i]) for i, (ref, v) in enumerate(zip(held, held_v))]
    samples_in = copy_of(samples_ref, samples_v, sems.at[2, 1])
    inverse_in = copy_of(inverse_ref.at[block], inverse_v, sems.at[2, 0])
    wait_all(*in_flight)

    @stage(live_ref)
    def _():
        points_v[0], points_v[1] = points_of(found_v[...], held_v, slots_v[:, (block + 1) * size : (block + 2) * size])

    samples_in.wait()
    copies = make_columns(live_ref, samples_v, (points_v[0], points_v[1]), columns_v, high_ref, low_ref, sems)
    wait_all(inverse_in, *copies)


def coefs_of(sums_ref, inverse_ref):
    return jnp.concatenate(split(dot3(split(sums_ref[...]), split(inverse_ref[...]), ((1,), (1,))).T), axis=1)


def updated(residual, high, low, coefs):
    width = residual.shape[1]
    both = dot(high, coefs, ((1,), (0,)))
    return residual - (both[:, :width] + both[:, width:] + dot(low, coefs[:, :width], ((1,), (0,))))


def middle_kernel(block, live_ref, sums_ref, inverse_ref, residual_ref, high_ref, low_ref, next_high, next_low, inverses, *refs):
    out_ref, total_ref, inverse_v, coefs_v, residual_v, columns_v, next_v, sems = refs
    parts = pieces(out_ref.shape[0])
    first_in = [
        [
            copy_of(residual_ref.at[at], residual_v.at[at], sems.at[0, i]),
            copy_of(high_ref.at[at], columns_v.at[0, at], sems.at[1, i]),
            copy_of(low_ref.at[at], columns_v.at[1, at], sems.at[2, i]),
        ]
        for i, at in enumerate(parts)
    ]
    next_in = [
        [copy_of(ref.at[at], next_v.at[kind, at], sems.at[3 + kind, i]) for kind, ref in enumerate((next_high, next_low))]
        for i, at in enumerate(parts)
    ]
    inverse_in = copy_of(inverses.at[block + 1], inverse_v, sems.at[5, 0])

    @stage(live_ref)
    def _():
        coefs_v[...] = coefs_of(sums_ref, inverse_ref)

    for copies, at in zip(first_in, parts):
        wait_all(*copies)

        @stage(live_ref)
        def _():
            out_ref[at, :] = updated(residual_v[at, :], columns_v[0, at, :], columns_v[1, at, :], coefs_v[...])

    for copies, at in zip(next_in, parts):
        wait_all(*copies)

        @stage(live_ref)
        def _():
            term = sum_of(out_ref[at, :], next_v[0, at, :], next_v[1, at, :])
            total_ref[...] = term if at.start == 0 else total_ref[...] + term

    inverse_in.wait()


def last_kernel(live_ref, sums_ref, inverse_ref, residual_ref, high_ref, low_ref, out_ref, coefs_v, residual_v, columns_v, sems):
    parts = pieces(out_ref.shape[0])
    end = parts.pop()
    parts += [pl.ds(end.start + part.start, part.size) for part in pieces(end.size, end.size // 2)]
    columns_in = [
        [copy_of(ref.at[at], columns_v.at[kind, at], sems.at[kind, i]) for kind, ref in enumerate((high_ref, low_ref))]
        for i, at in enumerate(parts)
    ]

    @stage(live_ref)
    def _():
        coefs_v[...] = coefs_of(sums_ref, inverse_ref)

    out = []
    for copies, at in zip(columns_in, parts):
        wait_all(*copies)

        @stage(live_ref)
        def _():
            residual_v[at, :] = updated(residual_ref[at, :], columns_v[0, at, :], columns_v[1, at, :], coefs_v[...])

        out.append(copy_of(residual_v.at[at], out_ref.at[at], sems.at[2, len(out)]))
    wait_all(*out)


SPACES = {"V": pltpu.VMEM, "H": pltpu.HBM, "S": pltpu.SMEM}


def local(kernel, args, places, outs, scratch_shapes, flops, name):
    args = [pltpu.with_memory_space_constraint(a, SPACES[p]) if p != "S" else a for a, p in zip(args, places)]
    moved = sum(a.size * a.dtype.itemsize for a in args)
    made = pl.pallas_call(
        kernel,
        out_shape=[SPACES[p](shape, dtype) for p, shape, dtype in outs],
        in_specs=[pl.BlockSpec(memory_space=SPACES[p]) for p in places],
        out_specs=[pl.BlockSpec(memory_space=SPACES[p]) for p, _, _ in outs],
        scratch_shapes=scratch_shapes,
        cost_estimate=pl.CostEstimate(flops=flops, bytes_accessed=moved, transcendentals=0),
        compiler_params=pltpu.CompilerParams(vmem_limit_bytes=LIMIT),
        name=name,
    )(*args)
    return made if len(outs) > 1 else made[0]


def sum_over_rows(totals, groups, beside):
    order = order_of(groups, SUMS_SEED)
    width, size = totals.shape
    piece = round_up(width, groups) // groups
    padded = jnp.pad(totals, ((0, piece * groups - width), (0, 0))) if piece * groups != width else totals
    got = exchange(padded.reshape(groups, piece, size), order)
    made = None
    if beside is not None:
        got, made = lax.optimization_barrier((got, beside()))
    own = jnp.sum(got, axis=0)
    back = exchange(jnp.broadcast_to(own[None], (groups, piece, size)), order)
    return back.reshape(groups * piece, size)[:width], made


def on_device(groups, cores, counts, samples, targets, point_ids, block_inverse):
    rows_here, feat = samples.shape
    blocks, size = point_ids.shape
    mean = blocks * size / groups
    caps = sorted({round_up(max(1, round((mean + spread * mean**0.5) / cores)), 8) for spread in (2, 4)})
    cap = caps[-1]

    order = order_of(groups, POINTS_SEED)
    rows, slots, most = local(
        functools.partial(pick_kernel, order, cores, caps),
        (counts, point_ids, samples),
        "SVH",
        [("V", (cap, feat), F32), ("V", (1, blocks * size), jnp.int32), ("S", (1,), jnp.int32)],
        [
            pltpu.VMEM(samples.shape, F32),
            pltpu.VMEM((cap, rows_here), BF16),
            pltpu.SemaphoreType.DMA((len(pieces(rows_here, HALF_STEP)),)),
        ],
        4 * cap * rows_here * feat,
        "pick",
    )

    def general(rows):
        ids = jnp.pad(point_ids.reshape(-1), (0, cores * groups * cap - blocks * size), constant_values=-1)
        ids = lax.dynamic_slice_in_dim(ids, lax.axis_index("tgt") * groups * cap, groups * cap)
        here = ids - lax.axis_index("rows") * rows_here
        taken = local(
            owned_kernel,
            (here[:, None], samples),
            "VH",
            [("V", (groups * cap, feat), F32)],
            [pltpu.VMEM(samples.shape, F32), pltpu.SemaphoreType.DMA((1,))],
            4 * groups * cap * rows_here * feat,
            "owned",
        )
        return jnp.sum(exchange(taken.reshape(groups, cap, feat), order), axis=0)

    def gather(rows, count=cap):
        sent = jnp.broadcast_to(rows[None, :count], (groups, count, feat))
        got = exchange(sent, order).reshape(groups * count, feat)
        return got if count == cap else jnp.pad(got, ((0, groups * (cap - count)), (0, 0)))

    choices = [functools.partial(gather, count=count) for count in caps] + [lambda rows: gather(general(rows))]
    got = lax.switch(sum((most[0] > count * cores).astype(jnp.int32) for count in caps), choices, rows)
    held = [lax.ppermute(got, "tgt", [((c + shift) % cores, c) for c in range(cores)]) for shift in range(1, cores)]
    found, samples_split = local(
        functools.partial(own_kernel, cores),
        (counts, slots, got, samples),
        "SVVH",
        [("V", (blocks, 2 * feat, size), BF16), ("V", (rows_here, 2 * feat), BF16)],
        [pltpu.VMEM(samples.shape, F32), pltpu.SemaphoreType.DMA((1,))],
        4 * groups * cap * feat * blocks * size,
        "own",
    )
    held, found = lax.optimization_barrier((held, found))

    width = targets.shape[1]
    columns_v = pltpu.VMEM((2, rows_here, size), BF16)
    residual_v = pltpu.VMEM((rows_here, width), F32)
    coefs_v = pltpu.VMEM((size, 2 * width), BF16)
    sems = pltpu.SemaphoreType.DMA((6, max(cores, len(pieces(rows_here)) + 1)))
    columns_out = [("H", (rows_here, size), BF16)] * 2
    inverse_out = ("V", (size, size), F32)
    totals_out = ("V", (width, size), F32)
    work = 6 * rows_here * size

    residual = targets
    points_v = pltpu.VMEM((2, feat, size), BF16)
    high, low, totals, slots_out, found, *held = local(
        functools.partial(first_kernel, cores),
        (counts, residual, samples_split, slots, found, *held),
        "SVVVV" + "V" * len(held),
        [
            *columns_out,
            totals_out,
            ("H", slots.shape, jnp.int32),
            ("H", (blocks - 1, 2 * feat, size), BF16),
            *[("H", h.shape, F32) for h in held],
        ],
        [points_v, columns_v, sems],
        work * (feat + width),
        "first",
    )
    columns = [high, low]
    for b in range(blocks - 1):

        def beside(b=b):
            return local(
                functools.partial(beside_kernel, b, cores),
                (counts, samples_split, slots_out, found, block_inverse, *held),
                "SHHHH" + "H" * len(held),
                [*columns_out, inverse_out],
                [
                    pltpu.VMEM((rows_here, 2 * feat), BF16),
                    points_v,
                    pltpu.VMEM(slots.shape, jnp.int32),
                    pltpu.VMEM((2 * feat, size), BF16),
                    *[pltpu.VMEM(h.shape, F32) for h in held],
                    columns_v,
                    sems,
                ],
                work * feat,
                "beside",
            )

        sums, (*following, inverse) = sum_over_rows(totals, groups, beside)
        residual, totals, inverse = local(
            functools.partial(middle_kernel, b),
            (counts, sums, inverse, residual, *columns, *following, block_inverse),
            "SVVHHHHHH",
            [("V", (rows_here, width), F32), totals_out, inverse_out],
            [coefs_v, residual_v, columns_v, columns_v, sems],
            2 * work * width,
            "middle",
        )
        columns = following
    sums, _ = sum_over_rows(totals, groups, None)
    return local(
        last_kernel,
        (counts, sums, inverse, residual, *columns),
        "SVVVHH",
        [("H", (rows_here, width), F32)],
        [coefs_v, residual_v, columns_v, sems],
        work * width,
        "last",
    )


def solution(mesh):
    return jax.shard_map(
        functools.partial(on_device, mesh.shape["rows"], mesh.shape["tgt"]),
        mesh=mesh,
        in_specs=(P("rows"), P("rows", None), P("rows", "tgt"), P(), P()),
        out_specs=P("rows", "tgt"),
        check_vma=False,
    )
```

```python
import functools
import random

import jax
import jax.numpy as jnp
from jax import lax
from jax.experimental import pallas as pl
from jax.experimental.pallas import tpu as pltpu
from jax.sharding import PartitionSpec as P

F32 = jnp.float32
BF16 = jnp.bfloat16
ROWS_STEP = 512
HALF_STEP = 512
LIMIT = 24 * 2**20
POINTS_SEED = 14
SUMS_SEED = 152


def order_of(groups, seed):
    order = list(range(groups))
    random.Random(seed).shuffle(order)
    return order


def exchange(x, order):
    return lax.all_to_all(x, "rows", 0, 0, axis_index_groups=[order])


def round_up(value, unit):
    return -(-value // unit) * unit


def split(x):
    high = x.astype(BF16)
    return high, (x - high.astype(F32)).astype(BF16)


def dot(a, b, dims):
    return lax.dot_general(a, b, (dims, ((), ())), preferred_element_type=F32)


def dot3(a, b, dims):
    return dot(a[0], b[0], dims) + dot(a[0], b[1], dims) + dot(a[1], b[0], dims)


def pieces(rows, step=ROWS_STEP):
    step = min(step, rows)
    return [pl.ds(start, step) for start in range(0, rows, step)]


def copy_of(source, target, sem):
    copy = pltpu.make_async_copy(source, target, sem)
    copy.start()
    return copy


def stage(live_ref):
    return pl.when(live_ref[0] >= 0)


def wait_all(*copies):
    for copy in copies:
        copy.wait()


def pick_kernel(order, cores, caps, live_ref, ids_ref, samples_ref, rows_ref, slots_ref, most_ref, samples_v, chosen_v, sems):
    (rows_here, feat), groups = samples_ref.shape, len(order)
    parts = pieces(rows_here, HALF_STEP)
    copies = [copy_of(samples_ref.at[at], samples_v.at[at], sems.at[i]) for i, at in enumerate(parts)]
    me, core = lax.axis_index("rows"), lax.axis_index("tgt")

    @stage(live_ref)
    def _():
        ids = jnp.concatenate([ids_ref[b : b + 1, :] for b in range(ids_ref.shape[0])], axis=1)
        count = ids.shape[1]
        owner = lax.div(ids, jnp.int32(rows_here))
        local = ids - owner * rows_here
        mine = lax.broadcasted_iota(jnp.int32, (groups, count), 0) == owner
        seen = mine.astype(jnp.int32)
        lane = lax.broadcasted_iota(jnp.int32, (groups, count), 1)
        step = 1
        while step < count:
            seen = seen + jnp.where(lane >= step, pltpu.roll(seen, step, 1), 0)
            step *= 2
        most = jnp.max(seen)
        rank = jnp.sum(jnp.where(mine, seen, 0), axis=0, keepdims=True) - 1
        cap = jnp.int32(caps[-1])
        for less in caps[-2::-1]:
            cap = jnp.where(most <= less * cores, less, cap)
        half = lax.div(rank, cap)
        turn = jnp.zeros_like(owner)
        for index, device in enumerate(order):
            turn = jnp.where(owner == device, index, turn)
        packed = half * (groups * caps[-1]) + turn * cap + (rank - half * cap)
        place = lax.broadcasted_iota(jnp.int32, (1, count), 1)
        slots_ref[...] = jnp.where(most > caps[-1] * cores, place, packed)
        most_ref[0] = most

        wanted = lax.broadcasted_iota(jnp.int32, (caps[-1], count), 0) + core * cap
        sent = jnp.sum(jnp.where((wanted == rank) & (owner == me), local, 0), axis=1, keepdims=True)
        chosen_v[...] = jnp.where(lax.broadcasted_iota(jnp.int32, (caps[-1], rows_here), 1) == sent, 1.0, 0.0).astype(BF16)

    for copy, at in zip(copies, parts):
        copy.wait()

        @stage(live_ref)
        def _():
            both = dot(chosen_v[:, at], jnp.concatenate(split(samples_v[at, :]), axis=1), ((1,), (0,)))
            found = both[:, :feat] + both[:, feat:]
            rows_ref[...] = found if at.start == 0 else rows_ref[...] + found


def owned_kernel(local_ref, samples_ref, out_ref, samples_v, sems):
    copy_of(samples_ref, samples_v, sems.at[0]).wait()
    rows, feat = samples_v.shape
    parts = jnp.concatenate(split(samples_v[...]), axis=1)
    for at in pieces(local_ref.shape[0], 128):
        chosen = lax.broadcasted_iota(jnp.int32, (at.size, rows), 1) == local_ref[at, :]
        both = dot(jnp.where(chosen, 1.0, 0.0).astype(BF16), parts, ((1,), (0,)))
        out_ref[at, :] = both[:, :feat] + both[:, feat:]


def found_in(ref, slots, shift, cores):
    depth = ref.shape[0]
    base = lax.rem(lax.axis_index("tgt") + shift, cores) * depth
    slot = lax.broadcasted_iota(jnp.int32, (depth, slots.shape[1]), 0) + base
    taken = jnp.where(slot == slots, 1.0, 0.0).astype(BF16)
    return dot(jnp.concatenate(split(ref[...]), axis=1), taken, ((0,), (0,)))


def own_kernel(cores, live_ref, slots_ref, held_ref, samples_ref, found_ref, parts_ref, samples_v, sems):
    blocks, _, size = found_ref.shape
    samples_in = copy_of(samples_ref, samples_v, sems.at[0])

    @stage(live_ref)
    def _():
        for b in range(blocks):
            found_ref[b] = found_in(held_ref, slots_ref[:, b * size : (b + 1) * size], 0, cores).astype(BF16)

    samples_in.wait()
    parts_ref[...] = jnp.concatenate(split(samples_v[...]), axis=1)


def make_columns(live_ref, samples_ref, points, columns_v, high_ref, low_ref, sems):
    rows, feat = samples_ref.shape[0], samples_ref.shape[1] // 2
    scale = 0.5 / feat**0.5
    copies = []
    for index, half in enumerate(pieces(rows, HALF_STEP)):
        for at in [pl.ds(half.start + part.start, part.size) for part in pieces(half.size)]:
            base = dot3((samples_ref[at, :feat], samples_ref[at, feat:]), points, ((1,), (0,))) * scale + 1.0
            slot = lax.broadcasted_iota(jnp.int32, (at.size, 1), 0) + at.start
            columns_v[0, at, :], columns_v[1, at, :] = split(jnp.where(slot < live_ref[0], base * base * base, 0.0))
        for kind, ref in enumerate((high_ref, low_ref)):
            copies.append(copy_of(columns_v.at[kind, half], ref.at[half], sems.at[kind, index]))
    return copies


def sum_of(residual, high, low):
    width = residual.shape[1]
    residual = split(residual)
    both = dot(jnp.concatenate(residual, axis=1), high, ((0,), (0,)))
    return both[:width] + both[width:] + dot(residual[0], low, ((0,), (0,)))


def points_of(found, held, slots):
    total = found.astype(F32)
    for shift, ref in enumerate(held):
        total = total + found_in(ref, slots, shift + 1, len(held) + 1)
    feat = total.shape[0] // 2
    return total[:feat].astype(BF16), total[feat:].astype(BF16)


def first_kernel(cores, live_ref, residual_ref, samples_ref, slots_ref, found_ref, *refs):
    held, refs = refs[: cores - 1], refs[cores - 1 :]
    high_ref, low_ref, total_ref, slots_out, found_out, *held_out, points_v, columns_v, sems = refs
    blocks, _, size = found_ref.shape
    copies = [copy_of(found_ref.at[pl.ds(1, blocks - 1)], found_out, sems.at[3, 0]), copy_of(slots_ref, slots_out, sems.at[3, 1])]
    copies += [copy_of(ref, out, sems.at[4, i]) for i, (ref, out) in enumerate(zip(held, held_out))]
    points_v[0], points_v[1] = points_of(found_ref[0], held, slots_ref[:, :size])
    copies += make_columns(live_ref, samples_ref, (points_v[0], points_v[1]), columns_v, high_ref, low_ref, sems)
    for index, at in enumerate(pieces(samples_ref.shape[0])):
        term = sum_of(residual_ref[at, :], columns_v[0, at, :], columns_v[1, at, :])
        total_ref[...] = term if index == 0 else total_ref[...] + term
    wait_all(*copies)


def beside_kernel(block, cores, live_ref, samples_ref, slots_ref, found_ref, inverse_ref, *refs):
    held, refs = refs[: cores - 1], refs[cores - 1 :]
    high_ref, low_ref, inverse_v, samples_v, points_v, slots_v, found_v, *held_v, columns_v, sems = refs
    size = found_v.shape[1]
    in_flight = [copy_of(found_ref.at[block], found_v, sems.at[3, 0]), copy_of(slots_ref, slots_v, sems.at[3, 1])]
    in_flight += [copy_of(ref, v, sems.at[4, i]) for i, (ref, v) in enumerate(zip(held, held_v))]
    samples_in = copy_of(samples_ref, samples_v, sems.at[2, 1])
    inverse_in = copy_of(inverse_ref.at[block], inverse_v, sems.at[2, 0])
    wait_all(*in_flight)

    @stage(live_ref)
    def _():
        points_v[0], points_v[1] = points_of(found_v[...], held_v, slots_v[:, (block + 1) * size : (block + 2) * size])

    samples_in.wait()
    copies = make_columns(live_ref, samples_v, (points_v[0], points_v[1]), columns_v, high_ref, low_ref, sems)
    wait_all(inverse_in, *copies)


def coefs_of(sums_ref, inverse_ref):
    return jnp.concatenate(split(dot3(split(sums_ref[...]), split(inverse_ref[...]), ((1,), (1,))).T), axis=1)


def updated(residual, high, low, coefs):
    width = residual.shape[1]
    both = dot(high, coefs, ((1,), (0,)))
    return residual - (both[:, :width] + both[:, width:] + dot(low, coefs[:, :width], ((1,), (0,))))


def middle_kernel(block, live_ref, sums_ref, inverse_ref, residual_ref, high_ref, low_ref, next_high, next_low, inverses, *refs):
    out_ref, total_ref, inverse_v, coefs_v, residual_v, columns_v, next_v, sems = refs
    parts = pieces(out_ref.shape[0])
    first_in = [
        [
            copy_of(residual_ref.at[at], residual_v.at[at], sems.at[0, i]),
            copy_of(high_ref.at[at], columns_v.at[0, at], sems.at[1, i]),
            copy_of(low_ref.at[at], columns_v.at[1, at], sems.at[2, i]),
        ]
        for i, at in enumerate(parts)
    ]
    next_in = [
        [copy_of(ref.at[at], next_v.at[kind, at], sems.at[3 + kind, i]) for kind, ref in enumerate((next_high, next_low))]
        for i, at in enumerate(parts)
    ]
    inverse_in = copy_of(inverses.at[block + 1], inverse_v, sems.at[5, 0])

    @stage(live_ref)
    def _():
        coefs_v[...] = coefs_of(sums_ref, inverse_ref)

    for copies, at in zip(first_in, parts):
        wait_all(*copies)

        @stage(live_ref)
        def _():
            out_ref[at, :] = updated(residual_v[at, :], columns_v[0, at, :], columns_v[1, at, :], coefs_v[...])

    for copies, at in zip(next_in, parts):
        wait_all(*copies)

        @stage(live_ref)
        def _():
            term = sum_of(out_ref[at, :], next_v[0, at, :], next_v[1, at, :])
            total_ref[...] = term if at.start == 0 else total_ref[...] + term

    inverse_in.wait()


def last_kernel(live_ref, sums_ref, inverse_ref, residual_ref, high_ref, low_ref, out_ref, coefs_v, residual_v, columns_v, sems):
    parts = pieces(out_ref.shape[0])
    end = parts.pop()
    parts += [pl.ds(end.start + part.start, part.size) for part in pieces(end.size, end.size // 2)]
    columns_in = [
        [copy_of(ref.at[at], columns_v.at[kind, at], sems.at[kind, i]) for kind, ref in enumerate((high_ref, low_ref))]
        for i, at in enumerate(parts)
    ]

    @stage(live_ref)
    def _():
        coefs_v[...] = coefs_of(sums_ref, inverse_ref)

    out = []
    for copies, at in zip(columns_in, parts):
        wait_all(*copies)

        @stage(live_ref)
        def _():
            residual_v[at, :] = updated(residual_ref[at, :], columns_v[0, at, :], columns_v[1, at, :], coefs_v[...])

        out.append(copy_of(residual_v.at[at], out_ref.at[at], sems.at[2, len(out)]))
    wait_all(*out)


SPACES = {"V": pltpu.VMEM, "H": pltpu.HBM, "S": pltpu.SMEM}


def local(kernel, args, places, outs, scratch_shapes, flops, name):
    args = [pltpu.with_memory_space_constraint(a, SPACES[p]) if p != "S" else a for a, p in zip(args, places)]
    moved = sum(a.size * a.dtype.itemsize for a in args)
    made = pl.pallas_call(
        kernel,
        out_shape=[SPACES[p](shape, dtype) for p, shape, dtype in outs],
        in_specs=[pl.BlockSpec(memory_space=SPACES[p]) for p in places],
        out_specs=[pl.BlockSpec(memory_space=SPACES[p]) for p, _, _ in outs],
        scratch_shapes=scratch_shapes,
        cost_estimate=pl.CostEstimate(flops=flops, bytes_accessed=moved, transcendentals=0),
        compiler_params=pltpu.CompilerParams(vmem_limit_bytes=LIMIT),
        name=name,
    )(*args)
    return made if len(outs) > 1 else made[0]


def sum_over_rows(totals, groups, beside):
    order = order_of(groups, SUMS_SEED)
    width, size = totals.shape
    piece = round_up(width, groups) // groups
    padded = jnp.pad(totals, ((0, piece * groups - width), (0, 0))) if piece * groups != width else totals
    got = exchange(padded.reshape(groups, piece, size), order)
    made = None
    if beside is not None:
        got, made = lax.optimization_barrier((got, beside()))
    own = jnp.sum(got, axis=0)
    back = exchange(jnp.broadcast_to(own[None], (groups, piece, size)), order)
    return back.reshape(groups * piece, size)[:width], made


def on_device(groups, cores, counts, samples, targets, point_ids, block_inverse):
    rows_here, feat = samples.shape
    blocks, size = point_ids.shape
    mean = blocks * size / groups
    caps = sorted({round_up(max(1, round((mean + spread * mean**0.5) / cores)), 8) for spread in (2, 4)})
    cap = caps[-1]

    order = order_of(groups, POINTS_SEED)
    rows, slots, most = local(
        functools.partial(pick_kernel, order, cores, caps),
        (counts, point_ids, samples),
        "SVH",
        [("V", (cap, feat), F32), ("V", (1, blocks * size), jnp.int32), ("S", (1,), jnp.int32)],
        [
            pltpu.VMEM(samples.shape, F32),
            pltpu.VMEM((cap, rows_here), BF16),
            pltpu.SemaphoreType.DMA((len(pieces(rows_here, HALF_STEP)),)),
        ],
        4 * cap * rows_here * feat,
        "pick",
    )

    def general(rows):
        ids = jnp.pad(point_ids.reshape(-1), (0, cores * groups * cap - blocks * size), constant_values=-1)
        ids = lax.dynamic_slice_in_dim(ids, lax.axis_index("tgt") * groups * cap, groups * cap)
        here = ids - lax.axis_index("rows") * rows_here
        taken = local(
            owned_kernel,
            (here[:, None], samples),
            "VH",
            [("V", (groups * cap, feat), F32)],
            [pltpu.VMEM(samples.shape, F32), pltpu.SemaphoreType.DMA((1,))],
            4 * groups * cap * rows_here * feat,
            "owned",
        )
        return jnp.sum(exchange(taken.reshape(groups, cap, feat), order), axis=0)

    def gather(rows, count=cap):
        sent = jnp.broadcast_to(rows[None, :count], (groups, count, feat))
        got = exchange(sent, order).reshape(groups * count, feat)
        return got if count == cap else jnp.pad(got, ((0, groups * (cap - count)), (0, 0)))

    choices = [functools.partial(gather, count=count) for count in caps] + [lambda rows: gather(general(rows))]
    got = lax.switch(sum((most[0] > count * cores).astype(jnp.int32) for count in caps), choices, rows)
    held = [lax.ppermute(got, "tgt", [((c + shift) % cores, c) for c in range(cores)]) for shift in range(1, cores)]
    found, samples_split = local(
        functools.partial(own_kernel, cores),
        (counts, slots, got, samples),
        "SVVH",
        [("V", (blocks, 2 * feat, size), BF16), ("V", (rows_here, 2 * feat), BF16)],
        [pltpu.VMEM(samples.shape, F32), pltpu.SemaphoreType.DMA((1,))],
        4 * groups * cap * feat * blocks * size,
        "own",
    )
    held, found = lax.optimization_barrier((held, found))

    width = targets.shape[1]
    columns_v = pltpu.VMEM((2, rows_here, size), BF16)
    residual_v = pltpu.VMEM((rows_here, width), F32)
    coefs_v = pltpu.VMEM((size, 2 * width), BF16)
    sems = pltpu.SemaphoreType.DMA((6, max(cores, len(pieces(rows_here)) + 1)))
    columns_out = [("H", (rows_here, size), BF16)] * 2
    inverse_out = ("V", (size, size), F32)
    totals_out = ("V", (width, size), F32)
    work = 6 * rows_here * size

    residual = targets
    points_v = pltpu.VMEM((2, feat, size), BF16)
    high, low, totals, slots_out, found, *held = local(
        functools.partial(first_kernel, cores),
        (counts, residual, samples_split, slots, found, *held),
        "SVVVV" + "V" * len(held),
        [
            *columns_out,
            totals_out,
            ("H", slots.shape, jnp.int32),
            ("H", (blocks - 1, 2 * feat, size), BF16),
            *[("H", h.shape, F32) for h in held],
        ],
        [points_v, columns_v, sems],
        work * (feat + width),
        "first",
    )
    columns = [high, low]
    for b in range(blocks - 1):

        def beside(b=b):
            return local(
                functools.partial(beside_kernel, b, cores),
                (counts, samples_split, slots_out, found, block_inverse, *held),
                "SHHHH" + "H" * len(held),
                [*columns_out, inverse_out],
                [
                    pltpu.VMEM((rows_here, 2 * feat), BF16),
                    points_v,
                    pltpu.VMEM(slots.shape, jnp.int32),
                    pltpu.VMEM((2 * feat, size), BF16),
                    *[pltpu.VMEM(h.shape, F32) for h in held],
                    columns_v,
                    sems,
                ],
                work * feat,
                "beside",
            )

        sums, (*following, inverse) = sum_over_rows(totals, groups, beside)
        residual, totals, inverse = local(
            functools.partial(middle_kernel, b),
            (counts, sums, inverse, residual, *columns, *following, block_inverse),
            "SVVHHHHHH",
            [("V", (rows_here, width), F32), totals_out, inverse_out],
            [coefs_v, residual_v, columns_v, columns_v, sems],
            2 * work * width,
            "middle",
        )
        columns = following
    sums, _ = sum_over_rows(totals, groups, None)
    return local(
        last_kernel,
        (counts, sums, inverse, residual, *columns),
        "SVVVHH",
        [("H", (rows_here, width), F32)],
        [coefs_v, residual_v, columns_v, sems],
        work * width,
        "last",
    )


def solution(mesh):
    return jax.shard_map(
        functools.partial(on_device, mesh.shape["rows"], mesh.shape["tgt"]),
        mesh=mesh,
        in_specs=(P("rows"), P("rows", None), P("rows", "tgt"), P(), P()),
        out_specs=P("rows", "tgt"),
        check_vma=False,
    )
```
